32 devices in a mesh: kvh: 2 (over x), ctx: 16 (over z, y, core).
Axes of the slice: x: 2, y: 2, z: 4, core: 2. Of those that a mesh axis runs over, the one named last changes fastest.
Arguments:
- queries: bfloat16 [512, 32, 128], P('ctx', 'kvh'), parts along dimension 1, may hold values from -6 to 6
- cache_keys: bfloat16 [16384, 256], P('ctx', 'kvh'), parts along dimension 1, may hold values from -6 to 6
- cache_values: bfloat16 [16384, 256], P('ctx', 'kvh'), parts along dimension 1, may hold values from -6 to 6
- span_offset: int32 [1], replicated, may hold values from 0 to 8191
- positions: int32 [512], replicated, may hold values from 0 to 8191
Outputs:
- attended: bfloat16 [512, 32, 128], P('ctx', 'kvh'), parts along dimension 1
The draws below stay inside these ranges and needn't reach their ends.
There are 2 independent parts, one for each index of `kvh`. The reference program is written for one: setup_inputs(seed, part) draws one part's arguments, and reference() takes and returns one part's arrays. A program takes and returns all parts, laid end to end along the dimension named above; an argument that names none is the same for every part. Nothing has to cross between parts.
All inputs are finite; a program needn't handle non-finite values.
Results may differ from the reference program's by a relative error of at most 0.0029.
Values may be sent and summed in bfloat16 or wider, within the bound.
No kernel may reach another device: no remote copies, remote signals or barrier semaphores. Data moves between devices by JAX's collectives and lax.ppermute only.
A program may use at most 64 MiB of HBM per device.

```python
import jax
import jax.numpy as jnp
from jax import lax

HD = 128
QH = 16
TOK = 512
CTX_DEV = 1024
CONTEXT = 16384


def draw_queries(key, part):
    normal_part = jnp.clip(jax.random.normal(jax.random.fold_in(key, 13), (TOK, QH, HD), jnp.float32), -4.0, 4.0)
    return normal_part.astype(jnp.bfloat16)


def draw_cache_keys(key, part):
    normal_part = jnp.clip(jax.random.normal(jax.random.fold_in(key, 23), (CONTEXT, HD), jnp.float32), -3.0, 3.0)
    row_scale = jnp.exp(jax.random.uniform(jax.random.fold_in(key, 24), (CONTEXT, 1), jnp.float32, jnp.log(0.5), jnp.log(2.0)))
    normal_part = normal_part * row_scale
    return normal_part.astype(jnp.bfloat16)


def set_ends(result, rng, least, largest):
    longest = result.shape.index(max(result.shape))
    spots = []
    for shift in (0, 1):
        where = [jax.random.randint(jax.random.fold_in(rng, axis), (), 0, length) for axis, length in enumerate(result.shape)]
        where[longest] = (where[longest] + shift) % result.shape[longest]
        spots.append(tuple(where))
    return result.at[spots[0]].set(least).at[spots[1]].set(largest)


def block_levels(own_key, dims, shards, low, largest):
    def one(axis_at, shards_of):
        steps = jax.random.uniform(jax.random.fold_in(jax.random.fold_in(own_key, 6), axis_at), (shards_of,), jnp.float32, low / len(shards), largest / len(shards))
        return jnp.repeat(jnp.exp(steps), dims[axis_at] // shards_of).reshape((-1,) + (1,) * (len(dims) - axis_at - 1))

    factor_of = one(*shards[0])
    for cut in shards[1:]:
        factor_of = factor_of * one(*cut)
    return factor_of


def scatter_about(key, dims, scale, reach, split=(), held_as=jnp.bfloat16):
    loudness = block_levels(key, dims, split, -0.22, 0.18) if split else 1.0
    array = jax.random.normal(key, dims, jnp.float32) * scale * loudness
    return jnp.minimum(jnp.maximum(array, -reach), reach).astype(held_as)


def setup_inputs(seed: int = 0, part: int = 0) -> dict:
    splits = jax.random.split(jax.random.key(seed), 6)
    part_splits = jax.random.split(jax.random.fold_in(splits[5], part), 6)
    queries = draw_queries(jax.random.fold_in(jax.random.fold_in(splits[5], part), 71), part)
    cache_keys = draw_cache_keys(jax.random.fold_in(jax.random.fold_in(splits[5], part), 71), part)
    cache_values = scatter_about(part_splits[2], (CONTEXT, HD), 1.0, 6.0, ((0, 16),))
    span_offset = jax.random.randint(splits[3], (1,), 0, CONTEXT // 2).astype(jnp.int32)
    positions = set_ends(jax.random.randint(splits[4], (TOK,), 0, CONTEXT // 2), jax.random.fold_in(splits[4], 1), 0, (CONTEXT // 2) - 1).astype(jnp.int32)
    return {"queries": queries, "cache_keys": cache_keys, "cache_values": cache_values, "span_offset": span_offset, "positions": positions}


def reference(queries, cache_keys, cache_values, span_offset, positions):
    token_count, head_count, head_width = queries.shape
    row_count = token_count * head_count
    query_rows = queries.reshape(row_count, head_width)
    row_limit = jnp.repeat(span_offset[0] + positions, head_count)
    shard_total = cache_keys.shape[0] // CTX_DEV
    key_shards = cache_keys.reshape(shard_total, CTX_DEV, head_width)
    value_shards = cache_values.reshape(shard_total, CTX_DEV, head_width)
    score_scale = head_width ** -0.5

    def combine_shard(running, inputs):
        key_block, value_block, shard_index = inputs
        key_position = shard_index * CTX_DEV + jnp.arange(CTX_DEV, dtype=jnp.int32)
        scores = jnp.dot(query_rows, key_block.T, preferred_element_type=jnp.float32) * score_scale
        visible = key_position[None, :] <= row_limit[:, None]
        shard_max = jnp.max(jnp.where(visible, scores, -1e30), axis=1)
        weights = jnp.where(visible, jnp.exp(scores - shard_max[:, None]), 0.0).astype(jnp.bfloat16)
        shard_den = jnp.sum(weights.astype(jnp.float32), axis=1)
        shard_num = jnp.dot(weights, value_block, preferred_element_type=jnp.float32)
        run_top, run_num, run_den = running
        new_top = jnp.maximum(run_top, shard_max)
        keep = jnp.exp(run_top - new_top)
        fresh = jnp.exp(shard_max - new_top)
        return (new_top, run_num * keep[:, None] + shard_num * fresh[:, None], run_den * keep + shard_den * fresh), None

    start = (jnp.full((row_count,), -1e30, jnp.float32), jnp.zeros((row_count, head_width), jnp.float32), jnp.zeros((row_count,), jnp.float32))
    final_state, unused = lax.scan(combine_shard, start, (key_shards, value_shards, jnp.arange(shard_total, dtype=jnp.int32)))
    run_top, run_num, run_den = final_state
    return (run_num / run_den[:, None]).reshape(token_count, head_count, head_width).astype(jnp.bfloat16)
```

```python
import functools

import jax
import jax.numpy as jnp
from jax import lax
from jax.experimental import pallas as pl
from jax.experimental.pallas import tpu as pltpu
from jax.sharding import PartitionSpec as P


masked_floor = -1e30
log2_e = 1.4426950408889634
inner = 4
extra_rows = 16


def block_update(state, query, keys, values, limit, base, scale):
    shard_keys = keys.shape[0]
    scores = lax.dot_general(keys, query, (((1,), (1,)), ((), ())), preferred_element_type=jnp.float32)
    key_position = lax.broadcasted_iota(jnp.int32, scores.shape, 0)
    scores = jnp.where(key_position <= limit - base, scores, masked_floor)
    shard_max = jnp.max(scores, axis=0, keepdims=True)
    weights = jnp.exp2((scores - shard_max) * scale).astype(jnp.bfloat16)
    ones = jnp.ones((extra_rows, shard_keys), jnp.bfloat16)
    values_t = jnp.concatenate([values.T, ones], axis=0)
    sums = lax.dot_general(values_t, weights, (((1,), (0,)), ((), ())), preferred_element_type=jnp.float32)
    width = values.shape[1]
    num, den = sums[:width], sums[width : width + 1]
    if state is None:
        return shard_max, den, num
    top, run_den, run_num = state
    new_top = jnp.maximum(top, shard_max)
    keep = jnp.exp2((top - new_top) * scale)
    fresh = jnp.exp2((shard_max - new_top) * scale)
    return new_top, run_den * keep + den * fresh, run_num * keep + num * fresh


def first_kernel(scale, base_ref, q_ref, k0_ref, v0_ref, k1_ref, v1_ref, lim_ref, top_ref, den_ref, num_ref):
    query, limit = q_ref[...], lim_ref[...]
    state = block_update(None, query, k0_ref[...], v0_ref[...], limit, base_ref[0], scale)
    state = block_update(state, query, k1_ref[...], v1_ref[...], limit, base_ref[1], scale)
    top_ref[...], den_ref[...], num_ref[...] = state


def second_kernel(
    scale, base_ref, q_ref, k0_ref, v0_ref, k1_ref, v1_ref, lim_ref, top_ref, den_ref, num_ref, out_ref
):
    query, limit = q_ref[...], lim_ref[...]
    state = (top_ref[...], den_ref[...], num_ref[...])
    state = block_update(state, query, k0_ref[...], v0_ref[...], limit, base_ref[2], scale)
    top, den, num = block_update(state, query, k1_ref[...], v1_ref[...], limit, base_ref[3], scale)
    width = num.shape[0]
    level = top * scale + jnp.log2(den)
    high = level.astype(jnp.bfloat16)
    rest = level - high.astype(jnp.float32)
    middle = rest.astype(jnp.bfloat16)
    low = rest - middle.astype(jnp.float32)
    row = lax.broadcasted_iota(jnp.int32, (extra_rows, num.shape[1]), 0)
    packed = jnp.where(row == 0, high.astype(jnp.float32), jnp.where(row == 1, middle.astype(jnp.float32), low))
    out_ref[:width, :] = (num * (1.0 / den)).astype(out_ref.dtype)
    out_ref[width:, :] = packed.astype(out_ref.dtype)


def merge_kernel(count, *refs):
    parts, out_ref = refs[:count], refs[count]
    width = parts[0].shape[0] - extra_rows
    levels = []
    for part in parts:
        stats = part[width:, :].astype(jnp.float32)
        levels.append(stats[0:1] + stats[1:2] + stats[2:3])
    top = functools.reduce(jnp.maximum, levels)
    factors = [jnp.exp2(level - top) for level in levels]
    total = functools.reduce(jnp.add, factors)
    inverse = 1.0 / total
    num = sum(part[:width, :].astype(jnp.float32) * (factor * inverse) for part, factor in zip(parts, factors))
    out_ref[...] = num.T.astype(out_ref.dtype)


def local(size, queries, cache_keys, cache_values, span_offset, positions):
    own_tokens, head_count, head_width = queries.shape
    shard_keys = cache_keys.shape[0]
    outer = size // inner
    rows = own_tokens * head_count
    me = lax.axis_index("ctx")
    place = me % inner
    scale = head_width ** (-0.5) * log2_e

    def swap(array, step):
        return lax.ppermute(array, "ctx", [(i, i ^ step) for i in range(size)])

    query = queries.reshape(rows, head_width)
    far_keys, far_values = swap(cache_keys, 2), swap(cache_values, 2)
    got = [query] + [swap(query, inner * k) for k in range(1, outer)]
    near_keys, near_values = swap(cache_keys, 1), swap(cache_values, 1)
    across_keys, across_values = swap(far_keys, 1), swap(far_values, 1)

    bases = jnp.stack([me, me ^ 1, me ^ 2, me ^ 3]).astype(jnp.int32) * shard_keys
    limits = (span_offset[0] + positions).reshape(outer, inner, own_tokens)
    limits = jnp.repeat(lax.dynamic_index_in_dim(limits, place, 1, keepdims=False), head_count, axis=1)
    owner = me // inner
    limit_of = [
        lax.dynamic_slice_in_dim(limits, owner ^ k, 1, axis=0) for k in range(outer)
    ]

    per_stage = max(outer // 4, 1)
    stages = [list(range(s, s + per_stage)) for s in range(0, outer, per_stage)]

    def join(items, axis):
        return items[0] if len(items) == 1 else jnp.concatenate(items, axis=axis)

    vmem = pl.BlockSpec(memory_space=pltpu.VMEM)
    smem = pl.BlockSpec(memory_space=pltpu.SMEM)
    params = pltpu.CompilerParams(vmem_limit_bytes=40 << 20)
    stage_rows = rows * per_stage
    stat = jax.ShapeDtypeStruct((1, stage_rows), jnp.float32)

    stage_query = [join([got[k] for k in stage], 0) for stage in stages]
    stage_limit = [join([limit_of[k] for k in stage], 1) for stage in stages]
    states = [
        pl.pallas_call(
            functools.partial(first_kernel, scale),
            in_specs=[smem] + [vmem] * 6,
            out_specs=[vmem] * 3,
            out_shape=[stat, stat, jax.ShapeDtypeStruct((head_width, stage_rows), jnp.float32)],
            compiler_params=params,
            name="first",
        )(bases, q, cache_keys, cache_values, near_keys, near_values, lim)
        for q, lim in zip(stage_query, stage_limit)
    ]
    parts = {}
    for index in reversed(range(len(stages))):
        stage = stages[index]
        packed = pl.pallas_call(
            functools.partial(second_kernel, scale),
            in_specs=[smem] + [vmem] * 9,
            out_specs=vmem,
            out_shape=jax.ShapeDtypeStruct((head_width + extra_rows, stage_rows), jnp.bfloat16),
            compiler_params=params,
            name="second",
        )(
            bases, stage_query[index], far_keys, far_values, across_keys, across_values, stage_limit[index],
            *states[index],
        )
        for at, k in enumerate(stage):
            piece = packed if per_stage == 1 else packed[:, at * rows : (at + 1) * rows]
            parts[k] = piece if k == 0 else swap(piece, inner * k)
    merged = pl.pallas_call(
        functools.partial(merge_kernel, outer),
        in_specs=[vmem] * outer,
        out_specs=vmem,
        out_shape=jax.ShapeDtypeStruct((rows, head_width), jnp.bfloat16),
        compiler_params=params,
        name="merge",
    )(*[parts[k] for k in range(outer)])
    return merged.reshape(own_tokens, head_count, head_width)


def solution(mesh):
    in_specs = (P("ctx", "kvh", None), P("ctx", "kvh"), P("ctx", "kvh"), P(), P())
    out_specs = P("ctx", "kvh", None)
    step = functools.partial(local, mesh.shape["ctx"])
    return jax.shard_map(step, mesh=mesh, in_specs=in_specs, out_specs=out_specs, check_vma=False)
```

```python
import functools

import jax
import jax.numpy as jnp
from jax import lax
from jax.experimental import pallas as pl
from jax.experimental.pallas import tpu as pltpu
from jax.sharding import PartitionSpec as P


masked_floor = -1e30
log2_e = 1.4426950408889634
inner = 4
extra_rows = 16
code_span = 240.0
code_low = -120.0


def block_update(state, query, keys, values, limit, scale):
    shard_keys, width = keys.shape
    scores = lax.dot_general(keys, query, (((1,), (1,)), ((), ())), preferred_element_type=jnp.float32)
    key_position = lax.broadcasted_iota(jnp.int32, scores.shape, 0)
    scores = jnp.where(key_position <= limit, scores, masked_floor)
    shard_max = jnp.max(scores, axis=0, keepdims=True)
    weights = jnp.exp2((scores - shard_max) * scale).astype(jnp.bfloat16)
    ones = jnp.ones((extra_rows, shard_keys), jnp.bfloat16)
    values_t = jnp.concatenate([values.T, ones], axis=0)
    sums = lax.dot_general(values_t, weights, (((1,), (0,)), ((), ())), preferred_element_type=jnp.float32)
    num, den = sums[:width], sums[width : width + 1]
    if state is None:
        return shard_max, den, num
    top, run_den, run_num = state
    new_top = jnp.maximum(top, shard_max)
    keep = jnp.exp2((top - new_top) * scale)
    fresh = jnp.exp2((shard_max - new_top) * scale)
    return new_top, run_den * keep + den * fresh, run_num * keep + num * fresh


def encode(values, level):
    _, lanes = values.shape
    size = jnp.abs(values)
    peak = jnp.maximum(jnp.max(size, axis=0, keepdims=True), 1e-30).astype(jnp.bfloat16).astype(jnp.float32)
    code = jnp.exp2(size * (code_span / peak) + code_low)
    code = jnp.where(values < 0, -code, code)
    high = level.astype(jnp.bfloat16).astype(jnp.float32)
    rest = level - high
    middle = rest.astype(jnp.bfloat16).astype(jnp.float32)
    row = lax.broadcasted_iota(jnp.int32, (extra_rows, lanes), 0)
    tail = jnp.where(row == 0, high, jnp.where(row == 1, middle, jnp.where(row == 2, rest - middle, peak)))
    return code.astype(jnp.bfloat16), tail.astype(jnp.bfloat16)


def decode(codes, tail):
    codes, tail = codes.astype(jnp.float32), tail.astype(jnp.float32)
    level = tail[0:1] + tail[1:2] + tail[2:3]
    size = (jnp.log2(jnp.abs(codes)) - code_low) * (tail[3:4] * (1.0 / code_span))
    return jnp.where(codes < 0, -size, size), level


def attend_kernel(scale, rows_of, has_state, form, own_rows, *refs):
    limits_ref, q_ref = refs[:2]
    pair_refs = refs[2 : 2 + len(rows_of)]
    rest = refs[2 + len(rows_of) :]
    query = q_ref[...]
    state = None
    if has_state:
        state = tuple(ref[...] for ref in rest[:3])
        rest = rest[3:]
    for row, pair_ref in zip(rows_of, pair_refs):
        shard_keys = pair_ref.shape[0] // 2
        state = block_update(
            state, query, pair_ref[:shard_keys, :], pair_ref[shard_keys:, :], limits_ref[row : row + 1, :], scale
        )
    if form == "state":
        for ref, value in zip(rest, state):
            ref[...] = value
        return
    top, den, num = state
    width = num.shape[0]
    level = top * scale + jnp.log2(den)
    out = num * (1.0 / den)
    rest = list(rest)
    if own_rows:
        out_ref, level_ref = rest[:2]
        rest = rest[2:]
        out_ref[...] = out[:, :own_rows]
        level_ref[...] = level[:, :own_rows]
    if rest:
        code, tail = encode(out, level)
        rest[0][:width, :] = code
        rest[0][width:, :] = tail


def merge_kernel(count, *refs):
    own_ref, own_level_ref = refs[:2]
    parts, out_ref = refs[2 : 1 + count], refs[1 + count]
    width = own_ref.shape[0]
    values, levels = [own_ref[...]], [own_level_ref[...]]
    for part in parts:
        value, level = decode(part[:width, :], part[width:, :])
        values.append(value)
        levels.append(level)
    top = functools.reduce(jnp.maximum, levels)
    factors = [jnp.exp2(level - top) for level in levels]
    inverse = 1.0 / functools.reduce(jnp.add, factors)
    num = functools.reduce(jnp.add, [value * (factor * inverse) for value, factor in zip(values, factors)])
    out_ref[...] = num.T.astype(out_ref.dtype)


def local(size, queries, cache_keys, cache_values, span_offset, positions):
    own_tokens, head_count, head_width = queries.shape
    shard_keys = cache_keys.shape[0]
    outer = size // inner
    rows = own_tokens * head_count
    me = lax.axis_index("ctx")
    place, owner = me % inner, me // inner
    scale = head_width ** (-0.5) * log2_e

    def swap(array, step):
        return lax.ppermute(array, "ctx", [(i, i ^ step) for i in range(size)])

    query = queries.reshape(rows, head_width)
    own_pair = jnp.concatenate([cache_keys, cache_values], axis=0)
    far_pair = swap(own_pair, 2)
    got = [query] + [swap(query, inner * k) for k in range(1, outer)]
    near_pair = swap(own_pair, 1)

    per_stage = max(outer // 4, 1)
    stages = [list(range(s, s + per_stage)) for s in range(0, outer, per_stage)]
    stage_rows = rows * per_stage

    limits = (span_offset[0] + positions).reshape(outer, inner, own_tokens)
    limits = lax.dynamic_index_in_dim(limits, place, 1, keepdims=False)
    limits = jnp.concatenate([lax.dynamic_slice_in_dim(limits, owner ^ k, 1, axis=0) for k in range(outer)], axis=0)
    limits = jnp.repeat(limits, head_count, axis=1).reshape(len(stages), 1, stage_rows)
    bases = (me ^ lax.iota(jnp.int32, inner)) * shard_keys
    limits = (limits - bases[None, :, None]).reshape(len(stages) * inner, stage_rows)

    def join(items, axis):
        return items[0] if len(items) == 1 else jnp.concatenate(items, axis=axis)

    vmem = pl.BlockSpec(memory_space=pltpu.VMEM)
    params = pltpu.CompilerParams(vmem_limit_bytes=40 << 20)
    pairs = [own_pair, near_pair]
    stage_query = [join([got[k] for k in stage], 0) for stage in stages]
    stat = jax.ShapeDtypeStruct((1, stage_rows), jnp.float32)
    state_shapes = [stat, stat, jax.ShapeDtypeStruct((head_width, stage_rows), jnp.float32)]
    packed_shape = jax.ShapeDtypeStruct((head_width + extra_rows, stage_rows), jnp.bfloat16)
    own_shapes = [jax.ShapeDtypeStruct((head_width, rows), jnp.float32), jax.ShapeDtypeStruct((1, rows), jnp.float32)]
    chain = [limits]
    states = [None] * len(stages)

    def attend(index, blocks, form):
        own_rows = rows if form == "packed" and index == 0 else 0
        if form == "state":
            shapes = state_shapes
        else:
            shapes = (own_shapes if own_rows else []) + ([packed_shape] if index or per_stage > 1 else [])
        operands = [chain[0], stage_query[index]] + [pairs[b] for b in blocks] + list(states[index] or ())
        results = pl.pallas_call(
            functools.partial(
                attend_kernel, scale, [index * inner + b for b in blocks], states[index] is not None, form, own_rows
            ),
            in_specs=[vmem] * len(operands),
            out_specs=[vmem] * len(shapes),
            out_shape=shapes,
            compiler_params=params,
        )(*operands)
        chain[0], results = lax.optimization_barrier((chain[0], results))
        if form == "state":
            states[index] = results
        return results

    attend(0, [0], "state")
    attend(0, [1], "state")
    for index in range(1, len(stages)):
        attend(index, [0, 1], "state")

    chain[0], far_pair = lax.optimization_barrier((chain[0], far_pair))
    across_pair = swap(far_pair, 1)
    pairs += [far_pair, across_pair]
    parts = [None] * outer

    def send(index, packed):
        for at, k in enumerate(stages[index]):
            if k:
                piece = packed if per_stage == 1 else packed[:, at * rows : (at + 1) * rows]
                parts[k] = swap(piece, inner * k)

    last = len(stages) - 1
    attend(last, [2], "state")
    send(last, attend(last, [3], "packed")[0])
    for index in range(last - 1, 0, -1):
        send(index, attend(index, [2, 3], "packed")[0])
    results = attend(0, [2, 3], "packed")
    if per_stage > 1:
        send(0, results[2])
    merged = pl.pallas_call(
        functools.partial(merge_kernel, outer),
        in_specs=[vmem] * (outer + 1),
        out_specs=vmem,
        out_shape=jax.ShapeDtypeStruct((rows, head_width), jnp.bfloat16),
        compiler_params=params,
        name="merge",
    )(results[0], results[1], *parts[1:])
    return merged.reshape(own_tokens, head_count, head_width)


def solution(mesh):
    in_specs = (P("ctx", "kvh", None), P("ctx", "kvh"), P("ctx", "kvh"), P(), P())
    out_specs = P("ctx", "kvh", None)
    size = mesh.shape["ctx"]

    def body(*args):
        return local(size, *args)

    return jax.shard_map(body, mesh=mesh, in_specs=in_specs, out_specs=out_specs, check_vma=False)
```

```python
import functools

import jax
import jax.numpy as jnp
from jax import lax
from jax.experimental import pallas as pl
from jax.experimental.pallas import tpu as pltpu
from jax.sharding import PartitionSpec as P


masked_floor = -1e30
log2_e = 1.4426950408889634
inner = 4
extra_rows = 16
code_span = 240.0
code_low = -120.0


def block_update(state, query, keys, values, limit, scale):
    shard_keys, width = keys.shape
    scores = lax.dot_general(keys, query, (((1,), (1,)), ((), ())), preferred_element_type=jnp.float32)
    key_position = lax.broadcasted_iota(jnp.int32, scores.shape, 0)
    scores = jnp.where(key_position <= limit, scores, masked_floor)
    shard_max = jnp.max(scores, axis=0, keepdims=True)
    weights = jnp.exp2((scores - shard_max) * scale).astype(jnp.bfloat16)
    ones = jnp.ones((extra_rows, shard_keys), jnp.bfloat16)
    values_t = jnp.concatenate([values.T, ones], axis=0)
    sums = lax.dot_general(values_t, weights, (((1,), (0,)), ((), ())), preferred_element_type=jnp.float32)
    num, den = sums[:width], sums[width : width + 1]
    if state is None:
        return shard_max, den, num
    top, run_den, run_num = state
    new_top = jnp.maximum(top, shard_max)
    keep = jnp.exp2((top - new_top) * scale)
    fresh = jnp.exp2((shard_max - new_top) * scale)
    return new_top, run_den * keep + den * fresh, run_num * keep + num * fresh


def encode(values, level):
    _, lanes = values.shape
    size = jnp.abs(values)
    peak = jnp.maximum(jnp.max(size, axis=0, keepdims=True), 1e-30).astype(jnp.bfloat16).astype(jnp.float32)
    code = jnp.exp2(size * (code_span / peak) + code_low)
    code = jnp.where(values < 0, -code, code)
    high = level.astype(jnp.bfloat16).astype(jnp.float32)
    rest = level - high
    middle = rest.astype(jnp.bfloat16).astype(jnp.float32)
    row = lax.broadcasted_iota(jnp.int32, (extra_rows, lanes), 0)
    tail = jnp.where(row == 0, high, jnp.where(row == 1, middle, jnp.where(row == 2, rest - middle, peak)))
    return code.astype(jnp.bfloat16), tail.astype(jnp.bfloat16)


def decode(codes, tail):
    codes, tail = codes.astype(jnp.float32), tail.astype(jnp.float32)
    level = tail[0:1] + tail[1:2] + tail[2:3]
    size = (jnp.log2(jnp.abs(codes)) - code_low) * (tail[3:4] * (1.0 / code_span))
    return jnp.where(codes < 0, -size, size), level


def attend_kernel(scale, rows_of, has_state, form, own_rows, *refs):
    limits_ref, q_ref = refs[:2]
    pair_refs = refs[2 : 2 + 2 * len(rows_of)]
    rest = refs[2 + 2 * len(rows_of) :]
    query = q_ref[...]
    state = None
    if has_state:
        state = tuple(ref[...] for ref in rest[:3])
        rest = rest[3:]
    for at, row in enumerate(rows_of):
        keys, values = pair_refs[2 * at][...], pair_refs[2 * at + 1][...]
        state = block_update(state, query, keys, values, limits_ref[row : row + 1, :], scale)
    if form == "state":
        for ref, value in zip(rest, state):
            ref[...] = value
        return
    top, den, num = state
    width = num.shape[0]
    level = top * scale + jnp.log2(den)
    out = num * (1.0 / den)
    rest = list(rest)
    if own_rows:
        out_ref, level_ref = rest[:2]
        rest = rest[2:]
        out_ref[...] = out[:, :own_rows]
        level_ref[...] = level[:, :own_rows]
    if rest:
        code, tail = encode(out, level)
        rest[0][:width, :] = code
        rest[0][width:, :] = tail


def merge_kernel(count, *refs):
    own_ref, own_level_ref = refs[:2]
    parts, out_ref = refs[2 : 1 + count], refs[1 + count]
    width = own_ref.shape[0]
    values, levels = [own_ref[...]], [own_level_ref[...]]
    for part in parts:
        value, level = decode(part[:width, :], part[width:, :])
        values.append(value)
        levels.append(level)
    top = functools.reduce(jnp.maximum, levels)
    factors = [jnp.exp2(level - top) for level in levels]
    inverse = 1.0 / functools.reduce(jnp.add, factors)
    num = functools.reduce(jnp.add, [value * (factor * inverse) for value, factor in zip(values, factors)])
    out_ref[...] = num.T.astype(out_ref.dtype)


def local(size, queries, cache_keys, cache_values, span_offset, positions):
    own_tokens, head_count, head_width = queries.shape
    shard_keys = cache_keys.shape[0]
    outer = size // inner
    rows = own_tokens * head_count
    me = lax.axis_index("ctx")
    place, owner = me % inner, me // inner
    scale = head_width ** (-0.5) * log2_e

    def swap(array, step):
        return lax.ppermute(array, "ctx", [(i, i ^ step) for i in range(size)])

    query = queries.reshape(rows, head_width)
    per_stage = max(outer // 4, 1)
    stages = [list(range(s, s + per_stage)) for s in range(0, outer, per_stage)]
    last = len(stages) - 1

    far_pair = [swap(cache_keys, 2), swap(cache_values, 2)]
    near_pair = [swap(cache_keys, 1), swap(cache_values, 1)]
    got = [query] + [None] * (outer - 1)

    def gather(index):
        for k in stages[index]:
            if k:
                low = k & -k
                got[k] = swap(got[k ^ low], inner * low)

    stage_rows = rows * per_stage

    limits = (span_offset[0] + positions).reshape(outer, inner, own_tokens)
    limits = lax.dynamic_index_in_dim(limits, place, 1, keepdims=False)
    limits = jnp.concatenate([lax.dynamic_slice_in_dim(limits, owner ^ k, 1, axis=0) for k in range(outer)], axis=0)
    limits = jnp.repeat(limits, head_count, axis=1).reshape(len(stages), 1, stage_rows)
    bases = (me ^ lax.iota(jnp.int32, inner)) * shard_keys
    limits = (limits - bases[None, :, None]).reshape(len(stages) * inner, stage_rows)

    def join(items, axis):
        return items[0] if len(items) == 1 else jnp.concatenate(items, axis=axis)

    vmem = pl.BlockSpec(memory_space=pltpu.VMEM)
    params = pltpu.CompilerParams(vmem_limit_bytes=40 << 20)
    pairs = [[cache_keys, cache_values], near_pair]
    stat = jax.ShapeDtypeStruct((1, stage_rows), jnp.float32)
    state_shapes = [stat, stat, jax.ShapeDtypeStruct((head_width, stage_rows), jnp.float32)]
    packed_shape = jax.ShapeDtypeStruct((head_width + extra_rows, stage_rows), jnp.bfloat16)
    own_shapes = [jax.ShapeDtypeStruct((head_width, rows), jnp.float32), jax.ShapeDtypeStruct((1, rows), jnp.float32)]
    chain = [limits]
    states = [None] * len(stages)

    def attend(index, blocks, form):
        own_rows = rows if form == "packed" and index == 0 else 0
        if form == "state":
            shapes = state_shapes
        else:
            shapes = (own_shapes if own_rows else []) + ([packed_shape] if index or per_stage > 1 else [])
        operands = [chain[0], stage_query[index]] + [array for b in blocks for array in pairs[b]] + list(states[index] or ())
        results = pl.pallas_call(
            functools.partial(
                attend_kernel, scale, [index * inner + b for b in blocks], states[index] is not None, form, own_rows
            ),
            in_specs=[vmem] * len(operands),
            out_specs=[vmem] * len(shapes),
            out_shape=shapes,
            compiler_params=params,
        )(*operands)
        chain[0], results = lax.optimization_barrier((chain[0], results))
        if form == "state":
            states[index] = results
        return results

    def hold(*arrays):
        chain[0], arrays = lax.optimization_barrier((chain[0], arrays))
        return list(arrays)

    stage_query = [None] * len(stages)

    def ready(index):
        stage_query[index] = join([got[k] for k in stages[index]], 0)

    for index in range(len(stages) - 1):
        gather(index)
        ready(index)
    attend(0, [0], "state")
    attend(0, [1], "state")
    for index in range(1, last):
        if index == last - 1:
            source = stages[index][0]
            (got[source],) = hold(got[source])
            gather(last)
            ready(last)
        attend(index, [0, 1], "state")
    far_pair = hold(*far_pair)
    pairs += [far_pair, [swap(array, 1) for array in far_pair]]
    attend(last, [0, 1], "state")
    parts = [None] * outer

    def send(index, packed):
        for at, k in enumerate(stages[index]):
            if k:
                piece = packed if per_stage == 1 else packed[:, at * rows : (at + 1) * rows]
                parts[k] = swap(piece, inner * k)

    for index in [last - 1, last] + list(range(last - 2, 0, -1)):
        send(index, attend(index, [2, 3], "packed")[0])
    results = attend(0, [2, 3], "packed")
    if per_stage > 1:
        send(0, results[2])
    merged = pl.pallas_call(
        functools.partial(merge_kernel, outer),
        in_specs=[vmem] * (outer + 1),
        out_specs=vmem,
        out_shape=jax.ShapeDtypeStruct((rows, head_width), jnp.bfloat16),
        compiler_params=params,
        name="merge",
    )(results[0], results[1], *parts[1:])
    return merged.reshape(own_tokens, head_count, head_width)


def solution(mesh):
    in_specs = (P("ctx", "kvh", None), P("ctx", "kvh"), P("ctx", "kvh"), P(), P())
    out_specs = P("ctx", "kvh", None)
    size = mesh.shape["ctx"]

    def body(*args):
        return local(size, *args)

    return jax.shard_map(body, mesh=mesh, in_specs=in_specs, out_specs=out_specs, check_vma=False)
```

```python
import functools

import jax
import jax.numpy as jnp
from jax import lax
from jax.experimental import pallas as pl
from jax.experimental.pallas import tpu as pltpu
from jax.sharding import PartitionSpec as P


masked_floor = -1e30
log2_e = 1.4426950408889634
inner = 4
extra_rows = 16
tail_rows = 8
code_span = 240.0
code_low = -120.0


def attend_tiles(scale, query, keys, values, limits, states, scores_ref, weights_ref, values_ref):
    rows, width = query.shape
    shard_keys = keys[0].shape[0]
    tile = scores_ref.shape[2]
    chunk = min(512, shard_keys)
    chunks = shard_keys // chunk
    scaled = query.astype(jnp.float32) * scale
    high = scaled.astype(jnp.bfloat16)
    low = (scaled - high.astype(jnp.float32)).astype(jnp.bfloat16)
    query_pair = jnp.concatenate([high, low], axis=1)
    for b, value in enumerate(values):
        values_ref[b, :width, :] = value[...].T
        values_ref[b, width:, :] = jnp.ones((extra_rows, shard_keys), jnp.bfloat16)
    sublane = lax.broadcasted_iota(jnp.int32, (8, tile), 0)
    tiles = [(b, h) for b in range(len(keys)) for h in range(rows // tile)]
    count = len(tiles)
    running, tops = [None] * count, [None] * count
    states = list(states)
    for step in range(count + 2):
        for c in range(chunks):
            span = slice(c * chunk, (c + 1) * chunk)
            if step < count:
                b, h = tiles[step]
                lanes = slice(h * tile, (h + 1) * tile)
                key = keys[b][span, :]
                scores = lax.dot_general(
                    jnp.concatenate([key, key], axis=1),
                    query_pair[lanes],
                    (((1,), (1,)), ((), ())),
                    preferred_element_type=jnp.float32,
                ).reshape(chunk // 8, 8, tile)
                position = lax.broadcasted_iota(jnp.int32, scores.shape, 0) * 8 + c * chunk
                scores = jnp.where(position <= (limits[b][:, lanes] - sublane)[None], scores, masked_floor)
                peak = jnp.max(scores, axis=0)
                running[step] = peak if c == 0 else jnp.maximum(running[step], peak)
                scores_ref[step % 2, span, :] = scores.reshape(chunk, tile)
            if 1 <= step <= count:
                t = step - 1
                if c == 0:
                    tops[t] = jnp.max(running[t], axis=0, keepdims=True)
                weights_ref[t % 2, span, :] = jnp.exp2(scores_ref[t % 2, span, :] - tops[t]).astype(jnp.bfloat16)
            if step >= 2 and c == min(1, chunks - 1):
                b, h = tiles[step - 2]
                shard_max = tops[step - 2]
                sums = lax.dot_general(
                    values_ref[b],
                    weights_ref[step % 2],
                    (((1,), (0,)), ((), ())),
                    preferred_element_type=jnp.float32,
                )
                num, den = sums[:width], sums[width : width + 1]
                if states[h] is None:
                    states[h] = (shard_max, den, num)
                else:
                    top, run_den, run_num = states[h]
                    new_top = jnp.maximum(top, shard_max)
                    keep, fresh = jnp.exp2(top - new_top), jnp.exp2(shard_max - new_top)
                    states[h] = (new_top, run_den * keep + den * fresh, run_num * keep + num * fresh)
    return states


def encode(values, level):
    _, lanes = values.shape
    size = jnp.abs(values)
    peak = jnp.maximum(jnp.max(size, axis=0, keepdims=True), 1e-30).astype(jnp.bfloat16).astype(jnp.float32)
    code = jnp.exp2(size * (code_span / peak) + code_low)
    code = jnp.where(values < 0, -code, code)
    high = level.astype(jnp.bfloat16).astype(jnp.float32)
    rest = level - high
    middle = rest.astype(jnp.bfloat16).astype(jnp.float32)
    row = lax.broadcasted_iota(jnp.int32, (tail_rows, lanes), 0)
    tail = jnp.where(row == 0, high, jnp.where(row == 1, middle, jnp.where(row == 2, rest - middle, peak)))
    return code.astype(jnp.bfloat16), tail.astype(jnp.bfloat16)


def decode(codes, tail):
    codes, tail = codes.astype(jnp.float32), tail.astype(jnp.float32)
    level = tail[0:1] + tail[1:2] + tail[2:3]
    size = (jnp.log2(jnp.abs(codes)) - code_low) * (tail[3:4] * (1.0 / code_span))
    return jnp.where(codes < 0, -size, size), level


def attend_kernel(scale, rows_of, has_state, form, own_rows, *refs):
    refs, scratch = refs[:-3], refs[-3:]
    limits_ref, q_ref = refs[:2]
    keys = list(refs[2 : 2 + 2 * len(rows_of) : 2])
    values = list(refs[3 : 3 + 2 * len(rows_of) : 2])
    rest = list(refs[2 + 2 * len(rows_of) :])
    rows, width = q_ref.shape
    tile = scratch[0].shape[2]
    spans = [slice(at, at + tile) for at in range(0, rows, tile)]
    states = [None] * len(spans)
    if has_state:
        states = [tuple(ref[:, span] for ref in rest[:3]) for span in spans]
        rest = rest[3:]
    limits = [limits_ref[row : row + 1, :] for row in rows_of]
    states = attend_tiles(scale, q_ref[...], keys, values, limits, states, *scratch)
    for span, state in zip(spans, states):
        if form == "state":
            for ref, value in zip(rest, state):
                ref[:, span] = value
            continue
        top, den, num = state
        level = top + jnp.log2(den)
        out = num * (1.0 / den)
        outs = rest
        if own_rows:
            own_span = slice(span.start, min(span.stop, own_rows))
            if own_span.start < own_span.stop:
                outs[0][:, own_span] = out[:, : own_span.stop - own_span.start]
                outs[1][:, own_span] = level[:, : own_span.stop - own_span.start]
            outs = outs[2:]
        if outs:
            code, tail = encode(out, level)
            outs[0][:width, span] = code
            outs[0][width:, span] = tail


def merge_kernel(count, *refs):
    own_ref, own_level_ref = refs[:2]
    parts, out_ref = refs[2 : 1 + count], refs[1 + count]
    width = own_ref.shape[0]
    values, levels = [own_ref[...]], [own_level_ref[...]]
    for part in parts:
        value, level = decode(part[:width, :], part[width:, :])
        values.append(value)
        levels.append(level)
    top = functools.reduce(jnp.maximum, levels)
    factors = [jnp.exp2(level - top) for level in levels]
    inverse = 1.0 / functools.reduce(jnp.add, factors)
    num = functools.reduce(jnp.add, [value * (factor * inverse) for value, factor in zip(values, factors)])
    out_ref[...] = num.T.astype(out_ref.dtype)


def local(size, queries, cache_keys, cache_values, span_offset, positions):
    own_tokens, head_count, head_width = queries.shape
    shard_keys = cache_keys.shape[0]
    outer = size // inner
    rows = own_tokens * head_count
    me = lax.axis_index("ctx")
    place, owner = me % inner, me // inner
    scale = head_width ** (-0.5) * log2_e

    def swap(array, step):
        return lax.ppermute(array, "ctx", [(i, i ^ step) for i in range(size)])

    query = queries.reshape(rows, head_width)
    per_stage = max(outer // 4, 1)
    stages = [list(range(s, s + per_stage)) for s in range(0, outer, per_stage)]
    last = len(stages) - 1

    far_pair = [swap(cache_keys, 2), swap(cache_values, 2)]
    near_pair = [swap(cache_keys, 1), swap(cache_values, 1)]
    got = [query] + [None] * (outer - 1)

    def gather(index):
        for k in stages[index]:
            if k:
                low = k & -k
                got[k] = swap(got[k ^ low], inner * low)

    stage_rows = rows * per_stage
    tile = 256 if stage_rows % 256 == 0 else stage_rows

    limits = (span_offset[0] + positions).reshape(outer, inner, own_tokens)
    limits = lax.dynamic_index_in_dim(limits, place, 1, keepdims=False)
    limits = jnp.concatenate([lax.dynamic_slice_in_dim(limits, owner ^ k, 1, axis=0) for k in range(outer)], axis=0)
    limits = jnp.repeat(limits, head_count, axis=1).reshape(len(stages), 1, stage_rows)
    bases = (me ^ lax.iota(jnp.int32, inner)) * shard_keys
    limits = (limits - bases[None, :, None]).reshape(len(stages) * inner, stage_rows)

    def join(items, axis):
        return items[0] if len(items) == 1 else jnp.concatenate(items, axis=axis)

    vmem = pl.BlockSpec(memory_space=pltpu.VMEM)
    params = pltpu.CompilerParams(vmem_limit_bytes=20 << 20)
    pairs = [[cache_keys, cache_values], near_pair]
    stat = jax.ShapeDtypeStruct((1, stage_rows), jnp.float32)
    state_shapes = [stat, stat, jax.ShapeDtypeStruct((head_width, stage_rows), jnp.float32)]
    packed_shape = jax.ShapeDtypeStruct((head_width + tail_rows, stage_rows), jnp.bfloat16)
    own_shapes = [jax.ShapeDtypeStruct((head_width, rows), jnp.float32), jax.ShapeDtypeStruct((1, rows), jnp.float32)]
    chain = [limits]
    states = [None] * len(stages)

    def attend(index, blocks, form):
        own_rows = rows if form == "packed" and index == 0 else 0
        if form == "state":
            shapes = state_shapes
        else:
            shapes = (own_shapes if own_rows else []) + ([packed_shape] if index or per_stage > 1 else [])
        operands = [chain[0], stage_query[index]] + [array for b in blocks for array in pairs[b]] + list(states[index] or ())
        results = pl.pallas_call(
            functools.partial(
                attend_kernel, scale, [index * inner + b for b in blocks], states[index] is not None, form, own_rows
            ),
            in_specs=[vmem] * len(operands),
            out_specs=[vmem] * len(shapes),
            out_shape=shapes,
            scratch_shapes=[
                pltpu.VMEM((2, shard_keys, tile), jnp.float32),
                pltpu.VMEM((2, shard_keys, tile), jnp.bfloat16),
                pltpu.VMEM((len(blocks), head_width + extra_rows, shard_keys), jnp.bfloat16),
            ],
            compiler_params=params,
        )(*operands)
        chain[0], results = lax.optimization_barrier((chain[0], results))
        if form == "state":
            states[index] = results
        return results

    def hold(*arrays):
        chain[0], arrays = lax.optimization_barrier((chain[0], arrays))
        return list(arrays)

    stage_query = [None] * len(stages)

    def ready(index):
        stage_query[index] = join([got[k] for k in stages[index]], 0)

    for index in range(len(stages) - 1):
        gather(index)
        ready(index)
    attend(0, [0, 1], "state")
    for index in range(1, last):
        if index == last - 1:
            source = stages[index][0]
            (got[source],) = hold(got[source])
            gather(last)
            ready(last)
        attend(index, [0, 1], "state")
    far_pair = hold(*far_pair)
    pairs += [far_pair, [swap(array, 1) for array in far_pair]]
    attend(last, [0, 1], "state")
    parts = [None] * outer

    def send(index, packed):
        for at, k in enumerate(stages[index]):
            if k:
                piece = packed if per_stage == 1 else packed[:, at * rows : (at + 1) * rows]
                parts[k] = swap(piece, inner * k)

    for index in [last - 1, last] + list(range(last - 2, 0, -1)):
        send(index, attend(index, [2, 3], "packed")[0])
    results = attend(0, [2, 3], "packed")
    if per_stage > 1:
        send(0, results[2])
    merged = pl.pallas_call(
        functools.partial(merge_kernel, outer),
        in_specs=[vmem] * (outer + 1),
        out_specs=vmem,
        out_shape=jax.ShapeDtypeStruct((rows, head_width), jnp.bfloat16),
        compiler_params=params,
        name="merge",
    )(results[0], results[1], *parts[1:])
    return merged.reshape(own_tokens, head_count, head_width)


def solution(mesh):
    in_specs = (P("ctx", "kvh", None), P("ctx", "kvh"), P("ctx", "kvh"), P(), P())
    out_specs = P("ctx", "kvh", None)
    size = mesh.shape["ctx"]

    def body(*args):
        return local(size, *args)

    return jax.shard_map(body, mesh=mesh, in_specs=in_specs, out_specs=out_specs, check_vma=False)
```

```python
import functools

import jax
import jax.numpy as jnp
from jax import lax
from jax.experimental import pallas as pl
from jax.experimental.pallas import tpu as pltpu
from jax.sharding import PartitionSpec as P


masked_floor = -1e30
log2_e = 1.4426950408889634
inner = 4
extra_rows = 16
tail_rows = 8
code_span = 240.0
code_low = -120.0


def attend_tiles(scale, query, keys, values, limits, states, scores_ref, weights_ref, values_ref):
    rows, width = query.shape
    shard_keys = keys[0].shape[0]
    tile = scores_ref.shape[2]
    chunk = min(512, shard_keys)
    chunks = shard_keys // chunk
    scaled = query.astype(jnp.float32) * scale
    high = scaled.astype(jnp.bfloat16)
    low = (scaled - high.astype(jnp.float32)).astype(jnp.bfloat16)
    query_pair = jnp.concatenate([high, low], axis=1)
    for b, value in enumerate(values):
        values_ref[b, :width, :] = value[...].T
        values_ref[b, width:, :] = jnp.ones((extra_rows, shard_keys), jnp.bfloat16)
    sublane = lax.broadcasted_iota(jnp.int32, (8, tile), 0)
    tiles = [(b, h) for b in range(len(keys)) for h in range(rows // tile)]
    count = len(tiles)
    running, tops = [None] * count, [None] * count
    states = list(states)
    for step in range(count + 2):
        for c in range(chunks):
            span = slice(c * chunk, (c + 1) * chunk)
            if step < count:
                b, h = tiles[step]
                lanes = slice(h * tile, (h + 1) * tile)
                key = keys[b][span, :]
                scores = lax.dot_general(
                    jnp.concatenate([key, key], axis=1),
                    query_pair[lanes],
                    (((1,), (1,)), ((), ())),
                    preferred_element_type=jnp.float32,
                ).reshape(chunk // 8, 8, tile)
                position = lax.broadcasted_iota(jnp.int32, scores.shape, 0) * 8 + c * chunk
                scores = jnp.where(position <= (limits[b][:, lanes] - sublane)[None], scores, masked_floor)
                peak = jnp.max(scores, axis=0)
                running[step] = peak if c == 0 else jnp.maximum(running[step], peak)
                scores_ref[step % 2, span, :] = scores.reshape(chunk, tile)
            if 1 <= step <= count:
                t = step - 1
                if c == 0:
                    tops[t] = jnp.max(running[t], axis=0, keepdims=True)
                weights_ref[t % 2, span, :] = jnp.exp2(scores_ref[t % 2, span, :] - tops[t]).astype(jnp.bfloat16)
            if step >= 2 and c == min(1, chunks - 1):
                b, h = tiles[step - 2]
                shard_max = tops[step - 2]
                sums = lax.dot_general(
                    values_ref[b],
                    weights_ref[step % 2],
                    (((1,), (0,)), ((), ())),
                    preferred_element_type=jnp.float32,
                )
                num, den = sums[:width], sums[width : width + 1]
                if states[h] is None:
                    states[h] = (shard_max, den, num)
                else:
                    top, run_den, run_num = states[h]
                    new_top = jnp.maximum(top, shard_max)
                    keep, fresh = jnp.exp2(top - new_top), jnp.exp2(shard_max - new_top)
                    states[h] = (new_top, run_den * keep + den * fresh, run_num * keep + num * fresh)
    return states


def encode(values, level):
    _, lanes = values.shape
    size = jnp.abs(values)
    peak = jnp.maximum(jnp.max(size, axis=0, keepdims=True), 1e-30).astype(jnp.bfloat16).astype(jnp.float32)
    code = jnp.exp2(size * (code_span / peak) + code_low)
    code = jnp.where(values < 0, -code, code)
    high = level.astype(jnp.bfloat16).astype(jnp.float32)
    rest = level - high
    middle = rest.astype(jnp.bfloat16).astype(jnp.float32)
    row = lax.broadcasted_iota(jnp.int32, (tail_rows, lanes), 0)
    tail = jnp.where(row == 0, high, jnp.where(row == 1, middle, jnp.where(row == 2, rest - middle, peak)))
    return code.astype(jnp.bfloat16), tail.astype(jnp.bfloat16)


def decode(codes, tail):
    codes, tail = codes.astype(jnp.float32), tail.astype(jnp.float32)
    level = tail[0:1] + tail[1:2] + tail[2:3]
    size = (jnp.log2(jnp.abs(codes)) - code_low) * (tail[3:4] * (1.0 / code_span))
    return jnp.where(codes < 0, -size, size), level


def spread_limits(me, own_tokens, head_count, offsets_ref, span_ref, limits_ref):
    count, lanes = limits_ref.shape
    width = offsets_ref.shape[1]
    per_row = width // own_tokens
    parts = []
    for k in range(count):
        device = me ^ (k * inner)
        row = offsets_ref[pl.ds(device // per_row, 1), :]
        row = pltpu.roll(row, (width - (device % per_row) * own_tokens) % width, 1)
        parts += [row >> 8, row & 255]
    parts = jnp.concatenate(parts, axis=0).astype(jnp.float32).astype(jnp.bfloat16)
    token = lax.broadcasted_iota(jnp.int32, (width, lanes), 0)
    lane = lax.broadcasted_iota(jnp.int32, (width, lanes), 1)
    first = token * head_count
    spread = jnp.where((lane >= first) & (lane < first + head_count), 1.0, 0.0).astype(jnp.bfloat16)
    wide = lax.dot_general(parts, spread, (((1,), (0,)), ((), ())), preferred_element_type=jnp.float32)
    wide = wide.astype(jnp.int32)
    for k in range(count):
        limits_ref[k : k + 1, :] = wide[2 * k : 2 * k + 1] * 256 + wide[2 * k + 1 : 2 * k + 2] + span_ref[...]


def attend_kernel(scale, index, blocks, has_state, form, own_rows, setup, *refs):
    me = lax.axis_index("ctx")
    refs = list(refs)
    if setup:
        offsets_ref, span_ref, q_hbm, k_hbm, v_hbm = refs[:5]
        arrived, q_ref = refs.pop(), refs.pop()
        scratch = [refs.pop() for _ in range(3)][::-1]
        v_ref, k_ref, limits_ref = refs.pop(), refs.pop(), refs.pop()
        pairs = ((q_hbm, q_ref), (k_hbm, k_ref), (v_hbm, v_ref))
        copies = [pltpu.make_async_copy(*pair, arrived.at[at]) for at, pair in enumerate(pairs)]
        for copy in copies:
            copy.start()
        spread_limits(me, *setup, offsets_ref, span_ref, limits_ref)
        for copy in copies:
            copy.wait()
        refs = [limits_ref, q_ref, k_ref, v_ref] + refs[5:]
    else:
        scratch = [refs.pop() for _ in range(3)][::-1]
        limits_ref, q_ref = refs[:2]
    keys = refs[2 : 2 + 2 * len(blocks) : 2]
    values = refs[3 : 3 + 2 * len(blocks) : 2]
    rest = list(refs[2 + 2 * len(blocks) :])
    rows, width = q_ref.shape
    tile = scratch[0].shape[2]
    spans = [slice(at, at + tile) for at in range(0, rows, tile)]
    states = [None] * len(spans)
    if has_state:
        states = [tuple(ref[:, span] for ref in rest[:3]) for span in spans]
        rest = rest[3:]
    limits = [limits_ref[index : index + 1, :] - (me ^ b) * keys[0].shape[0] for b in blocks]
    states = attend_tiles(scale, q_ref[...], keys, values, limits, states, *scratch)
    for span, state in zip(spans, states):
        if form == "state":
            for ref, value in zip(rest, state):
                ref[:, span] = value
            continue
        top, den, num = state
        level = top + jnp.log2(den)
        out = num * (1.0 / den)
        outs = rest
        if own_rows:
            own_span = slice(span.start, min(span.stop, own_rows))
            if own_span.start < own_span.stop:
                outs[0][:, own_span] = out[:, : own_span.stop - own_span.start]
                outs[1][:, own_span] = level[:, : own_span.stop - own_span.start]
            outs = outs[2:]
        if outs:
            code, tail = encode(out, level)
            outs[0][:width, span] = code
            outs[0][width:, span] = tail


def merge_kernel(count, *refs):
    own_ref, own_level_ref = refs[:2]
    parts, out_ref = refs[2 : 1 + count], refs[1 + count]
    width = own_ref.shape[0]
    values, levels = [own_ref[...]], [own_level_ref[...]]
    for part in parts:
        value, level = decode(part[:width, :], part[width:, :])
        values.append(value)
        levels.append(level)
    top = functools.reduce(jnp.maximum, levels)
    factors = [jnp.exp2(level - top) for level in levels]
    inverse = 1.0 / functools.reduce(jnp.add, factors)
    num = functools.reduce(jnp.add, [value * (factor * inverse) for value, factor in zip(values, factors)])
    out_ref[...] = num.T.astype(out_ref.dtype)


def local(size, queries, cache_keys, cache_values, span_offset, positions):
    own_tokens, head_count, head_width = queries.shape
    shard_keys = cache_keys.shape[0]
    outer = size // inner
    rows = own_tokens * head_count
    me = lax.axis_index("ctx")
    place, owner = me % inner, me // inner
    scale = head_width ** (-0.5) * log2_e

    def swap(array, step):
        return lax.ppermute(array, "ctx", [(i, i ^ step) for i in range(size)])

    query = queries.reshape(rows, head_width)
    per_stage = max(outer // 4, 1)
    stages = [list(range(s, s + per_stage)) for s in range(0, outer, per_stage)]
    last = len(stages) - 1

    far_pair = [swap(cache_keys, 2), swap(cache_values, 2)]
    near_pair = [swap(cache_keys, 1), swap(cache_values, 1)]
    got = [query] + [None] * (outer - 1)

    def gather(index):
        for k in stages[index]:
            if k:
                low = k & -k
                got[k] = swap(got[k ^ low], inner * low)

    stage_rows = rows * per_stage
    tile = 256 if stage_rows % 256 == 0 else stage_rows

    fused_setup = per_stage == 1 and positions.shape[0] % 128 == 0 and 128 % own_tokens == 0
    if fused_setup:
        chain = [None]
    else:
        limits = (span_offset[0] + positions).reshape(outer, inner, own_tokens)
        limits = lax.dynamic_index_in_dim(limits, place, 1, keepdims=False)
        limits = [lax.dynamic_slice_in_dim(limits, owner ^ k, 1, axis=0) for k in range(outer)]
        limits = jnp.repeat(jnp.concatenate(limits, axis=0), head_count, axis=1)
        chain = [limits.reshape(len(stages), stage_rows)]

    def join(items, axis):
        return items[0] if len(items) == 1 else jnp.concatenate(items, axis=axis)

    vmem = pl.BlockSpec(memory_space=pltpu.VMEM)
    params = pltpu.CompilerParams(vmem_limit_bytes=20 << 20)
    pairs = [[cache_keys, cache_values], near_pair]
    stat = jax.ShapeDtypeStruct((1, stage_rows), jnp.float32)
    state_shapes = [stat, stat, jax.ShapeDtypeStruct((head_width, stage_rows), jnp.float32)]
    packed_shape = jax.ShapeDtypeStruct((head_width + tail_rows, stage_rows), jnp.bfloat16)
    own_shapes = [jax.ShapeDtypeStruct((head_width, rows), jnp.float32), jax.ShapeDtypeStruct((1, rows), jnp.float32)]
    states = [None] * len(stages)

    def attend(index, blocks, form):
        own_rows = rows if form == "packed" and index == 0 else 0
        if form == "state":
            shapes = state_shapes
        else:
            shapes = (own_shapes if own_rows else []) + ([packed_shape] if index or per_stage > 1 else [])
        setup = None
        if chain[0] is None:
            setup = (own_tokens, head_count)
            shapes = shapes + [jax.ShapeDtypeStruct((len(stages), stage_rows), jnp.int32)]
            shapes += [jax.ShapeDtypeStruct(array.shape, array.dtype) for array in pairs[0]]
            own = [pltpu.with_memory_space_constraint(array, pltpu.HBM) for array in (query, *pairs[0])]
            operands = [positions.reshape(-1, 128), span_offset.reshape(1, 1)] + own
            specs = [vmem] * 2 + [pl.BlockSpec(memory_space=pltpu.HBM)] * 3
            extra = [pltpu.VMEM(query.shape, query.dtype), pltpu.SemaphoreType.DMA((3,))]
            operands += [array for b in blocks[1:] for array in pairs[b]]
        else:
            operands = [chain[0], stage_query[index]] + [array for b in blocks for array in pairs[b]]
            operands += list(states[index] or ())
            specs, extra = [], []
        results = pl.pallas_call(
            functools.partial(attend_kernel, scale, index, blocks, states[index] is not None, form, own_rows, setup),
            in_specs=specs + [vmem] * (len(operands) - len(specs)),
            out_specs=[vmem] * len(shapes),
            out_shape=shapes,
            scratch_shapes=[
                pltpu.VMEM((2, shard_keys, tile), jnp.float32),
                pltpu.VMEM((2, shard_keys, tile), jnp.bfloat16),
                pltpu.VMEM((len(blocks), head_width + extra_rows, shard_keys), jnp.bfloat16),
            ]
            + extra,
            compiler_params=params,
        )(*operands)
        if setup:
            chain[0], pairs[0], results = results[-3], list(results[-2:]), results[:-3]
        chain[0], results = lax.optimization_barrier((chain[0], results))
        if form == "state":
            states[index] = results
        return results

    def hold(*arrays):
        chain[0], arrays = lax.optimization_barrier((chain[0], arrays))
        return list(arrays)

    stage_query = [None] * len(stages)

    def ready(index):
        stage_query[index] = join([got[k] for k in stages[index]], 0)

    for index in range(len(stages) - 1):
        gather(index)
        ready(index)
    attend(0, [0, 1], "state")
    source = stages[last][0] ^ (stages[last][0] & -stages[last][0])
    (got[source],) = hold(got[source])
    gather(last)
    ready(last)
    for index in range(1, last):
        attend(index, [0, 1], "state")
    far_pair = hold(*far_pair)
    pairs += [far_pair, [swap(array, 1) for array in far_pair]]
    attend(last, [0, 1], "state")
    parts = [None] * outer

    def send(index, packed):
        for at, k in enumerate(stages[index]):
            if k:
                piece = packed if per_stage == 1 else packed[:, at * rows : (at + 1) * rows]
                parts[k] = swap(piece, inner * k)

    for index in [last - 1, last] + list(range(last - 2, 0, -1)):
        send(index, attend(index, [2, 3], "packed")[0])
    results = attend(0, [2, 3], "packed")
    if per_stage > 1:
        send(0, results[2])
    merged = pl.pallas_call(
        functools.partial(merge_kernel, outer),
        in_specs=[vmem] * (outer + 1),
        out_specs=vmem,
        out_shape=jax.ShapeDtypeStruct((rows, head_width), jnp.bfloat16),
        compiler_params=params,
        name="merge",
    )(results[0], results[1], *parts[1:])
    return merged.reshape(own_tokens, head_count, head_width)


def solution(mesh):
    in_specs = (P("ctx", "kvh", None), P("ctx", "kvh"), P("ctx", "kvh"), P(), P())
    out_specs = P("ctx", "kvh", None)
    size = mesh.shape["ctx"]

    def body(*args):
        return local(size, *args)

    return jax.shard_map(body, mesh=mesh, in_specs=in_specs, out_specs=out_specs, check_vma=False)
```

```python
import functools

import jax
import jax.numpy as jnp
from jax import lax
from jax.experimental import pallas as pl
from jax.experimental.pallas import tpu as pltpu
from jax.sharding import PartitionSpec as P


masked_floor = -1e30
log2_e = 1.4426950408889634
inner = 4
extra_rows = 16
tail_rows = 8
code_span = 240.0
code_low = -120.0


def attend_tiles(scale, query, keys, values, limits, states, scores_ref, weights_ref, values_ref):
    rows, width = query.shape
    shard_keys = keys[0].shape[0]
    tile = scores_ref.shape[2]
    chunk = min(512, shard_keys)
    chunks = shard_keys // chunk
    scaled = query.astype(jnp.float32) * scale
    high = scaled.astype(jnp.bfloat16)
    low = (scaled - high.astype(jnp.float32)).astype(jnp.bfloat16)
    query_pair = jnp.concatenate([high, low], axis=1)
    for b, value in enumerate(values):
        values_ref[b, :width, :] = value[...].T
        values_ref[b, width:, :] = jnp.ones((extra_rows, shard_keys), jnp.bfloat16)
    sublane = lax.broadcasted_iota(jnp.int32, (8, tile), 0)
    tiles = [(b, h) for b in range(len(keys)) for h in range(rows // tile)]
    count = len(tiles)
    running, tops = [None] * count, [None] * count
    states = list(states)
    for step in range(count + 2):
        for c in range(chunks):
            span = slice(c * chunk, (c + 1) * chunk)
            if step < count:
                b, h = tiles[step]
                lanes = slice(h * tile, (h + 1) * tile)
                key = keys[b][span, :]
                scores = lax.dot_general(
                    jnp.concatenate([key, key], axis=1),
                    query_pair[lanes],
                    (((1,), (1,)), ((), ())),
                    preferred_element_type=jnp.float32,
                ).reshape(chunk // 8, 8, tile)
                position = lax.broadcasted_iota(jnp.int32, scores.shape, 0) * 8 + c * chunk
                scores = jnp.where(position <= (limits[b][:, lanes] - sublane)[None], scores, masked_floor)
                peak = jnp.max(scores, axis=0)
                running[step] = peak if c == 0 else jnp.maximum(running[step], peak)
                scores_ref[step % 2, span, :] = scores.reshape(chunk, tile)
            if 1 <= step <= count:
                t = step - 1
                if c == 0:
                    tops[t] = jnp.max(running[t], axis=0, keepdims=True)
                weights_ref[t % 2, span, :] = jnp.exp2(scores_ref[t % 2, span, :] - tops[t]).astype(jnp.bfloat16)
            if step >= 2 and c == min(1, chunks - 1):
                b, h = tiles[step - 2]
                shard_max = tops[step - 2]
                sums = lax.dot_general(
                    values_ref[b],
                    weights_ref[step % 2],
                    (((1,), (0,)), ((), ())),
                    preferred_element_type=jnp.float32,
                )
                num, den = sums[:width], sums[width : width + 1]
                if states[h] is None:
                    states[h] = (shard_max, den, num)
                else:
                    top, run_den, run_num = states[h]
                    new_top = jnp.maximum(top, shard_max)
                    keep, fresh = jnp.exp2(top - new_top), jnp.exp2(shard_max - new_top)
                    states[h] = (new_top, run_den * keep + den * fresh, run_num * keep + num * fresh)
    return states


def encode(values, level):
    _, lanes = values.shape
    size = jnp.abs(values)
    peak = jnp.maximum(jnp.max(size, axis=0, keepdims=True), 1e-30).astype(jnp.bfloat16).astype(jnp.float32)
    code = jnp.exp2(size * (code_span / peak) + code_low)
    code = jnp.where(values < 0, -code, code)
    high = level.astype(jnp.bfloat16).astype(jnp.float32)
    rest = level - high
    middle = rest.astype(jnp.bfloat16).astype(jnp.float32)
    row = lax.broadcasted_iota(jnp.int32, (tail_rows, lanes), 0)
    tail = jnp.where(row == 0, high, jnp.where(row == 1, middle, jnp.where(row == 2, rest - middle, peak)))
    return code.astype(jnp.bfloat16), tail.astype(jnp.bfloat16)


def decode(codes, tail):
    codes, tail = codes.astype(jnp.float32), tail.astype(jnp.float32)
    level = tail[0:1] + tail[1:2] + tail[2:3]
    size = (jnp.log2(jnp.abs(codes)) - code_low) * (tail[3:4] * (1.0 / code_span))
    return jnp.where(codes < 0, -size, size), level


def spread_limits(me, own_tokens, head_count, offsets_ref, span_ref, limits_ref):
    count, lanes = limits_ref.shape
    width = offsets_ref.shape[1]
    per_row = width // own_tokens
    parts = []
    for k in range(count):
        device = me ^ (k * inner)
        row = offsets_ref[pl.ds(device // per_row, 1), :]
        row = pltpu.roll(row, (width - (device % per_row) * own_tokens) % width, 1)
        parts += [row >> 8, row & 255]
    parts = jnp.concatenate(parts, axis=0).astype(jnp.float32).astype(jnp.bfloat16)
    token = lax.broadcasted_iota(jnp.int32, (width, lanes), 0)
    lane = lax.broadcasted_iota(jnp.int32, (width, lanes), 1)
    first = token * head_count
    spread = jnp.where((lane >= first) & (lane < first + head_count), 1.0, 0.0).astype(jnp.bfloat16)
    wide = lax.dot_general(parts, spread, (((1,), (0,)), ((), ())), preferred_element_type=jnp.float32)
    wide = wide.astype(jnp.int32)
    for k in range(count):
        limits_ref[k : k + 1, :] = wide[2 * k : 2 * k + 1] * 256 + wide[2 * k + 1 : 2 * k + 2] + span_ref[...]


def attend_kernel(scale, index, blocks, has_state, plan, setup, *refs):
    me = lax.axis_index("ctx")
    refs = list(refs)
    if setup:
        offsets_ref, span_ref, q_hbm, k_hbm, v_hbm = refs[:5]
        arrived, q_ref = refs.pop(), refs.pop()
        scratch = [refs.pop() for _ in range(3)][::-1]
        v_ref, k_ref, limits_ref = refs.pop(), refs.pop(), refs.pop()
        pairs = ((q_hbm, q_ref), (k_hbm, k_ref), (v_hbm, v_ref))
        copies = [pltpu.make_async_copy(*pair, arrived.at[at]) for at, pair in enumerate(pairs)]
        for copy in copies:
            copy.start()
        spread_limits(me, *setup, offsets_ref, span_ref, limits_ref)
        for copy in copies:
            copy.wait()
        refs = [limits_ref, q_ref, k_ref, v_ref] + refs[5:]
    else:
        scratch = [refs.pop() for _ in range(3)][::-1]
        limits_ref, q_ref = refs[:2]
    keys = refs[2 : 2 + 2 * len(blocks) : 2]
    values = refs[3 : 3 + 2 * len(blocks) : 2]
    rest = list(refs[2 + 2 * len(blocks) :])
    rows, _ = q_ref.shape
    tile = scratch[0].shape[2]
    spans = [slice(at, at + tile) for at in range(0, rows, tile)]
    states = [None] * len(spans)
    if has_state:
        states = [tuple(ref[:, span] for ref in rest[:3]) for span in spans]
        rest = rest[3:]
    limits = [limits_ref[index : index + 1, :] - (me ^ b) * keys[0].shape[0] for b in blocks]
    states = attend_tiles(scale, q_ref[...], keys, values, limits, states, *scratch)
    if plan is None:
        for span, state in zip(spans, states):
            for ref, value in zip(rest, state):
                ref[:, span] = value
        return
    for at, form, out, offset, count in plan:
        top, den, num = (value[:, :count] for value in states[at])
        write_partial(rest[out:], form, slice(offset, offset + count), num * (1.0 / den), top + jnp.log2(den))


def write_partial(refs, form, span, value, level):
    width = value.shape[0]
    if form == "float":
        refs[0][:, span] = value
        refs[1][:, span] = level
    else:
        code, tail = encode(value, level)
        refs[0][:width, span] = code
        refs[0][width:, span] = tail


def combine(values, levels):
    top = functools.reduce(jnp.maximum, levels)
    factors = [jnp.exp2(level - top) for level in levels]
    total = functools.reduce(jnp.add, factors)
    inverse = 1.0 / total
    value = functools.reduce(jnp.add, [value * (factor * inverse) for value, factor in zip(values, factors)])
    return value, top + jnp.log2(total)


def combine_kernel(value_ref, level_ref, part_ref, out_ref):
    width, lanes = value_ref.shape
    value, level = decode(part_ref[:width, :], part_ref[width:, :])
    value, level = combine([value_ref[...], value], [level_ref[...], level])
    write_partial([out_ref], "code", slice(0, lanes), value, level)


def merge_kernel(groups, *refs):
    own_ref, own_level_ref = refs[:2]
    parts, out_ref = refs[2:-1], refs[-1]
    width = own_ref.shape[0]
    for span, members in groups:
        values, levels = [own_ref[:, span]], [own_level_ref[:, span]]
        for at, offset in members:
            lanes = slice(offset, offset + span.stop - span.start)
            value, level = decode(parts[at][:width, lanes], parts[at][width:, lanes])
            values.append(value)
            levels.append(level)
        out_ref[span, :] = combine(values, levels)[0].T.astype(out_ref.dtype)


def local(size, queries, cache_keys, cache_values, span_offset, positions):
    own_tokens, head_count, head_width = queries.shape
    shard_keys = cache_keys.shape[0]
    outer = size // inner
    rows = own_tokens * head_count
    me = lax.axis_index("ctx")
    place, owner = me % inner, me // inner
    scale = head_width ** (-0.5) * log2_e

    def swap(array, step):
        return lax.ppermute(array, "ctx", [(i, i ^ step) for i in range(size)])

    query = queries.reshape(rows, head_width)
    per_stage = max(outer // 4, 1)
    stages = [list(range(s, s + per_stage)) for s in range(0, outer, per_stage)]
    last = len(stages) - 1

    far_pair = [swap(cache_keys, 2), swap(cache_values, 2)]
    near_pair = [swap(cache_keys, 1), swap(cache_values, 1)]
    got = [query] + [None] * (outer - 1)

    def gather(index):
        for k in stages[index]:
            if k:
                low = k & -k
                got[k] = swap(got[k ^ low], inner * low)

    stage_rows = rows * per_stage
    tile = 256 if stage_rows % 256 == 0 else stage_rows

    fused_setup = per_stage == 1 and positions.shape[0] % 128 == 0 and 128 % own_tokens == 0
    if fused_setup:
        chain = [None]
    else:
        limits = (span_offset[0] + positions).reshape(outer, inner, own_tokens)
        limits = lax.dynamic_index_in_dim(limits, place, 1, keepdims=False)
        limits = [lax.dynamic_slice_in_dim(limits, owner ^ k, 1, axis=0) for k in range(outer)]
        limits = jnp.repeat(jnp.concatenate(limits, axis=0), head_count, axis=1)
        chain = [limits.reshape(len(stages), stage_rows)]

    def join(items, axis):
        return items[0] if len(items) == 1 else jnp.concatenate(items, axis=axis)

    vmem = pl.BlockSpec(memory_space=pltpu.VMEM)
    params = pltpu.CompilerParams(vmem_limit_bytes=20 << 20)
    pairs = [[cache_keys, cache_values], near_pair]
    stat = jax.ShapeDtypeStruct((1, stage_rows), jnp.float32)
    state_shapes = [stat, stat, jax.ShapeDtypeStruct((head_width, stage_rows), jnp.float32)]

    def packed_shape(lanes):
        return jax.ShapeDtypeStruct((head_width + tail_rows, lanes), jnp.bfloat16)

    def float_shapes(lanes):
        return [jax.ShapeDtypeStruct((size_of, lanes), jnp.float32) for size_of in (head_width, 1)]

    tiles = range(stage_rows // tile)
    whole_plan = [(at, "code", 0, at * tile, tile) for at in tiles]
    states = [None] * len(stages)

    def attend(index, blocks, plan=None, shapes=state_shapes):
        setup = None
        if chain[0] is None:
            setup = (own_tokens, head_count)
            shapes = shapes + [jax.ShapeDtypeStruct((len(stages), stage_rows), jnp.int32)]
            shapes += [jax.ShapeDtypeStruct(array.shape, array.dtype) for array in pairs[0]]
            own = [pltpu.with_memory_space_constraint(array, pltpu.HBM) for array in (query, *pairs[0])]
            operands = [positions.reshape(-1, 128), span_offset.reshape(1, 1)] + own
            specs = [vmem] * 2 + [pl.BlockSpec(memory_space=pltpu.HBM)] * 3
            extra = [pltpu.VMEM(query.shape, query.dtype), pltpu.SemaphoreType.DMA((3,))]
            operands += [array for b in blocks[1:] for array in pairs[b]]
        else:
            operands = [chain[0], stage_query[index]] + [array for b in blocks for array in pairs[b]]
            operands += list(states[index] or ())
            specs, extra = [], []
        results = pl.pallas_call(
            functools.partial(
                attend_kernel, scale, index, blocks, states[index] is not None, plan, setup
            ),
            in_specs=specs + [vmem] * (len(operands) - len(specs)),
            out_specs=[vmem] * len(shapes),
            out_shape=shapes,
            scratch_shapes=[
                pltpu.VMEM((2, shard_keys, tile), jnp.float32),
                pltpu.VMEM((2, shard_keys, tile), jnp.bfloat16),
                pltpu.VMEM((len(blocks), head_width + extra_rows, shard_keys), jnp.bfloat16),
            ]
            + extra,
            compiler_params=params,
        )(*operands)
        if setup:
            chain[0], pairs[0], results = results[-3], list(results[-2:]), results[:-3]
        chain[0], results = lax.optimization_barrier((chain[0], results))
        if plan is None:
            states[index] = results
        return results

    def hold(*arrays):
        chain[0], arrays = lax.optimization_barrier((chain[0], arrays))
        return list(arrays)

    stage_query = [None] * len(stages)

    def ready(index):
        stage_query[index] = join([got[k] for k in stages[index]], 0)

    for index in range(len(stages) - 1):
        gather(index)
        ready(index)
    attend(0, [0, 1])
    source = stages[last][0] ^ (stages[last][0] & -stages[last][0])
    (got[source],) = hold(got[source])
    gather(last)
    ready(last)
    for index in range(1, last):
        attend(index, [0, 1])
    far_pair = hold(*far_pair)
    pairs += [far_pair, [swap(array, 1) for array in far_pair]]
    attend(last, [0, 1])
    own_plan = [(at, "float", 0, at * tile, tile) for at in tiles]
    if outer == 4 and stage_rows == 2 * tile:
        halves = [slice(0, tile), slice(tile, 2 * tile)]
        plan = [(0, "code", 0, 0, tile), (1, "code", 1, 0, tile)]
        direct, handed = attend(3, [2, 3], plan, [packed_shape(tile)] * 2)
        handed = swap(handed, inner)
        third = swap(direct, 3 * inner)
        plan = [(0, "code", 0, 0, tile), (1, "float", 1, 0, tile)]
        direct, value, level = attend(2, [2, 3], plan, [packed_shape(tile)] + float_shapes(tile))
        second = swap(direct, 2 * inner)
        (packed,) = attend(1, [2, 3], whole_plan, [packed_shape(stage_rows)])
        first = swap(packed, inner)
        (handed,) = hold(handed)
        joined = pl.pallas_call(
            combine_kernel,
            in_specs=[vmem] * 3,
            out_specs=vmem,
            out_shape=packed_shape(tile),
            compiler_params=params,
            name="combine",
        )(value, level, handed)
        (joined,) = hold(joined)
        joined = swap(joined, 2 * inner)
        own = attend(0, [2, 3], own_plan, float_shapes(stage_rows))
        parts = [first, second, third, joined]
        groups = [(halves[0], [(0, 0), (1, 0), (2, 0)]), (halves[1], [(0, tile), (3, 0)])]
    else:
        parts = []

        def send(index, packed):
            for at, k in enumerate(stages[index]):
                if k:
                    piece = packed if per_stage == 1 else packed[:, at * rows : (at + 1) * rows]
                    parts.append(swap(piece, inner * k))

        for index in range(last, 0, -1):
            send(index, attend(index, [2, 3], whole_plan, [packed_shape(stage_rows)])[0])
        if per_stage == 1:
            own = attend(0, [2, 3], own_plan, float_shapes(rows))
        else:
            own_plan = [(0, "float", 1, 0, rows)]
            packed, *own = attend(
                0, [2, 3], whole_plan + own_plan, [packed_shape(stage_rows)] + float_shapes(rows)
            )
            send(0, packed)
        groups = [(slice(0, rows), [(at, 0) for at in range(len(parts))])]
    merged = pl.pallas_call(
        functools.partial(merge_kernel, groups),
        in_specs=[vmem] * (2 + len(parts)),
        out_specs=vmem,
        out_shape=jax.ShapeDtypeStruct((rows, head_width), jnp.bfloat16),
        compiler_params=params,
        name="merge",
    )(*own, *parts)
    return merged.reshape(own_tokens, head_count, head_width)


def solution(mesh):
    in_specs = (P("ctx", "kvh", None), P("ctx", "kvh"), P("ctx", "kvh"), P(), P())
    out_specs = P("ctx", "kvh", None)
    size = mesh.shape["ctx"]

    def body(*args):
        return local(size, *args)

    return jax.shard_map(body, mesh=mesh, in_specs=in_specs, out_specs=out_specs, check_vma=False)
```

```python
import functools

import jax
import jax.numpy as jnp
from jax import lax
from jax.experimental import pallas as pl
from jax.experimental.pallas import tpu as pltpu
from jax.sharding import PartitionSpec as P


masked_floor = -1e30
log2_e = 1.4426950408889634
inner = 4
extra_rows = 16
tail_rows = 8
code_span = 240.0
code_low = -120.0


def attend_tiles(scale, query, keys, values, limits, states, scores_ref, weights_ref, values_ref):
    rows, width = query.shape
    shard_keys = keys[0].shape[0]
    tile = scores_ref.shape[2]
    chunk = min(512, shard_keys)
    chunks = shard_keys // chunk
    scaled = query.astype(jnp.float32) * scale
    high = scaled.astype(jnp.bfloat16)
    low = (scaled - high.astype(jnp.float32)).astype(jnp.bfloat16)
    query_pair = jnp.concatenate([high, low], axis=1)
    for b, value in enumerate(values):
        values_ref[b, :width, :] = value[...].T
        values_ref[b, width:, :] = jnp.ones((extra_rows, shard_keys), jnp.bfloat16)
    sublane = lax.broadcasted_iota(jnp.int32, (8, tile), 0)
    tiles = [(b, h) for b in range(len(keys)) for h in range(rows // tile)]
    count = len(tiles)
    running, tops = [None] * count, [None] * count
    states = list(states)
    for step in range(count + 2):
        for c in range(chunks):
            span = slice(c * chunk, (c + 1) * chunk)
            if step < count:
                b, h = tiles[step]
                lanes = slice(h * tile, (h + 1) * tile)
                key = keys[b][span, :]
                scores = lax.dot_general(
                    jnp.concatenate([key, key], axis=1),
                    query_pair[lanes],
                    (((1,), (1,)), ((), ())),
                    preferred_element_type=jnp.float32,
                ).reshape(chunk // 8, 8, tile)
                position = lax.broadcasted_iota(jnp.int32, scores.shape, 0) * 8 + c * chunk
                scores = jnp.where(position <= (limits[b][:, lanes] - sublane)[None], scores, masked_floor)
                peak = jnp.max(scores, axis=0)
                running[step] = peak if c == 0 else jnp.maximum(running[step], peak)
                scores_ref[step % 2, span, :] = scores.reshape(chunk, tile)
            if 1 <= step <= count:
                t = step - 1
                if c == 0:
                    tops[t] = jnp.max(running[t], axis=0, keepdims=True)
                weights_ref[t % 2, span, :] = jnp.exp2(scores_ref[t % 2, span, :] - tops[t]).astype(jnp.bfloat16)
            if step >= 2 and c == min(1, chunks - 1):
                b, h = tiles[step - 2]
                shard_max = tops[step - 2]
                sums = lax.dot_general(
                    values_ref[b],
                    weights_ref[step % 2],
                    (((1,), (0,)), ((), ())),
                    preferred_element_type=jnp.float32,
                )
                num, den = sums[:width], sums[width : width + 1]
                if states[h] is None:
                    states[h] = (shard_max, den, num)
                else:
                    top, run_den, run_num = states[h]
                    new_top = jnp.maximum(top, shard_max)
                    keep, fresh = jnp.exp2(top - new_top), jnp.exp2(shard_max - new_top)
                    states[h] = (new_top, run_den * keep + den * fresh, run_num * keep + num * fresh)
    return states


def encode(values, level):
    _, lanes = values.shape
    size = jnp.abs(values)
    peak = jnp.maximum(jnp.max(size, axis=0, keepdims=True), 1e-30).astype(jnp.bfloat16).astype(jnp.float32)
    code = jnp.exp2(size * (code_span / peak) + code_low)
    code = jnp.where(values < 0, -code, code)
    high = level.astype(jnp.bfloat16).astype(jnp.float32)
    rest = level - high
    middle = rest.astype(jnp.bfloat16).astype(jnp.float32)
    row = lax.broadcasted_iota(jnp.int32, (tail_rows, lanes), 0)
    tail = jnp.where(row == 0, high, jnp.where(row == 1, middle, jnp.where(row == 2, rest - middle, peak)))
    return code.astype(jnp.bfloat16), tail.astype(jnp.bfloat16)


def decode(codes, tail):
    codes, tail = codes.astype(jnp.float32), tail.astype(jnp.float32)
    level = tail[0:1] + tail[1:2] + tail[2:3]
    size = (jnp.log2(jnp.abs(codes)) - code_low) * (tail[3:4] * (1.0 / code_span))
    return jnp.where(codes < 0, -size, size), level


def spread_limits(me, own_tokens, head_count, offsets_ref, span_ref, limits_ref):
    count, lanes = limits_ref.shape
    width = offsets_ref.shape[1]
    per_row = width // own_tokens
    parts = []
    for k in range(count):
        device = me ^ (k * inner)
        row = offsets_ref[pl.ds(device // per_row, 1), :]
        row = pltpu.roll(row, (width - (device % per_row) * own_tokens) % width, 1)
        parts += [row >> 8, row & 255]
    parts = jnp.concatenate(parts, axis=0).astype(jnp.float32).astype(jnp.bfloat16)
    token = lax.broadcasted_iota(jnp.int32, (width, lanes), 0)
    lane = lax.broadcasted_iota(jnp.int32, (width, lanes), 1)
    first = token * head_count
    spread = jnp.where((lane >= first) & (lane < first + head_count), 1.0, 0.0).astype(jnp.bfloat16)
    wide = lax.dot_general(parts, spread, (((1,), (0,)), ((), ())), preferred_element_type=jnp.float32)
    wide = wide.astype(jnp.int32)
    for k in range(count):
        limits_ref[k : k + 1, :] = wide[2 * k : 2 * k + 1] * 256 + wide[2 * k + 1 : 2 * k + 2] + span_ref[...]


def attend_kernel(scale, index, blocks, has_state, plan, setup, *refs):
    me = lax.axis_index("ctx")
    refs = list(refs)
    if setup:
        offsets_ref, span_ref, q_hbm, k_hbm, v_hbm = refs[:5]
        arrived, q_ref = refs.pop(), refs.pop()
        scratch = [refs.pop() for _ in range(3)][::-1]
        v_ref, k_ref, limits_ref = refs.pop(), refs.pop(), refs.pop()
        pairs = ((q_hbm, q_ref), (k_hbm, k_ref), (v_hbm, v_ref))
        copies = [pltpu.make_async_copy(*pair, arrived.at[at]) for at, pair in enumerate(pairs)]
        for copy in copies:
            copy.start()
        spread_limits(me, *setup, offsets_ref, span_ref, limits_ref)
        for copy in copies:
            copy.wait()
        refs = [limits_ref, q_ref, k_ref, v_ref] + refs[5:]
    else:
        scratch = [refs.pop() for _ in range(3)][::-1]
        limits_ref, q_ref = refs[:2]
    keys = refs[2 : 2 + 2 * len(blocks) : 2]
    values = refs[3 : 3 + 2 * len(blocks) : 2]
    rest = list(refs[2 + 2 * len(blocks) :])
    rows, _ = q_ref.shape
    tile = scratch[0].shape[2]
    spans = [slice(at, at + tile) for at in range(0, rows, tile)]
    states = [None] * len(spans)
    if has_state:
        states = [tuple(ref[:, span] for ref in rest[:3]) for span in spans]
        rest = rest[3:]
    limits = [limits_ref[index : index + 1, :] - (me ^ b) * keys[0].shape[0] for b in blocks]
    states = attend_tiles(scale, q_ref[...], keys, values, limits, states, *scratch)
    if plan is None:
        for span, state in zip(spans, states):
            for ref, value in zip(rest, state):
                ref[:, span] = value
        return
    for at, form, out, offset, count in plan:
        top, den, num = (value[:, :count] for value in states[at])
        write_partial(rest[out:], form, slice(offset, offset + count), num * (1.0 / den), top + jnp.log2(den))


def write_partial(refs, form, span, value, level):
    width = value.shape[0]
    if form == "float":
        refs[0][:, span] = value
        refs[1][:, span] = level
    else:
        code, tail = encode(value, level)
        refs[0][:width, span] = code
        refs[0][width:, span] = tail


def combine(values, levels):
    top = functools.reduce(jnp.maximum, levels)
    factors = [jnp.exp2(level - top) for level in levels]
    total = functools.reduce(jnp.add, factors)
    inverse = 1.0 / total
    value = functools.reduce(jnp.add, [value * (factor * inverse) for value, factor in zip(values, factors)])
    return value, top + jnp.log2(total)


def merge_kernel(groups, *refs):
    own_ref, own_level_ref = refs[:2]
    parts, out_ref = refs[2:-1], refs[-1]
    width = own_ref.shape[0]
    for span, members in groups:
        values, levels = [own_ref[:, span]], [own_level_ref[:, span]]
        for at, offset in members:
            lanes = slice(offset, offset + span.stop - span.start)
            value, level = decode(parts[at][:width, lanes], parts[at][width:, lanes])
            values.append(value)
            levels.append(level)
        out_ref[span, :] = combine(values, levels)[0].T.astype(out_ref.dtype)


def local(size, queries, cache_keys, cache_values, span_offset, positions):
    own_tokens, head_count, head_width = queries.shape
    shard_keys = cache_keys.shape[0]
    outer = size // inner
    rows = own_tokens * head_count
    me = lax.axis_index("ctx")
    place, owner = me % inner, me // inner
    scale = head_width ** (-0.5) * log2_e

    def swap(array, step):
        return lax.ppermute(array, "ctx", [(i, i ^ step) for i in range(size)])

    query = queries.reshape(rows, head_width)
    per_stage = max(outer // 4, 1)
    stages = [list(range(s, s + per_stage)) for s in range(0, outer, per_stage)]
    last = len(stages) - 1

    far_pair = [swap(cache_keys, 2), swap(cache_values, 2)]
    near_pair = [swap(cache_keys, 1), swap(cache_values, 1)]
    got = [query] + [None] * (outer - 1)

    def gather(index):
        for k in stages[index]:
            if k:
                low = k & -k
                got[k] = swap(got[k ^ low], inner * low)

    stage_rows = rows * per_stage
    tile = 256 if stage_rows % 256 == 0 else stage_rows

    fused_setup = per_stage == 1 and positions.shape[0] % 128 == 0 and 128 % own_tokens == 0
    if fused_setup:
        chain = [None]
    else:
        limits = (span_offset[0] + positions).reshape(outer, inner, own_tokens)
        limits = lax.dynamic_index_in_dim(limits, place, 1, keepdims=False)
        limits = [lax.dynamic_slice_in_dim(limits, owner ^ k, 1, axis=0) for k in range(outer)]
        limits = jnp.repeat(jnp.concatenate(limits, axis=0), head_count, axis=1)
        chain = [limits.reshape(len(stages), stage_rows)]

    def join(items, axis):
        return items[0] if len(items) == 1 else jnp.concatenate(items, axis=axis)

    vmem = pl.BlockSpec(memory_space=pltpu.VMEM)
    params = pltpu.CompilerParams(vmem_limit_bytes=20 << 20)
    pairs = [[cache_keys, cache_values], near_pair]
    stat = jax.ShapeDtypeStruct((1, stage_rows), jnp.float32)
    state_shapes = [stat, stat, jax.ShapeDtypeStruct((head_width, stage_rows), jnp.float32)]

    def packed_shape(lanes):
        return jax.ShapeDtypeStruct((head_width + tail_rows, lanes), jnp.bfloat16)

    def float_shapes(lanes):
        return [jax.ShapeDtypeStruct((size_of, lanes), jnp.float32) for size_of in (head_width, 1)]

    tiles = range(stage_rows // tile)
    whole_plan = [(at, "code", 0, at * tile, tile) for at in tiles]
    states = [None] * len(stages)

    def attend(index, blocks, plan=None, shapes=state_shapes):
        setup = None
        if chain[0] is None:
            setup = (own_tokens, head_count)
            shapes = shapes + [jax.ShapeDtypeStruct((len(stages), stage_rows), jnp.int32)]
            shapes += [jax.ShapeDtypeStruct(array.shape, array.dtype) for array in pairs[0]]
            own = [pltpu.with_memory_space_constraint(array, pltpu.HBM) for array in (query, *pairs[0])]
            operands = [positions.reshape(-1, 128), span_offset.reshape(1, 1)] + own
            specs = [vmem] * 2 + [pl.BlockSpec(memory_space=pltpu.HBM)] * 3
            extra = [pltpu.VMEM(query.shape, query.dtype), pltpu.SemaphoreType.DMA((3,))]
            operands += [array for b in blocks[1:] for array in pairs[b]]
        else:
            operands = [chain[0], stage_query[index]] + [array for b in blocks for array in pairs[b]]
            operands += list(states[index] or ())
            specs, extra = [], []
        results = pl.pallas_call(
            functools.partial(
                attend_kernel, scale, index, blocks, states[index] is not None, plan, setup
            ),
            in_specs=specs + [vmem] * (len(operands) - len(specs)),
            out_specs=[vmem] * len(shapes),
            out_shape=shapes,
            scratch_shapes=[
                pltpu.VMEM((2, shard_keys, tile), jnp.float32),
                pltpu.VMEM((2, shard_keys, tile), jnp.bfloat16),
                pltpu.VMEM((len(blocks), head_width + extra_rows, shard_keys), jnp.bfloat16),
            ]
            + extra,
            compiler_params=params,
        )(*operands)
        if setup:
            chain[0], pairs[0], results = results[-3], list(results[-2:]), results[:-3]
        chain[0], results = lax.optimization_barrier((chain[0], results))
        if plan is None:
            states[index] = results
        return results

    def hold(*arrays):
        chain[0], arrays = lax.optimization_barrier((chain[0], arrays))
        return list(arrays)

    stage_query = [None] * len(stages)

    def ready(index):
        stage_query[index] = join([got[k] for k in stages[index]], 0)

    for index in range(len(stages) - 1):
        gather(index)
        ready(index)
    attend(0, [0, 1])
    source = stages[last][0] ^ (stages[last][0] & -stages[last][0])
    (got[source],) = hold(got[source])
    gather(last)
    ready(last)
    for index in range(last - 1, 0, -1):
        attend(index, [0, 1])
    far_pair = hold(*far_pair)
    pairs += [far_pair, [swap(array, 1) for array in far_pair]]
    attend(last, [0, 1])
    own_plan = [(at, "float", 0, at * tile, tile) for at in tiles]
    parts = []

    def send(index, packed):
        for at, k in enumerate(stages[index]):
            if k:
                piece = packed if per_stage == 1 else packed[:, at * rows : (at + 1) * rows]
                parts.append(swap(piece, inner * k))

    for index in range(last, 0, -1):
        send(index, attend(index, [2, 3], whole_plan, [packed_shape(stage_rows)])[0])
    if per_stage == 1:
        own = attend(0, [2, 3], own_plan, float_shapes(rows))
    else:
        own_plan = [(0, "float", 1, 0, rows)]
        packed, *own = attend(
            0, [2, 3], whole_plan + own_plan, [packed_shape(stage_rows)] + float_shapes(rows)
        )
        send(0, packed)
    groups = [(slice(0, rows), [(at, 0) for at in range(len(parts))])]
    merged = pl.pallas_call(
        functools.partial(merge_kernel, groups),
        in_specs=[vmem] * (2 + len(parts)),
        out_specs=vmem,
        out_shape=jax.ShapeDtypeStruct((rows, head_width), jnp.bfloat16),
        compiler_params=params,
        name="merge",
    )(*own, *parts)
    return merged.reshape(own_tokens, head_count, head_width)


def solution(mesh):
    in_specs = (P("ctx", "kvh", None), P("ctx", "kvh"), P("ctx", "kvh"), P(), P())
    out_specs = P("ctx", "kvh", None)
    size = mesh.shape["ctx"]

    def body(*args):
        return local(size, *args)

    return jax.shard_map(body, mesh=mesh, in_specs=in_specs, out_specs=out_specs, check_vma=False)
```

```python
import functools

import jax
import jax.numpy as jnp
from jax import lax
from jax.experimental import pallas as pl
from jax.experimental.pallas import tpu as pltpu
from jax.sharding import PartitionSpec as P


masked_floor = -1e30
log2_e = 1.4426950408889634
inner = 4
extra_rows = 16
tail_rows = 8
code_span = 240.0
code_low = -120.0


def attend_tiles(scale, query, keys, values, limits, states, scores_ref, weights_ref, values_ref):
    rows, width = query.shape
    shard_keys = keys[0].shape[0]
    tile = scores_ref.shape[2]
    chunk = min(512, shard_keys)
    chunks = shard_keys // chunk
    scaled = query.astype(jnp.float32) * scale
    high = scaled.astype(jnp.bfloat16)
    low = (scaled - high.astype(jnp.float32)).astype(jnp.bfloat16)
    query_pair = jnp.concatenate([high, low], axis=1)
    for b, value in enumerate(values):
        values_ref[b, :width, :] = value[...].T
        values_ref[b, width:, :] = jnp.ones((extra_rows, shard_keys), jnp.bfloat16)
    sublane = lax.broadcasted_iota(jnp.int32, (8, tile), 0)
    tiles = [(b, h) for b in range(len(keys)) for h in range(rows // tile)]
    count = len(tiles)
    running, tops = [None] * count, [None] * count
    states = list(states)
    for step in range(count + 2):
        for c in range(chunks):
            span = slice(c * chunk, (c + 1) * chunk)
            if step < count:
                b, h = tiles[step]
                lanes = slice(h * tile, (h + 1) * tile)
                key = keys[b][span, :]
                scores = lax.dot_general(
                    jnp.concatenate([key, key], axis=1),
                    query_pair[lanes],
                    (((1,), (1,)), ((), ())),
                    preferred_element_type=jnp.float32,
                ).reshape(chunk // 8, 8, tile)
                position = lax.broadcasted_iota(jnp.int32, scores.shape, 0) * 8 + c * chunk
                scores = jnp.where(position <= (limits[b][:, lanes] - sublane)[None], scores, masked_floor)
                peak = jnp.max(scores, axis=0)
                running[step] = peak if c == 0 else jnp.maximum(running[step], peak)
                scores_ref[step % 2, span, :] = scores.reshape(chunk, tile)
            if 1 <= step <= count:
                t = step - 1
                if c == 0:
                    tops[t] = jnp.max(running[t], axis=0, keepdims=True)
                weights_ref[t % 2, span, :] = jnp.exp2(scores_ref[t % 2, span, :] - tops[t]).astype(jnp.bfloat16)
            if step >= 2 and c == min(1, chunks - 1):
                b, h = tiles[step - 2]
                shard_max = tops[step - 2]
                sums = lax.dot_general(
                    values_ref[b],
                    weights_ref[step % 2],
                    (((1,), (0,)), ((), ())),
                    preferred_element_type=jnp.float32,
                )
                num, den = sums[:width], sums[width : width + 1]
                if states[h] is None:
                    states[h] = (shard_max, den, num)
                else:
                    top, run_den, run_num = states[h]
                    new_top = jnp.maximum(top, shard_max)
                    keep, fresh = jnp.exp2(top - new_top), jnp.exp2(shard_max - new_top)
                    states[h] = (new_top, run_den * keep + den * fresh, run_num * keep + num * fresh)
    return states


def encode(values, level):
    _, lanes = values.shape
    size = jnp.abs(values)
    peak = jnp.maximum(jnp.max(size, axis=0, keepdims=True), 1e-30).astype(jnp.bfloat16).astype(jnp.float32)
    code = jnp.exp2(size * (code_span / peak) + code_low)
    code = jnp.where(values < 0, -code, code)
    high = level.astype(jnp.bfloat16).astype(jnp.float32)
    rest = level - high
    middle = rest.astype(jnp.bfloat16).astype(jnp.float32)
    row = lax.broadcasted_iota(jnp.int32, (tail_rows, lanes), 0)
    tail = jnp.where(row == 0, high, jnp.where(row == 1, middle, jnp.where(row == 2, rest - middle, peak)))
    return code.astype(jnp.bfloat16), tail.astype(jnp.bfloat16)


def decode(codes, tail):
    codes, tail = codes.astype(jnp.float32), tail.astype(jnp.float32)
    level = tail[0:1] + tail[1:2] + tail[2:3]
    size = (jnp.log2(jnp.abs(codes)) - code_low) * (tail[3:4] * (1.0 / code_span))
    return jnp.where(codes < 0, -size, size), level


def spread_limits(me, own_tokens, head_count, offsets_ref, span_ref, limits_ref):
    count, lanes = limits_ref.shape
    width = offsets_ref.shape[1]
    per_row = width // own_tokens
    parts = []
    for k in range(count):
        device = me ^ (k * inner)
        row = offsets_ref[pl.ds(device // per_row, 1), :]
        row = pltpu.roll(row, (width - (device % per_row) * own_tokens) % width, 1)
        parts += [row >> 8, row & 255]
    parts = jnp.concatenate(parts, axis=0).astype(jnp.float32).astype(jnp.bfloat16)
    token = lax.broadcasted_iota(jnp.int32, (width, lanes), 0)
    lane = lax.broadcasted_iota(jnp.int32, (width, lanes), 1)
    first = token * head_count
    spread = jnp.where((lane >= first) & (lane < first + head_count), 1.0, 0.0).astype(jnp.bfloat16)
    wide = lax.dot_general(parts, spread, (((1,), (0,)), ((), ())), preferred_element_type=jnp.float32)
    wide = wide.astype(jnp.int32)
    for k in range(count):
        limits_ref[k : k + 1, :] = wide[2 * k : 2 * k + 1] * 256 + wide[2 * k + 1 : 2 * k + 2] + span_ref[...]


def attend_kernel(scale, index, blocks, has_state, plan, setup, *refs):
    me = lax.axis_index("ctx")
    refs = list(refs)
    if setup:
        offsets_ref, span_ref, q_hbm, k_hbm, v_hbm = refs[:5]
        arrived, q_ref = refs.pop(), refs.pop()
        scratch = [refs.pop() for _ in range(3)][::-1]
        v_ref, k_ref, limits_ref = refs.pop(), refs.pop(), refs.pop()
        pairs = ((q_hbm, q_ref), (k_hbm, k_ref), (v_hbm, v_ref))
        copies = [pltpu.make_async_copy(*pair, arrived.at[at]) for at, pair in enumerate(pairs)]
        for copy in copies:
            copy.start()
        spread_limits(me, *setup, offsets_ref, span_ref, limits_ref)
        for copy in copies:
            copy.wait()
        refs = [limits_ref, q_ref, k_ref, v_ref] + refs[5:]
    else:
        scratch = [refs.pop() for _ in range(3)][::-1]
        limits_ref, q_ref = refs[:2]
    keys = refs[2 : 2 + 2 * len(blocks) : 2]
    values = refs[3 : 3 + 2 * len(blocks) : 2]
    rest = list(refs[2 + 2 * len(blocks) :])
    rows, _ = q_ref.shape
    tile = scratch[0].shape[2]
    spans = [slice(at, at + tile) for at in range(0, rows, tile)]
    states = [None] * len(spans)
    if has_state:
        states = [tuple(ref[:, span] for ref in rest[:3]) for span in spans]
        rest = rest[3:]
    limits = [limits_ref[index : index + 1, :] - (me ^ b) * keys[0].shape[0] for b in blocks]
    states = attend_tiles(scale, q_ref[...], keys, values, limits, states, *scratch)
    if plan is None:
        for span, state in zip(spans, states):
            for ref, value in zip(rest, state):
                ref[:, span] = value
        return
    for at, form, out, offset, count in plan:
        top, den, num = (value[:, :count] for value in states[at])
        write_partial(rest[out:], form, slice(offset, offset + count), num * (1.0 / den), top + jnp.log2(den))


def write_partial(refs, form, span, value, level):
    width = value.shape[0]
    if form == "float":
        refs[0][:, span] = value
        refs[1][:, span] = level
    else:
        code, tail = encode(value, level)
        refs[0][:width, span] = code
        refs[0][width:, span] = tail


def combine(values, levels):
    top = functools.reduce(jnp.maximum, levels)
    factors = [jnp.exp2(level - top) for level in levels]
    total = functools.reduce(jnp.add, factors)
    inverse = 1.0 / total
    value = functools.reduce(jnp.add, [value * (factor * inverse) for value, factor in zip(values, factors)])
    return value, top + jnp.log2(total)


def merge_kernel(groups, *refs):
    own_ref, own_level_ref = refs[:2]
    parts, out_ref = refs[2:-1], refs[-1]
    width = own_ref.shape[0]
    for span, members in groups:
        values, levels = [own_ref[:, span]], [own_level_ref[:, span]]
        for at, offset in members:
            lanes = slice(offset, offset + span.stop - span.start)
            value, level = decode(parts[at][:width, lanes], parts[at][width:, lanes])
            values.append(value)
            levels.append(level)
        out_ref[span, :] = combine(values, levels)[0].T.astype(out_ref.dtype)


def local(size, queries, cache_keys, cache_values, span_offset, positions):
    own_tokens, head_count, head_width = queries.shape
    shard_keys = cache_keys.shape[0]
    outer = size // inner
    rows = own_tokens * head_count
    me = lax.axis_index("ctx")
    place, owner = me % inner, me // inner
    scale = head_width ** (-0.5) * log2_e

    def swap(array, step):
        return lax.ppermute(array, "ctx", [(i, i ^ step) for i in range(size)])

    query = queries.reshape(rows, head_width)
    per_stage = max(outer // 4, 1)
    stages = [list(range(s, s + per_stage)) for s in range(0, outer, per_stage)]
    last = len(stages) - 1

    far_pair = [swap(cache_keys, 2), swap(cache_values, 2)]
    near_pair = [swap(cache_keys, 1), swap(cache_values, 1)]
    got = [query] + [None] * (outer - 1)

    def gather(index):
        for k in stages[index]:
            if k:
                low = k & -k
                got[k] = swap(got[k ^ low], inner * low)

    stage_rows = rows * per_stage
    tile = 256 if stage_rows % 256 == 0 else stage_rows

    fused_setup = per_stage == 1 and positions.shape[0] % 128 == 0 and 128 % own_tokens == 0
    if fused_setup:
        chain = [None]
    else:
        limits = (span_offset[0] + positions).reshape(outer, inner, own_tokens)
        limits = lax.dynamic_index_in_dim(limits, place, 1, keepdims=False)
        limits = [lax.dynamic_slice_in_dim(limits, owner ^ k, 1, axis=0) for k in range(outer)]
        limits = jnp.repeat(jnp.concatenate(limits, axis=0), head_count, axis=1)
        chain = [limits.reshape(len(stages), stage_rows)]

    def join(items, axis):
        return items[0] if len(items) == 1 else jnp.concatenate(items, axis=axis)

    vmem = pl.BlockSpec(memory_space=pltpu.VMEM)
    params = pltpu.CompilerParams(vmem_limit_bytes=20 << 20)
    pairs = [[cache_keys, cache_values], near_pair]
    stat = jax.ShapeDtypeStruct((1, stage_rows), jnp.float32)
    state_shapes = [stat, stat, jax.ShapeDtypeStruct((head_width, stage_rows), jnp.float32)]

    def packed_shape(lanes):
        return jax.ShapeDtypeStruct((head_width + tail_rows, lanes), jnp.bfloat16)

    def float_shapes(lanes):
        return [jax.ShapeDtypeStruct((size_of, lanes), jnp.float32) for size_of in (head_width, 1)]

    tiles = range(stage_rows // tile)
    whole_plan = [(at, "code", 0, at * tile, tile) for at in tiles]
    states = [None] * len(stages)

    def attend(index, blocks, plan=None, shapes=state_shapes):
        setup = None
        if chain[0] is None:
            setup = (own_tokens, head_count)
            shapes = shapes + [jax.ShapeDtypeStruct((len(stages), stage_rows), jnp.int32)]
            shapes += [jax.ShapeDtypeStruct(array.shape, array.dtype) for array in pairs[0]]
            own = [pltpu.with_memory_space_constraint(array, pltpu.HBM) for array in (query, *pairs[0])]
            operands = [positions.reshape(-1, 128), span_offset.reshape(1, 1)] + own
            specs = [vmem] * 2 + [pl.BlockSpec(memory_space=pltpu.HBM)] * 3
            extra = [pltpu.VMEM(query.shape, query.dtype), pltpu.SemaphoreType.DMA((3,))]
            operands += [array for b in blocks[1:] for array in pairs[b]]
        else:
            operands = [chain[0], stage_query[index]] + [array for b in blocks for array in pairs[b]]
            operands += list(states[index] or ())
            specs, extra = [], []
        results = pl.pallas_call(
            functools.partial(
                attend_kernel, scale, index, blocks, states[index] is not None, plan, setup
            ),
            in_specs=specs + [vmem] * (len(operands) - len(specs)),
            out_specs=[vmem] * len(shapes),
            out_shape=shapes,
            scratch_shapes=[
                pltpu.VMEM((2, shard_keys, tile), jnp.float32),
                pltpu.VMEM((2, shard_keys, tile), jnp.bfloat16),
                pltpu.VMEM((len(blocks), head_width + extra_rows, shard_keys), jnp.bfloat16),
            ]
            + extra,
            compiler_params=params,
        )(*operands)
        if setup:
            chain[0], pairs[0], results = results[-3], list(results[-2:]), results[:-3]
        chain[0], results = lax.optimization_barrier((chain[0], results))
        if plan is None:
            states[index] = results
        return results

    def hold(*arrays):
        chain[0], arrays = lax.optimization_barrier((chain[0], arrays))
        return list(arrays)

    stage_query = [None] * len(stages)

    def ready(index):
        stage_query[index] = join([got[k] for k in stages[index]], 0)

    for index in range(len(stages) - 1):
        gather(index)
        ready(index)
    attend(0, [0, 1])
    for index in range(1, last - 1):
        attend(index, [0, 1])
    source = stages[last][0] ^ (stages[last][0] & -stages[last][0])
    (got[source],) = hold(got[source])
    gather(last)
    ready(last)
    far_pair[0], = hold(far_pair[0])
    across_keys = swap(far_pair[0], 1)
    attend(last - 1, [0, 1])
    far_pair[1], = hold(far_pair[1])
    across_values = swap(far_pair[1], 1)
    pairs += [far_pair, [across_keys, across_values]]
    own_plan = [(at, "float", 0, at * tile, tile) for at in tiles]
    parts = []

    def send(index, packed):
        for at, k in enumerate(stages[index]):
            if k:
                piece = packed if per_stage == 1 else packed[:, at * rows : (at + 1) * rows]
                parts.append(swap(piece, inner * k))

    coded = [packed_shape(stage_rows)]
    attend(last - 1, [2])
    send(last - 1, attend(last - 1, [3], whole_plan, coded)[0])
    send(last, attend(last, [0, 1, 2, 3], whole_plan, coded)[0])
    for index in range(last - 2, 0, -1):
        send(index, attend(index, [2, 3], whole_plan, coded)[0])
    if per_stage == 1:
        own = attend(0, [2, 3], own_plan, float_shapes(rows))
    else:
        own_plan = [(0, "float", 1, 0, rows)]
        packed, *own = attend(
            0, [2, 3], whole_plan + own_plan, [packed_shape(stage_rows)] + float_shapes(rows)
        )
        send(0, packed)
    groups = [(slice(0, rows), [(at, 0) for at in range(len(parts))])]
    merged = pl.pallas_call(
        functools.partial(merge_kernel, groups),
        in_specs=[vmem] * (2 + len(parts)),
        out_specs=vmem,
        out_shape=jax.ShapeDtypeStruct((rows, head_width), jnp.bfloat16),
        compiler_params=params,
        name="merge",
    )(*own, *parts)
    return merged.reshape(own_tokens, head_count, head_width)


def solution(mesh):
    in_specs = (P("ctx", "kvh", None), P("ctx", "kvh"), P("ctx", "kvh"), P(), P())
    out_specs = P("ctx", "kvh", None)
    size = mesh.shape["ctx"]

    def body(*args):
        return local(size, *args)

    return jax.shard_map(body, mesh=mesh, in_specs=in_specs, out_specs=out_specs, check_vma=False)
```

```python
import functools

import jax
import jax.numpy as jnp
from jax import lax
from jax.experimental import pallas as pl
from jax.experimental.pallas import tpu as pltpu
from jax.sharding import PartitionSpec as P


masked_floor = -1e30
log2_e = 1.4426950408889634
inner = 4
extra_rows = 16
tail_rows = 8
code_span = 240.0
code_low = -120.0


def attend_tiles(scale, query, keys, values, limits, states, scores_ref, weights_ref, values_ref):
    rows, width = query.shape
    shard_keys = keys[0].shape[0]
    tile = scores_ref.shape[2]
    chunk = min(512, shard_keys)
    chunks = shard_keys // chunk
    scaled = query.astype(jnp.float32) * scale
    high = scaled.astype(jnp.bfloat16)
    low = (scaled - high.astype(jnp.float32)).astype(jnp.bfloat16)
    query_pair = jnp.concatenate([high, low], axis=1)
    for b, value in enumerate(values):
        values_ref[b, :width, :] = value[...].T
        values_ref[b, width:, :] = jnp.ones((extra_rows, shard_keys), jnp.bfloat16)
    sublane = lax.broadcasted_iota(jnp.int32, (8, tile), 0)
    tiles = [(b, h) for b in range(len(keys)) for h in range(rows // tile)]
    count = len(tiles)
    running, tops = [None] * count, [None] * count
    states = list(states)
    for step in range(count + 2):
        for c in range(chunks):
            span = slice(c * chunk, (c + 1) * chunk)
            if step < count:
                b, h = tiles[step]
                lanes = slice(h * tile, (h + 1) * tile)
                key = keys[b][span, :]
                scores = lax.dot_general(
                    jnp.concatenate([key, key], axis=1),
                    query_pair[lanes],
                    (((1,), (1,)), ((), ())),
                    preferred_element_type=jnp.float32,
                ).reshape(chunk // 8, 8, tile)
                position = lax.broadcasted_iota(jnp.int32, scores.shape, 0) * 8 + c * chunk
                scores = jnp.where(position <= (limits[b][:, lanes] - sublane)[None], scores, masked_floor)
                peak = jnp.max(scores, axis=0)
                running[step] = peak if c == 0 else jnp.maximum(running[step], peak)
                scores_ref[step % 2, span, :] = scores.reshape(chunk, tile)
            if 1 <= step <= count:
                t = step - 1
                if c == 0:
                    tops[t] = jnp.max(running[t], axis=0, keepdims=True)
                weights_ref[t % 2, span, :] = jnp.exp2(scores_ref[t % 2, span, :] - tops[t]).astype(jnp.bfloat16)
            if step >= 2 and c == min(1, chunks - 1):
                b, h = tiles[step - 2]
                shard_max = tops[step - 2]
                sums = lax.dot_general(
                    values_ref[b],
                    weights_ref[step % 2],
                    (((1,), (0,)), ((), ())),
                    preferred_element_type=jnp.float32,
                )
                num, den = sums[:width], sums[width : width + 1]
                if states[h] is None:
                    states[h] = (shard_max, den, num)
                else:
                    top, run_den, run_num = states[h]
                    new_top = jnp.maximum(top, shard_max)
                    keep, fresh = jnp.exp2(top - new_top), jnp.exp2(shard_max - new_top)
                    states[h] = (new_top, run_den * keep + den * fresh, run_num * keep + num * fresh)
    return states


def encode(values, level):
    _, lanes = values.shape
    size = jnp.abs(values)
    peak = jnp.maximum(jnp.max(size, axis=0, keepdims=True), 1e-30).astype(jnp.bfloat16).astype(jnp.float32)
    code = jnp.exp2(size * (code_span / peak) + code_low)
    code = jnp.where(values < 0, -code, code)
    high = level.astype(jnp.bfloat16).astype(jnp.float32)
    rest = level - high
    middle = rest.astype(jnp.bfloat16).astype(jnp.float32)
    row = lax.broadcasted_iota(jnp.int32, (tail_rows, lanes), 0)
    tail = jnp.where(row == 0, high, jnp.where(row == 1, middle, jnp.where(row == 2, rest - middle, peak)))
    return code.astype(jnp.bfloat16), tail.astype(jnp.bfloat16)


def decode(codes, tail):
    codes, tail = codes.astype(jnp.float32), tail.astype(jnp.float32)
    level = tail[0:1] + tail[1:2] + tail[2:3]
    size = (jnp.log2(jnp.abs(codes)) - code_low) * (tail[3:4] * (1.0 / code_span))
    return jnp.where(codes < 0, -size, size), level


def spread_limits(me, own_tokens, head_count, offsets_ref, span_ref, limits_ref):
    count, lanes = limits_ref.shape
    width = offsets_ref.shape[1]
    per_row = width // own_tokens
    parts = []
    for k in range(count):
        device = me ^ (k * inner)
        row = offsets_ref[pl.ds(device // per_row, 1), :]
        row = pltpu.roll(row, (width - (device % per_row) * own_tokens) % width, 1)
        parts += [row >> 8, row & 255]
    parts = jnp.concatenate(parts, axis=0).astype(jnp.float32).astype(jnp.bfloat16)
    token = lax.broadcasted_iota(jnp.int32, (width, lanes), 0)
    lane = lax.broadcasted_iota(jnp.int32, (width, lanes), 1)
    first = token * head_count
    spread = jnp.where((lane >= first) & (lane < first + head_count), 1.0, 0.0).astype(jnp.bfloat16)
    wide = lax.dot_general(parts, spread, (((1,), (0,)), ((), ())), preferred_element_type=jnp.float32)
    wide = wide.astype(jnp.int32)
    for k in range(count):
        limits_ref[k : k + 1, :] = wide[2 * k : 2 * k + 1] * 256 + wide[2 * k + 1 : 2 * k + 2] + span_ref[...]


def attend_kernel(scale, index, blocks, has_state, plan, setup, *refs):
    me = lax.axis_index("ctx")
    refs = list(refs)
    if setup:
        offsets_ref, span_ref, q_hbm, k_hbm, v_hbm = refs[:5]
        arrived, q_ref = refs.pop(), refs.pop()
        scratch = [refs.pop() for _ in range(3)][::-1]
        v_ref, k_ref, limits_ref = refs.pop(), refs.pop(), refs.pop()
        pairs = ((q_hbm, q_ref), (k_hbm, k_ref), (v_hbm, v_ref))
        copies = [pltpu.make_async_copy(*pair, arrived.at[at]) for at, pair in enumerate(pairs)]
        for copy in copies:
            copy.start()
        spread_limits(me, *setup, offsets_ref, span_ref, limits_ref)
        for copy in copies:
            copy.wait()
        refs = [limits_ref, q_ref, k_ref, v_ref] + refs[5:]
    else:
        scratch = [refs.pop() for _ in range(3)][::-1]
        limits_ref, q_ref = refs[:2]
    keys = refs[2 : 2 + 2 * len(blocks) : 2]
    values = refs[3 : 3 + 2 * len(blocks) : 2]
    rest = list(refs[2 + 2 * len(blocks) :])
    rows, _ = q_ref.shape
    tile = scratch[0].shape[2]
    spans = [slice(at, at + tile) for at in range(0, rows, tile)]
    states = [None] * len(spans)
    if has_state:
        states = [tuple(ref[:, span] for ref in rest[:3]) for span in spans]
        rest = rest[3:]
    limits = [limits_ref[index : index + 1, :] - (me ^ b) * keys[0].shape[0] for b in blocks]
    states = attend_tiles(scale, q_ref[...], keys, values, limits, states, *scratch)
    if plan is None:
        for span, state in zip(spans, states):
            for ref, value in zip(rest, state):
                ref[:, span] = value
        return
    for at, form, out, offset, count in plan:
        top, den, num = (value[:, :count] for value in states[at])
        write_partial(rest[out:], form, slice(offset, offset + count), num * (1.0 / den), top + jnp.log2(den))


def write_partial(refs, form, span, value, level):
    width = value.shape[0]
    if form == "float":
        refs[0][:, span] = value
        refs[1][:, span] = level
    else:
        code, tail = encode(value, level)
        refs[0][:width, span] = code
        refs[0][width:, span] = tail


def combine(values, levels):
    top = functools.reduce(jnp.maximum, levels)
    factors = [jnp.exp2(level - top) for level in levels]
    total = functools.reduce(jnp.add, factors)
    inverse = 1.0 / total
    value = functools.reduce(jnp.add, [value * (factor * inverse) for value, factor in zip(values, factors)])
    return value, top + jnp.log2(total)


def combine_kernel(value_ref, level_ref, part_ref, out_ref):
    width, lanes = value_ref.shape
    value, level = decode(part_ref[:width, :], part_ref[width:, :])
    value, level = combine([value_ref[...], value], [level_ref[...], level])
    write_partial([out_ref], "code", slice(0, lanes), value, level)


def merge_kernel(groups, *refs):
    own_ref, own_level_ref = refs[:2]
    parts, out_ref = refs[2:-1], refs[-1]
    width = own_ref.shape[0]
    for span, members in groups:
        values, levels = [own_ref[:, span]], [own_level_ref[:, span]]
        for at, offset in members:
            lanes = slice(offset, offset + span.stop - span.start)
            value, level = decode(parts[at][:width, lanes], parts[at][width:, lanes])
            values.append(value)
            levels.append(level)
        out_ref[span, :] = combine(values, levels)[0].T.astype(out_ref.dtype)


def local(size, queries, cache_keys, cache_values, span_offset, positions):
    own_tokens, head_count, head_width = queries.shape
    shard_keys = cache_keys.shape[0]
    outer = size // inner
    rows = own_tokens * head_count
    me = lax.axis_index("ctx")
    place, owner = me % inner, me // inner
    scale = head_width ** (-0.5) * log2_e

    def swap(array, step):
        return lax.ppermute(array, "ctx", [(i, i ^ step) for i in range(size)])

    query = queries.reshape(rows, head_width)
    per_stage = max(outer // 4, 1)
    stages = [list(range(s, s + per_stage)) for s in range(0, outer, per_stage)]
    last = len(stages) - 1

    far_pair = [swap(cache_keys, 2), swap(cache_values, 2)]
    near_pair = [swap(cache_keys, 1), swap(cache_values, 1)]
    got = [query] + [None] * (outer - 1)

    def gather(index):
        for k in stages[index]:
            if k:
                low = k & -k
                got[k] = swap(got[k ^ low], inner * low)

    stage_rows = rows * per_stage
    tile = 256 if stage_rows % 256 == 0 else stage_rows

    fused_setup = per_stage == 1 and positions.shape[0] % 128 == 0 and 128 % own_tokens == 0
    if fused_setup:
        chain = [None]
    else:
        limits = (span_offset[0] + positions).reshape(outer, inner, own_tokens)
        limits = lax.dynamic_index_in_dim(limits, place, 1, keepdims=False)
        limits = [lax.dynamic_slice_in_dim(limits, owner ^ k, 1, axis=0) for k in range(outer)]
        limits = jnp.repeat(jnp.concatenate(limits, axis=0), head_count, axis=1)
        chain = [limits.reshape(len(stages), stage_rows)]

    def join(items, axis):
        return items[0] if len(items) == 1 else jnp.concatenate(items, axis=axis)

    vmem = pl.BlockSpec(memory_space=pltpu.VMEM)
    params = pltpu.CompilerParams(vmem_limit_bytes=20 << 20)
    pairs = [[cache_keys, cache_values], near_pair]
    stat = jax.ShapeDtypeStruct((1, stage_rows), jnp.float32)
    state_shapes = [stat, stat, jax.ShapeDtypeStruct((head_width, stage_rows), jnp.float32)]

    def packed_shape(lanes):
        return jax.ShapeDtypeStruct((head_width + tail_rows, lanes), jnp.bfloat16)

    def float_shapes(lanes):
        return [jax.ShapeDtypeStruct((size_of, lanes), jnp.float32) for size_of in (head_width, 1)]

    tiles = range(stage_rows // tile)
    whole_plan = [(at, "code", 0, at * tile, tile) for at in tiles]
    states = [None] * len(stages)

    def attend(index, blocks, plan=None, shapes=state_shapes):
        setup = None
        if chain[0] is None:
            setup = (own_tokens, head_count)
            shapes = shapes + [jax.ShapeDtypeStruct((len(stages), stage_rows), jnp.int32)]
            shapes += [jax.ShapeDtypeStruct(array.shape, array.dtype) for array in pairs[0]]
            own = [pltpu.with_memory_space_constraint(array, pltpu.HBM) for array in (query, *pairs[0])]
            operands = [positions.reshape(-1, 128), span_offset.reshape(1, 1)] + own
            specs = [vmem] * 2 + [pl.BlockSpec(memory_space=pltpu.HBM)] * 3
            extra = [pltpu.VMEM(query.shape, query.dtype), pltpu.SemaphoreType.DMA((3,))]
            operands += [array for b in blocks[1:] for array in pairs[b]]
        else:
            operands = [chain[0], stage_query[index]] + [array for b in blocks for array in pairs[b]]
            operands += list(states[index] or ())
            specs, extra = [], []
        results = pl.pallas_call(
            functools.partial(
                attend_kernel, scale, index, blocks, states[index] is not None, plan, setup
            ),
            in_specs=specs + [vmem] * (len(operands) - len(specs)),
            out_specs=[vmem] * len(shapes),
            out_shape=shapes,
            scratch_shapes=[
                pltpu.VMEM((2, shard_keys, tile), jnp.float32),
                pltpu.VMEM((2, shard_keys, tile), jnp.bfloat16),
                pltpu.VMEM((len(blocks), head_width + extra_rows, shard_keys), jnp.bfloat16),
            ]
            + extra,
            compiler_params=params,
        )(*operands)
        if setup:
            chain[0], pairs[0], results = results[-3], list(results[-2:]), results[:-3]
        chain[0], results = lax.optimization_barrier((chain[0], results))
        if plan is None:
            states[index] = results
        return results

    def hold(*arrays):
        chain[0], arrays = lax.optimization_barrier((chain[0], arrays))
        return list(arrays)

    stage_query = [None] * len(stages)

    def ready(index):
        stage_query[index] = join([got[k] for k in stages[index]], 0)

    for index in range(len(stages) - 1):
        gather(index)
        ready(index)
    attend(0, [0, 1])
    for index in range(1, last - 1):
        attend(index, [0, 1])
    source = stages[last][0] ^ (stages[last][0] & -stages[last][0])
    (got[source],) = hold(got[source])
    gather(last)
    ready(last)
    far_pair[0], = hold(far_pair[0])
    across_keys = swap(far_pair[0], 1)
    attend(last - 1, [0, 1])
    far_pair[1], = hold(far_pair[1])
    across_values = swap(far_pair[1], 1)
    pairs += [far_pair, [across_keys, across_values]]
    own_plan = [(at, "float", 0, at * tile, tile) for at in tiles]
    parts = []

    def send(index, packed):
        for at, k in enumerate(stages[index]):
            if k:
                piece = packed if per_stage == 1 else packed[:, at * rows : (at + 1) * rows]
                parts.append(swap(piece, inner * k))

    coded = [packed_shape(stage_rows)]
    attend(last - 1, [2])
    if outer == 4:
        (packed,) = attend(2, [3], whole_plan, coded)
        handed = swap(packed, inner)
        (packed,) = attend(1, [2, 3], whole_plan, coded)
        parts.append(swap(packed, inner))
        value, level = attend(3, [0, 1, 2, 3], own_plan, float_shapes(stage_rows))
        (handed,) = hold(handed)
        joined = pl.pallas_call(
            combine_kernel,
            in_specs=[vmem] * 3,
            out_specs=vmem,
            out_shape=coded[0],
            compiler_params=params,
            name="combine",
        )(value, level, handed)
        (joined,) = hold(joined)
        parts.append(swap(joined, 3 * inner))
    else:
        send(last - 1, attend(last - 1, [3], whole_plan, coded)[0])
        send(last, attend(last, [0, 1, 2, 3], whole_plan, coded)[0])
        for index in range(last - 2, 0, -1):
            send(index, attend(index, [2, 3], whole_plan, coded)[0])
    if per_stage == 1:
        own = attend(0, [2, 3], own_plan, float_shapes(rows))
    else:
        own_plan = [(0, "float", 1, 0, rows)]
        packed, *own = attend(
            0, [2, 3], whole_plan + own_plan, [packed_shape(stage_rows)] + float_shapes(rows)
        )
        send(0, packed)
    groups = [(slice(0, rows), [(at, 0) for at in range(len(parts))])]
    merged = pl.pallas_call(
        functools.partial(merge_kernel, groups),
        in_specs=[vmem] * (2 + len(parts)),
        out_specs=vmem,
        out_shape=jax.ShapeDtypeStruct((rows, head_width), jnp.bfloat16),
        compiler_params=params,
        name="merge",
    )(*own, *parts)
    return merged.reshape(own_tokens, head_count, head_width)


def solution(mesh):
    in_specs = (P("ctx", "kvh", None), P("ctx", "kvh"), P("ctx", "kvh"), P(), P())
    out_specs = P("ctx", "kvh", None)
    size = mesh.shape["ctx"]

    def body(*args):
        return local(size, *args)

    return jax.shard_map(body, mesh=mesh, in_specs=in_specs, out_specs=out_specs, check_vma=False)
```

```python
import functools

import jax
import jax.numpy as jnp
from jax import lax
from jax.experimental import pallas as pl
from jax.experimental.pallas import tpu as pltpu
from jax.sharding import PartitionSpec as P


masked_floor = -1e30
log2_e = 1.4426950408889634
inner = 4
extra_rows = 16
tail_rows = 8
code_span = 240.0
code_low = -120.0


def split_query(query, scale):
    scaled = query.astype(jnp.float32) * scale
    high = scaled.astype(jnp.bfloat16)
    low = (scaled - high.astype(jnp.float32)).astype(jnp.bfloat16)
    return jnp.concatenate([high, low], axis=1)


def transpose_values(values, values_ref):
    for b, value in enumerate(values):
        shard_keys, width = value.shape
        values_ref[b, :width, :] = value[...].T
        values_ref[b, width:, :] = jnp.ones((extra_rows, shard_keys), jnp.bfloat16)


def score_chunk(key, query_pair, limit, start, scores_ref, slot):
    chunk, tile = key.shape[0], query_pair.shape[0]
    scores = lax.dot_general(
        jnp.concatenate([key, key], axis=1), query_pair, (((1,), (1,)), ((), ())), preferred_element_type=jnp.float32
    ).reshape(chunk // 8, 8, tile)
    position = lax.broadcasted_iota(jnp.int32, scores.shape, 0) * 8 + start
    sublane = lax.broadcasted_iota(jnp.int32, (8, tile), 0)
    scores = jnp.where(position <= (limit - sublane)[None], scores, masked_floor)
    scores_ref[slot, start : start + chunk, :] = scores.reshape(chunk, tile)
    return jnp.max(scores, axis=0)


def add_block(state, values_t, weights, shard_max):
    width = values_t.shape[0] - extra_rows
    sums = lax.dot_general(values_t, weights, (((1,), (0,)), ((), ())), preferred_element_type=jnp.float32)
    num, den = sums[:width], sums[width : width + 1]
    if state is None:
        return shard_max, den, num
    top, run_den, run_num = state
    new_top = jnp.maximum(top, shard_max)
    keep, fresh = jnp.exp2(top - new_top), jnp.exp2(shard_max - new_top)
    return new_top, run_den * keep + den * fresh, run_num * keep + num * fresh


def sweep_tiles(rows, tile, query_pair, keys, limits, scores_ref, put_weights, finish):
    shard_keys = keys[0].shape[0]
    chunk = min(512, shard_keys)
    chunks = shard_keys // chunk
    tiles = [(b, h) for b in range(len(keys)) for h in range(rows // tile)]
    count = len(tiles)
    running, tops = [None] * count, [None] * count
    for step in range(count + 2):
        for c in range(chunks):
            span = slice(c * chunk, (c + 1) * chunk)
            if step < count:
                b, h = tiles[step]
                lanes = slice(h * tile, (h + 1) * tile)
                peak = score_chunk(
                    keys[b][span, :], query_pair[lanes], limits[b][:, lanes], c * chunk, scores_ref, step % 2
                )
                running[step] = peak if c == 0 else jnp.maximum(running[step], peak)
            if 1 <= step <= count:
                t = step - 1
                if c == 0:
                    tops[t] = jnp.max(running[t], axis=0, keepdims=True)
                put_weights(t, *tiles[t], span, jnp.exp2(scores_ref[t % 2, span, :] - tops[t]).astype(jnp.bfloat16))
            if step >= 2 and c == min(1, chunks - 1):
                finish(step - 2, *tiles[step - 2], tops[step - 2])


def attend_tiles(scale, query, keys, values, limits, states, scores_ref, weights_ref, values_ref):
    states = list(states)
    query_pair = split_query(query, scale)
    transpose_values(values, values_ref)

    def put_weights(t, b, h, span, weights):
        weights_ref[t % 2, span, :] = weights

    def finish(t, b, h, shard_max):
        states[h] = add_block(states[h], values_ref[b], weights_ref[t % 2], shard_max)

    sweep_tiles(query.shape[0], scores_ref.shape[2], query_pair, keys, limits, scores_ref, put_weights, finish)
    return states


def weigh_kernel(scale, index, blocks, limits_ref, q_ref, *refs):
    me = lax.axis_index("ctx")
    count = len(blocks)
    keys, weights, tops, scores_ref = refs[:count], refs[count : 2 * count], refs[2 * count : 3 * count], refs[-1]
    tile = scores_ref.shape[2]
    limits = [limits_ref[index : index + 1, :] - (me ^ b) * keys[0].shape[0] for b in blocks]

    def put_weights(t, b, h, span, value):
        weights[b][span, h * tile : (h + 1) * tile] = value

    def finish(t, b, h, shard_max):
        tops[b][:, h * tile : (h + 1) * tile] = shard_max

    query_pair = split_query(q_ref[...], scale)
    sweep_tiles(q_ref.shape[0], tile, query_pair, keys, limits, scores_ref, put_weights, finish)


def finish_kernel(count, plan, *refs):
    values, weights, tops = refs[:count], refs[count : 2 * count], refs[2 * count : 3 * count]
    state_refs, outs, values_ref = refs[3 * count : 3 * count + 3], refs[3 * count + 3 : -1], refs[-1]
    transpose_values(values, values_ref)
    for at, form, out, offset, lanes in plan:
        span = slice(at * lanes, (at + 1) * lanes)
        state = tuple(ref[:, span] for ref in state_refs)
        for b in range(count):
            state = add_block(state, values_ref[b], weights[b][:, span], tops[b][:, span])
        top, den, num = state
        write_partial(outs[out:], form, slice(offset, offset + lanes), num * (1.0 / den), top + jnp.log2(den))


def encode(values, level):
    _, lanes = values.shape
    size = jnp.abs(values)
    peak = jnp.maximum(jnp.max(size, axis=0, keepdims=True), 1e-30).astype(jnp.bfloat16).astype(jnp.float32)
    code = jnp.exp2(size * (code_span / peak) + code_low)
    code = jnp.where(values < 0, -code, code)
    high = level.astype(jnp.bfloat16).astype(jnp.float32)
    rest = level - high
    middle = rest.astype(jnp.bfloat16).astype(jnp.float32)
    row = lax.broadcasted_iota(jnp.int32, (tail_rows, lanes), 0)
    tail = jnp.where(row == 0, high, jnp.where(row == 1, middle, jnp.where(row == 2, rest - middle, peak)))
    return code.astype(jnp.bfloat16), tail.astype(jnp.bfloat16)


def decode(codes, tail):
    codes, tail = codes.astype(jnp.float32), tail.astype(jnp.float32)
    level = tail[0:1] + tail[1:2] + tail[2:3]
    size = (jnp.log2(jnp.abs(codes)) - code_low) * (tail[3:4] * (1.0 / code_span))
    return jnp.where(codes < 0, -size, size), level


def spread_limits(me, own_tokens, head_count, offsets_ref, span_ref, limits_ref):
    count, lanes = limits_ref.shape
    width = offsets_ref.shape[1]
    per_row = width // own_tokens
    parts = []
    for k in range(count):
        device = me ^ (k * inner)
        row = offsets_ref[pl.ds(device // per_row, 1), :]
        row = pltpu.roll(row, (width - (device % per_row) * own_tokens) % width, 1)
        parts += [row >> 8, row & 255]
    parts = jnp.concatenate(parts, axis=0).astype(jnp.float32).astype(jnp.bfloat16)
    token = lax.broadcasted_iota(jnp.int32, (width, lanes), 0)
    lane = lax.broadcasted_iota(jnp.int32, (width, lanes), 1)
    first = token * head_count
    spread = jnp.where((lane >= first) & (lane < first + head_count), 1.0, 0.0).astype(jnp.bfloat16)
    wide = lax.dot_general(parts, spread, (((1,), (0,)), ((), ())), preferred_element_type=jnp.float32)
    wide = wide.astype(jnp.int32)
    for k in range(count):
        limits_ref[k : k + 1, :] = wide[2 * k : 2 * k + 1] * 256 + wide[2 * k + 1 : 2 * k + 2] + span_ref[...]


def attend_kernel(scale, index, blocks, has_state, plan, setup, *refs):
    me = lax.axis_index("ctx")
    refs = list(refs)
    if setup:
        offsets_ref, span_ref, q_hbm, k_hbm, v_hbm = refs[:5]
        arrived, q_ref = refs.pop(), refs.pop()
        scratch = [refs.pop() for _ in range(3)][::-1]
        v_ref, k_ref, limits_ref = refs.pop(), refs.pop(), refs.pop()
        pairs = ((q_hbm, q_ref), (k_hbm, k_ref), (v_hbm, v_ref))
        copies = [pltpu.make_async_copy(*pair, arrived.at[at]) for at, pair in enumerate(pairs)]
        for copy in copies:
            copy.start()
        spread_limits(me, *setup, offsets_ref, span_ref, limits_ref)
        for copy in copies:
            copy.wait()
        refs = [limits_ref, q_ref, k_ref, v_ref] + refs[5:]
    else:
        scratch = [refs.pop() for _ in range(3)][::-1]
        limits_ref, q_ref = refs[:2]
    keys = refs[2 : 2 + 2 * len(blocks) : 2]
    values = refs[3 : 3 + 2 * len(blocks) : 2]
    rest = list(refs[2 + 2 * len(blocks) :])
    rows, _ = q_ref.shape
    tile = scratch[0].shape[2]
    spans = [slice(at, at + tile) for at in range(0, rows, tile)]
    states = [None] * len(spans)
    if has_state:
        states = [tuple(ref[:, span] for ref in rest[:3]) for span in spans]
        rest = rest[3:]
    limits = [limits_ref[index : index + 1, :] - (me ^ b) * keys[0].shape[0] for b in blocks]
    states = attend_tiles(scale, q_ref[...], keys, values, limits, states, *scratch)
    if plan is None:
        for span, state in zip(spans, states):
            for ref, value in zip(rest, state):
                ref[:, span] = value
        return
    for at, form, out, offset, count in plan:
        top, den, num = (value[:, :count] for value in states[at])
        write_partial(rest[out:], form, slice(offset, offset + count), num * (1.0 / den), top + jnp.log2(den))


def write_partial(refs, form, span, value, level):
    width = value.shape[0]
    if form == "float":
        refs[0][:, span] = value
        refs[1][:, span] = level
    else:
        code, tail = encode(value, level)
        refs[0][:width, span] = code
        refs[0][width:, span] = tail


def combine(values, levels):
    top = functools.reduce(jnp.maximum, levels)
    factors = [jnp.exp2(level - top) for level in levels]
    total = functools.reduce(jnp.add, factors)
    inverse = 1.0 / total
    value = functools.reduce(jnp.add, [value * (factor * inverse) for value, factor in zip(values, factors)])
    return value, top + jnp.log2(total)


def combine_kernel(value_ref, level_ref, part_ref, out_ref):
    width, lanes = value_ref.shape
    value, level = decode(part_ref[:width, :], part_ref[width:, :])
    value, level = combine([value_ref[...], value], [level_ref[...], level])
    write_partial([out_ref], "code", slice(0, lanes), value, level)


def merge_kernel(groups, *refs):
    own_ref, own_level_ref = refs[:2]
    parts, out_ref = refs[2:-1], refs[-1]
    width = own_ref.shape[0]
    for span, members in groups:
        values, levels = [own_ref[:, span]], [own_level_ref[:, span]]
        for at, offset in members:
            lanes = slice(offset, offset + span.stop - span.start)
            value, level = decode(parts[at][:width, lanes], parts[at][width:, lanes])
            values.append(value)
            levels.append(level)
        out_ref[span, :] = combine(values, levels)[0].T.astype(out_ref.dtype)


def local(size, queries, cache_keys, cache_values, span_offset, positions):
    own_tokens, head_count, head_width = queries.shape
    shard_keys = cache_keys.shape[0]
    outer = size // inner
    rows = own_tokens * head_count
    me = lax.axis_index("ctx")
    place, owner = me % inner, me // inner
    scale = head_width ** (-0.5) * log2_e

    def swap(array, step):
        return lax.ppermute(array, "ctx", [(i, i ^ step) for i in range(size)])

    query = queries.reshape(rows, head_width)
    per_stage = max(outer // 4, 1)
    stages = [list(range(s, s + per_stage)) for s in range(0, outer, per_stage)]
    last = len(stages) - 1

    far_pair = [swap(cache_keys, 2), swap(cache_values, 2)]
    near_pair = [swap(cache_keys, 1), swap(cache_values, 1)]
    got = [query] + [None] * (outer - 1)

    def gather(index):
        for k in stages[index]:
            if k:
                low = k & -k
                got[k] = swap(got[k ^ low], inner * low)

    stage_rows = rows * per_stage
    tile = 256 if stage_rows % 256 == 0 else stage_rows

    fused_setup = per_stage == 1 and positions.shape[0] % 128 == 0 and 128 % own_tokens == 0
    if fused_setup:
        chain = [None]
    else:
        limits = (span_offset[0] + positions).reshape(outer, inner, own_tokens)
        limits = lax.dynamic_index_in_dim(limits, place, 1, keepdims=False)
        limits = [lax.dynamic_slice_in_dim(limits, owner ^ k, 1, axis=0) for k in range(outer)]
        limits = jnp.repeat(jnp.concatenate(limits, axis=0), head_count, axis=1)
        chain = [limits.reshape(len(stages), stage_rows)]

    def join(items, axis):
        return items[0] if len(items) == 1 else jnp.concatenate(items, axis=axis)

    vmem = pl.BlockSpec(memory_space=pltpu.VMEM)
    params = pltpu.CompilerParams(vmem_limit_bytes=20 << 20)
    pairs = [[cache_keys, cache_values], near_pair]
    stat = jax.ShapeDtypeStruct((1, stage_rows), jnp.float32)
    state_shapes = [stat, stat, jax.ShapeDtypeStruct((head_width, stage_rows), jnp.float32)]

    def packed_shape(lanes):
        return jax.ShapeDtypeStruct((head_width + tail_rows, lanes), jnp.bfloat16)

    def float_shapes(lanes):
        return [jax.ShapeDtypeStruct((size_of, lanes), jnp.float32) for size_of in (head_width, 1)]

    tiles = range(stage_rows // tile)
    whole_plan = [(at, "code", 0, at * tile, tile) for at in tiles]
    states = [None] * len(stages)

    def attend(index, blocks, plan=None, shapes=state_shapes):
        setup = None
        if chain[0] is None:
            setup = (own_tokens, head_count)
            shapes = shapes + [jax.ShapeDtypeStruct((len(stages), stage_rows), jnp.int32)]
            shapes += [jax.ShapeDtypeStruct(array.shape, array.dtype) for array in pairs[0]]
            own = [pltpu.with_memory_space_constraint(array, pltpu.HBM) for array in (query, *pairs[0])]
            operands = [positions.reshape(-1, 128), span_offset.reshape(1, 1)] + own
            specs = [vmem] * 2 + [pl.BlockSpec(memory_space=pltpu.HBM)] * 3
            extra = [pltpu.VMEM(query.shape, query.dtype), pltpu.SemaphoreType.DMA((3,))]
            operands += [array for b in blocks[1:] for array in pairs[b]]
        else:
            operands = [chain[0], stage_query[index]] + [array for b in blocks for array in pairs[b]]
            operands += list(states[index] or ())
            specs, extra = [], []
        results = pl.pallas_call(
            functools.partial(
                attend_kernel, scale, index, blocks, states[index] is not None, plan, setup
            ),
            in_specs=specs + [vmem] * (len(operands) - len(specs)),
            out_specs=[vmem] * len(shapes),
            out_shape=shapes,
            scratch_shapes=[
                pltpu.VMEM((2, shard_keys, tile), jnp.float32),
                pltpu.VMEM((2, shard_keys, tile), jnp.bfloat16),
                pltpu.VMEM((len(blocks), head_width + extra_rows, shard_keys), jnp.bfloat16),
            ]
            + extra,
            compiler_params=params,
        )(*operands)
        if setup:
            chain[0], pairs[0], results = results[-3], list(results[-2:]), results[:-3]
        chain[0], results = lax.optimization_barrier((chain[0], results))
        if plan is None:
            states[index] = results
        return results

    def hold(*arrays):
        chain[0], arrays = lax.optimization_barrier((chain[0], arrays))
        return list(arrays)

    stage_query = [None] * len(stages)

    def ready(index):
        stage_query[index] = join([got[k] for k in stages[index]], 0)

    for index in range(len(stages) - 1):
        gather(index)
        ready(index)
    attend(0, [0])
    for index in range(1, last - 1):
        attend(index, [0, 1])
    source = stages[last][0] ^ (stages[last][0] & -stages[last][0])
    (got[source],) = hold(got[source])
    gather(last)
    ready(last)
    far_pair[0], = hold(far_pair[0])
    across_keys = swap(far_pair[0], 1)
    attend(last - 1, [0, 1])
    ahead = stage_query[last - 1]
    block = jax.ShapeDtypeStruct((shard_keys, stage_rows), jnp.bfloat16)
    weighed = pl.pallas_call(
        functools.partial(weigh_kernel, scale, last - 1, [2, 3]),
        in_specs=[vmem] * 4,
        out_specs=[vmem] * 4,
        out_shape=[block, block, stat, stat],
        scratch_shapes=[pltpu.VMEM((2, shard_keys, tile), jnp.float32)],
        compiler_params=params,
        name="weigh",
    )(chain[0], ahead, far_pair[0], across_keys)
    weighed = hold(*weighed)
    far_pair[1], = hold(far_pair[1])
    across_values = swap(far_pair[1], 1)
    pairs += [far_pair, [across_keys, across_values]]
    packed = pl.pallas_call(
        functools.partial(finish_kernel, 2, whole_plan),
        in_specs=[vmem] * 9,
        out_specs=vmem,
        out_shape=packed_shape(stage_rows),
        scratch_shapes=[pltpu.VMEM((2, head_width + extra_rows, shard_keys), jnp.bfloat16)],
        compiler_params=params,
        name="finish",
    )(far_pair[1], across_values, *weighed, *states[last - 1])
    (packed,) = hold(packed)
    own_plan = [(at, "float", 0, at * tile, tile) for at in tiles]
    parts = []

    def send(index, packed):
        for at, k in enumerate(stages[index]):
            if k:
                piece = packed if per_stage == 1 else packed[:, at * rows : (at + 1) * rows]
                parts.append(swap(piece, inner * k))

    coded = [packed_shape(stage_rows)]
    if outer == 4:
        handed = swap(packed, inner)
        (packed,) = attend(1, [2, 3], whole_plan, coded)
        parts.append(swap(packed, inner))
        value, level = attend(3, [0, 1, 2, 3], own_plan, float_shapes(stage_rows))
        (handed,) = hold(handed)
        joined = pl.pallas_call(
            combine_kernel,
            in_specs=[vmem] * 3,
            out_specs=vmem,
            out_shape=coded[0],
            compiler_params=params,
            name="combine",
        )(value, level, handed)
        (joined,) = hold(joined)
        parts.append(swap(joined, 3 * inner))
    else:
        send(last - 1, packed)
        send(last, attend(last, [0, 1, 2, 3], whole_plan, coded)[0])
        for index in range(last - 2, 0, -1):
            send(index, attend(index, [2, 3], whole_plan, coded)[0])
    if per_stage == 1:
        own = attend(0, [1, 2, 3], own_plan, float_shapes(rows))
    else:
        own_plan = [(0, "float", 1, 0, rows)]
        packed, *own = attend(
            0, [1, 2, 3], whole_plan + own_plan, [packed_shape(stage_rows)] + float_shapes(rows)
        )
        send(0, packed)
    groups = [(slice(0, rows), [(at, 0) for at in range(len(parts))])]
    merged = pl.pallas_call(
        functools.partial(merge_kernel, groups),
        in_specs=[vmem] * (2 + len(parts)),
        out_specs=vmem,
        out_shape=jax.ShapeDtypeStruct((rows, head_width), jnp.bfloat16),
        compiler_params=params,
        name="merge",
    )(*own, *parts)
    return merged.reshape(own_tokens, head_count, head_width)


def solution(mesh):
    in_specs = (P("ctx", "kvh", None), P("ctx", "kvh"), P("ctx", "kvh"), P(), P())
    out_specs = P("ctx", "kvh", None)
    size = mesh.shape["ctx"]

    def body(*args):
        return local(size, *args)

    return jax.shard_map(body, mesh=mesh, in_specs=in_specs, out_specs=out_specs, check_vma=False)
```

```python
import functools

import jax
import jax.numpy as jnp
from jax import lax
from jax.experimental import pallas as pl
from jax.experimental.pallas import tpu as pltpu
from jax.sharding import PartitionSpec as P


masked_floor = -1e30
log2_e = 1.4426950408889634
inner = 4
extra_rows = 16
tail_rows = 8
code_span = 240.0
code_low = -120.0


def split_query(query, scale):
    scaled = query.astype(jnp.float32) * scale
    high = scaled.astype(jnp.bfloat16)
    low = (scaled - high.astype(jnp.float32)).astype(jnp.bfloat16)
    return jnp.concatenate([high, low], axis=1)


def transpose_values(values, values_ref):
    for b, value in enumerate(values):
        shard_keys, width = value.shape
        values_ref[b, :width, :] = value[...].T
        values_ref[b, width:, :] = jnp.ones((extra_rows, shard_keys), jnp.bfloat16)


def score_chunk(key, query_pair, limit, start, scores_ref, slot):
    chunk, tile = key.shape[0], query_pair.shape[0]
    scores = lax.dot_general(
        jnp.concatenate([key, key], axis=1), query_pair, (((1,), (1,)), ((), ())), preferred_element_type=jnp.float32
    ).reshape(chunk // 8, 8, tile)
    position = lax.broadcasted_iota(jnp.int32, scores.shape, 0) * 8 + start
    sublane = lax.broadcasted_iota(jnp.int32, (8, tile), 0)
    scores = jnp.where(position <= (limit - sublane)[None], scores, masked_floor)
    scores_ref[slot, start : start + chunk, :] = scores.reshape(chunk, tile)
    return jnp.max(scores, axis=0)


def add_block(state, values_t, weights, shard_max):
    width = values_t.shape[0] - extra_rows
    sums = lax.dot_general(values_t, weights, (((1,), (0,)), ((), ())), preferred_element_type=jnp.float32)
    num, den = sums[:width], sums[width : width + 1]
    if state is None:
        return shard_max, den, num
    top, run_den, run_num = state
    new_top = jnp.maximum(top, shard_max)
    keep, fresh = jnp.exp2(top - new_top), jnp.exp2(shard_max - new_top)
    return new_top, run_den * keep + den * fresh, run_num * keep + num * fresh


def sweep_tiles(rows, tile, query_pair, keys, limits, scores_ref, put_weights, finish):
    shard_keys = keys[0].shape[0]
    chunk = min(512, shard_keys)
    chunks = shard_keys // chunk
    tiles = [(b, h) for b in range(len(keys)) for h in range(rows // tile)]
    count = len(tiles)
    running, tops = [None] * count, [None] * count
    for step in range(count + 2):
        for c in range(chunks):
            span = slice(c * chunk, (c + 1) * chunk)
            if step < count:
                b, h = tiles[step]
                lanes = slice(h * tile, (h + 1) * tile)
                peak = score_chunk(
                    keys[b][span, :], query_pair[lanes], limits[b][:, lanes], c * chunk, scores_ref, step % 2
                )
                running[step] = peak if c == 0 else jnp.maximum(running[step], peak)
            if 1 <= step <= count:
                t = step - 1
                if c == 0:
                    tops[t] = jnp.max(running[t], axis=0, keepdims=True)
                put_weights(t, *tiles[t], span, jnp.exp2(scores_ref[t % 2, span, :] - tops[t]).astype(jnp.bfloat16))
            if step >= 2 and c == min(1, chunks - 1):
                finish(step - 2, *tiles[step - 2], tops[step - 2])


def attend_tiles(scale, query, keys, values, limits, states, scores_ref, weights_ref, values_ref):
    states = list(states)
    query_pair = split_query(query, scale)
    transpose_values(values, values_ref)

    def put_weights(t, b, h, span, weights):
        weights_ref[t % 2, span, :] = weights

    def finish(t, b, h, shard_max):
        states[h] = add_block(states[h], values_ref[b], weights_ref[t % 2], shard_max)

    sweep_tiles(query.shape[0], scores_ref.shape[2], query_pair, keys, limits, scores_ref, put_weights, finish)
    return states


def weigh_kernel(scale, index, blocks, limits_ref, q_ref, *refs):
    me = lax.axis_index("ctx")
    count = len(blocks)
    keys, weights, tops, scores_ref = refs[:count], refs[count : 2 * count], refs[2 * count : 3 * count], refs[-1]
    tile = scores_ref.shape[2]
    limits = [limits_ref[index : index + 1, :] - (me ^ b) * keys[0].shape[0] for b in blocks]

    def put_weights(t, b, h, span, value):
        weights[b][span, h * tile : (h + 1) * tile] = value

    def finish(t, b, h, shard_max):
        tops[b][:, h * tile : (h + 1) * tile] = shard_max

    query_pair = split_query(q_ref[...], scale)
    sweep_tiles(q_ref.shape[0], tile, query_pair, keys, limits, scores_ref, put_weights, finish)


def finish_kernel(count, plan, *refs):
    values, weights, tops = refs[:count], refs[count : 2 * count], refs[2 * count : 3 * count]
    state_refs, outs, values_ref = refs[3 * count : 3 * count + 3], refs[3 * count + 3 : -1], refs[-1]
    transpose_values(values, values_ref)
    if plan is None:
        state = tuple(ref[...] for ref in state_refs)
        for b in range(count):
            state = add_block(state, values_ref[b], weights[b][...], tops[b][...])
        for ref, value in zip(outs, state):
            ref[...] = value
        return
    for at, form, out, offset, lanes in plan:
        span = slice(at * lanes, (at + 1) * lanes)
        state = tuple(ref[:, span] for ref in state_refs)
        for b in range(count):
            state = add_block(state, values_ref[b], weights[b][:, span], tops[b][:, span])
        top, den, num = state
        write_partial(outs[out:], form, slice(offset, offset + lanes), num * (1.0 / den), top + jnp.log2(den))


def encode(values, level):
    _, lanes = values.shape
    size = jnp.abs(values)
    peak = jnp.maximum(jnp.max(size, axis=0, keepdims=True), 1e-30).astype(jnp.bfloat16).astype(jnp.float32)
    code = jnp.exp2(size * (code_span / peak) + code_low)
    code = jnp.where(values < 0, -code, code)
    high = level.astype(jnp.bfloat16).astype(jnp.float32)
    rest = level - high
    middle = rest.astype(jnp.bfloat16).astype(jnp.float32)
    row = lax.broadcasted_iota(jnp.int32, (tail_rows, lanes), 0)
    tail = jnp.where(row == 0, high, jnp.where(row == 1, middle, jnp.where(row == 2, rest - middle, peak)))
    return code.astype(jnp.bfloat16), tail.astype(jnp.bfloat16)


def decode(codes, tail):
    codes, tail = codes.astype(jnp.float32), tail.astype(jnp.float32)
    level = tail[0:1] + tail[1:2] + tail[2:3]
    size = (jnp.log2(jnp.abs(codes)) - code_low) * (tail[3:4] * (1.0 / code_span))
    return jnp.where(codes < 0, -size, size), level


def spread_limits(me, own_tokens, head_count, offsets_ref, span_ref, limits_ref):
    count, lanes = limits_ref.shape
    width = offsets_ref.shape[1]
    per_row = width // own_tokens
    parts = []
    for k in range(count):
        device = me ^ (k * inner)
        row = offsets_ref[pl.ds(device // per_row, 1), :]
        row = pltpu.roll(row, (width - (device % per_row) * own_tokens) % width, 1)
        parts += [row >> 8, row & 255]
    parts = jnp.concatenate(parts, axis=0).astype(jnp.float32).astype(jnp.bfloat16)
    token = lax.broadcasted_iota(jnp.int32, (width, lanes), 0)
    lane = lax.broadcasted_iota(jnp.int32, (width, lanes), 1)
    first = token * head_count
    spread = jnp.where((lane >= first) & (lane < first + head_count), 1.0, 0.0).astype(jnp.bfloat16)
    wide = lax.dot_general(parts, spread, (((1,), (0,)), ((), ())), preferred_element_type=jnp.float32)
    wide = wide.astype(jnp.int32)
    for k in range(count):
        limits_ref[k : k + 1, :] = wide[2 * k : 2 * k + 1] * 256 + wide[2 * k + 1 : 2 * k + 2] + span_ref[...]


def attend_kernel(scale, index, blocks, has_state, plan, setup, *refs):
    me = lax.axis_index("ctx")
    refs = list(refs)
    if setup:
        offsets_ref, span_ref, q_hbm, k_hbm, v_hbm = refs[:5]
        arrived, q_ref = refs.pop(), refs.pop()
        scratch = [refs.pop() for _ in range(3)][::-1]
        v_ref, k_ref, limits_ref = refs.pop(), refs.pop(), refs.pop()
        pairs = ((q_hbm, q_ref), (k_hbm, k_ref), (v_hbm, v_ref))
        copies = [pltpu.make_async_copy(*pair, arrived.at[at]) for at, pair in enumerate(pairs)]
        for copy in copies:
            copy.start()
        spread_limits(me, *setup, offsets_ref, span_ref, limits_ref)
        for copy in copies:
            copy.wait()
        refs = [limits_ref, q_ref, k_ref, v_ref] + refs[5:]
    else:
        scratch = [refs.pop() for _ in range(3)][::-1]
        limits_ref, q_ref = refs[:2]
    keys = refs[2 : 2 + 2 * len(blocks) : 2]
    values = refs[3 : 3 + 2 * len(blocks) : 2]
    rest = list(refs[2 + 2 * len(blocks) :])
    rows, _ = q_ref.shape
    tile = scratch[0].shape[2]
    spans = [slice(at, at + tile) for at in range(0, rows, tile)]
    states = [None] * len(spans)
    if has_state:
        states = [tuple(ref[:, span] for ref in rest[:3]) for span in spans]
        rest = rest[3:]
    limits = [limits_ref[index : index + 1, :] - (me ^ b) * keys[0].shape[0] for b in blocks]
    states = attend_tiles(scale, q_ref[...], keys, values, limits, states, *scratch)
    if plan is None:
        for span, state in zip(spans, states):
            for ref, value in zip(rest, state):
                ref[:, span] = value
        return
    for at, form, out, offset, count in plan:
        top, den, num = (value[:, :count] for value in states[at])
        write_partial(rest[out:], form, slice(offset, offset + count), num * (1.0 / den), top + jnp.log2(den))


def write_partial(refs, form, span, value, level):
    width = value.shape[0]
    if form == "float":
        refs[0][:, span] = value
        refs[1][:, span] = level
    else:
        code, tail = encode(value, level)
        refs[0][:width, span] = code
        refs[0][width:, span] = tail


def combine(values, levels):
    top = functools.reduce(jnp.maximum, levels)
    factors = [jnp.exp2(level - top) for level in levels]
    total = functools.reduce(jnp.add, factors)
    inverse = 1.0 / total
    value = functools.reduce(jnp.add, [value * (factor * inverse) for value, factor in zip(values, factors)])
    return value, top + jnp.log2(total)


def combine_kernel(form, value_ref, level_ref, part_ref, *out_refs):
    width, lanes = value_ref.shape
    value, level = decode(part_ref[:width, :], part_ref[width:, :])
    value, level = combine([value_ref[...], value], [level_ref[...], level])
    write_partial(out_refs, form, slice(0, lanes), value, level)


def merge_kernel(groups, *refs):
    own_ref, own_level_ref = refs[:2]
    parts, out_ref = refs[2:-1], refs[-1]
    width = own_ref.shape[0]
    for span, members in groups:
        values, levels = [own_ref[:, span]], [own_level_ref[:, span]]
        for at, offset in members:
            lanes = slice(offset, offset + span.stop - span.start)
            value, level = decode(parts[at][:width, lanes], parts[at][width:, lanes])
            values.append(value)
            levels.append(level)
        out_ref[span, :] = combine(values, levels)[0].T.astype(out_ref.dtype)


def local(size, queries, cache_keys, cache_values, span_offset, positions):
    own_tokens, head_count, head_width = queries.shape
    shard_keys = cache_keys.shape[0]
    outer = size // inner
    rows = own_tokens * head_count
    me = lax.axis_index("ctx")
    place, owner = me % inner, me // inner
    scale = head_width ** (-0.5) * log2_e

    def swap(array, step):
        return lax.ppermute(array, "ctx", [(i, i ^ step) for i in range(size)])

    query = queries.reshape(rows, head_width)
    per_stage = max(outer // 4, 1)
    stages = [list(range(s, s + per_stage)) for s in range(0, outer, per_stage)]
    last = len(stages) - 1

    far_pair = [swap(cache_keys, 2), swap(cache_values, 2)]
    near_pair = [swap(cache_keys, 1), swap(cache_values, 1)]
    got = [query] + [None] * (outer - 1)

    def gather(index):
        for k in stages[index]:
            if k:
                low = k & -k
                got[k] = swap(got[k ^ low], inner * low)

    stage_rows = rows * per_stage
    tile = 256 if stage_rows % 256 == 0 else stage_rows

    fused_setup = per_stage == 1 and positions.shape[0] % 128 == 0 and 128 % own_tokens == 0
    if fused_setup:
        chain = [None]
    else:
        limits = (span_offset[0] + positions).reshape(outer, inner, own_tokens)
        limits = lax.dynamic_index_in_dim(limits, place, 1, keepdims=False)
        limits = [lax.dynamic_slice_in_dim(limits, owner ^ k, 1, axis=0) for k in range(outer)]
        limits = jnp.repeat(jnp.concatenate(limits, axis=0), head_count, axis=1)
        chain = [limits.reshape(len(stages), stage_rows)]

    def join(items, axis):
        return items[0] if len(items) == 1 else jnp.concatenate(items, axis=axis)

    vmem = pl.BlockSpec(memory_space=pltpu.VMEM)
    params = pltpu.CompilerParams(vmem_limit_bytes=20 << 20)
    pairs = [[cache_keys, cache_values], near_pair]
    stat = jax.ShapeDtypeStruct((1, stage_rows), jnp.float32)
    state_shapes = [stat, stat, jax.ShapeDtypeStruct((head_width, stage_rows), jnp.float32)]

    def packed_shape(lanes):
        return jax.ShapeDtypeStruct((head_width + tail_rows, lanes), jnp.bfloat16)

    def float_shapes(lanes):
        return [jax.ShapeDtypeStruct((size_of, lanes), jnp.float32) for size_of in (head_width, 1)]

    tiles = range(stage_rows // tile)
    whole_plan = [(at, "code", 0, at * tile, tile) for at in tiles]
    states = [None] * len(stages)

    def attend(index, blocks, plan=None, shapes=state_shapes):
        setup = None
        if chain[0] is None:
            setup = (own_tokens, head_count)
            shapes = shapes + [jax.ShapeDtypeStruct((len(stages), stage_rows), jnp.int32)]
            shapes += [jax.ShapeDtypeStruct(array.shape, array.dtype) for array in pairs[0]]
            own = [pltpu.with_memory_space_constraint(array, pltpu.HBM) for array in (query, *pairs[0])]
            operands = [positions.reshape(-1, 128), span_offset.reshape(1, 1)] + own
            specs = [vmem] * 2 + [pl.BlockSpec(memory_space=pltpu.HBM)] * 3
            extra = [pltpu.VMEM(query.shape, query.dtype), pltpu.SemaphoreType.DMA((3,))]
            operands += [array for b in blocks[1:] for array in pairs[b]]
        else:
            operands = [chain[0], stage_query[index]] + [array for b in blocks for array in pairs[b]]
            operands += list(states[index] or ())
            specs, extra = [], []
        results = pl.pallas_call(
            functools.partial(
                attend_kernel, scale, index, blocks, states[index] is not None, plan, setup
            ),
            in_specs=specs + [vmem] * (len(operands) - len(specs)),
            out_specs=[vmem] * len(shapes),
            out_shape=shapes,
            scratch_shapes=[
                pltpu.VMEM((2, shard_keys, tile), jnp.float32),
                pltpu.VMEM((2, shard_keys, tile), jnp.bfloat16),
                pltpu.VMEM((len(blocks), head_width + extra_rows, shard_keys), jnp.bfloat16),
            ]
            + extra,
            compiler_params=params,
        )(*operands)
        if setup:
            chain[0], pairs[0], results = results[-3], list(results[-2:]), results[:-3]
        chain[0], results = lax.optimization_barrier((chain[0], results))
        if plan is None:
            states[index] = results
        return results

    def hold(*arrays):
        chain[0], arrays = lax.optimization_barrier((chain[0], arrays))
        return list(arrays)

    stage_query = [None] * len(stages)

    def ready(index):
        stage_query[index] = join([got[k] for k in stages[index]], 0)

    for index in range(len(stages) - 1):
        gather(index)
        ready(index)
    attend(0, [0])
    for index in range(1, last - 1):
        attend(index, [0, 1])
    far_pair[0], = hold(far_pair[0])
    across_keys = swap(far_pair[0], 1)
    attend(last - 1, [0, 1])
    source = stages[last][0] ^ (stages[last][0] & -stages[last][0])
    (got[source],) = hold(got[source])
    gather(last)
    ready(last)
    ahead = stage_query[last - 1]
    block = jax.ShapeDtypeStruct((shard_keys, stage_rows), jnp.bfloat16)
    weighed = pl.pallas_call(
        functools.partial(weigh_kernel, scale, last - 1, [2, 3]),
        in_specs=[vmem] * 4,
        out_specs=[vmem] * 4,
        out_shape=[block, block, stat, stat],
        scratch_shapes=[pltpu.VMEM((2, shard_keys, tile), jnp.float32)],
        compiler_params=params,
        name="weigh",
    )(chain[0], ahead, far_pair[0], across_keys)
    weighed = hold(*weighed)
    far_pair[1], = hold(far_pair[1])
    across_values = swap(far_pair[1], 1)
    pairs += [far_pair, [across_keys, across_values]]

    def finish(values, weights, top, plan, shapes):
        results = pl.pallas_call(
            functools.partial(finish_kernel, 1, plan),
            in_specs=[vmem] * 6,
            out_specs=[vmem] * len(shapes),
            out_shape=shapes,
            scratch_shapes=[pltpu.VMEM((1, head_width + extra_rows, shard_keys), jnp.bfloat16)],
            compiler_params=params,
        )(values, weights, top, *states[last - 1])
        return hold(*results)

    states[last - 1] = finish(far_pair[1], weighed[0], weighed[2], None, state_shapes)
    if outer == 4:
        attend(1, [2])
    (across_values,) = hold(across_values)
    pairs[3] = [across_keys, across_values]
    (packed,) = finish(across_values, weighed[1], weighed[3], whole_plan, [packed_shape(stage_rows)])
    own_plan = [(at, "float", 0, at * tile, tile) for at in tiles]
    parts = []

    def send(index, packed):
        for at, k in enumerate(stages[index]):
            if k:
                piece = packed if per_stage == 1 else packed[:, at * rows : (at + 1) * rows]
                parts.append(swap(piece, inner * k))

    coded = [packed_shape(stage_rows)]

    def fold(form, value, level, part, shapes):
        return pl.pallas_call(
            functools.partial(combine_kernel, form),
            in_specs=[vmem] * 3,
            out_specs=[vmem] * len(shapes),
            out_shape=shapes,
            compiler_params=params,
        )(value, level, part)

    if outer == 4:
        handed = swap(packed, inner)
        (packed,) = attend(1, [3], whole_plan, coded)
        parts.append(swap(packed, inner))
        value, level = attend(3, [0, 1, 2, 3], own_plan, float_shapes(stage_rows))
        (handed,) = hold(handed)
        (joined,) = fold("code", value, level, handed, coded)
        (joined,) = hold(joined)
        parts.append(swap(joined, 3 * inner))
    else:
        send(last - 1, packed)
        send(last, attend(last, [0, 1, 2, 3], whole_plan, coded)[0])
        for index in range(last - 2, 0, -1):
            send(index, attend(index, [2, 3], whole_plan, coded)[0])
    if per_stage == 1:
        own = attend(0, [1, 2, 3], own_plan, float_shapes(rows))
        if outer == 4:
            own = fold("float", *own, parts.pop(0), float_shapes(rows))
    else:
        own_plan = [(0, "float", 1, 0, rows)]
        packed, *own = attend(
            0, [1, 2, 3], whole_plan + own_plan, [packed_shape(stage_rows)] + float_shapes(rows)
        )
        send(0, packed)
    groups = [(slice(0, rows), [(at, 0) for at in range(len(parts))])]
    merged = pl.pallas_call(
        functools.partial(merge_kernel, groups),
        in_specs=[vmem] * (2 + len(parts)),
        out_specs=vmem,
        out_shape=jax.ShapeDtypeStruct((rows, head_width), jnp.bfloat16),
        compiler_params=params,
        name="merge",
    )(*own, *parts)
    return merged.reshape(own_tokens, head_count, head_width)


def solution(mesh):
    in_specs = (P("ctx", "kvh", None), P("ctx", "kvh"), P("ctx", "kvh"), P(), P())
    out_specs = P("ctx", "kvh", None)
    size = mesh.shape["ctx"]

    def body(*args):
        return local(size, *args)

    return jax.shard_map(body, mesh=mesh, in_specs=in_specs, out_specs=out_specs, check_vma=False)
```

```python
import functools

import jax
import jax.numpy as jnp
from jax import lax
from jax.experimental import pallas as pl
from jax.experimental.pallas import tpu as pltpu
from jax.sharding import PartitionSpec as P


masked_floor = -1e30
log2_e = 1.4426950408889634
inner = 4
extra_rows = 16
tail_rows = 8
code_span = 240.0
code_low = -120.0


def split_query(query, scale):
    scaled = query.astype(jnp.float32) * scale
    high = scaled.astype(jnp.bfloat16)
    low = (scaled - high.astype(jnp.float32)).astype(jnp.bfloat16)
    return jnp.concatenate([high, low], axis=1)


def transpose_values(values, values_ref):
    shard_keys = values_ref.shape[2]
    for b, pieces in enumerate(values):
        for at, piece in enumerate(pieces):
            count, width = piece.shape
            values_ref[b, :width, at * count : (at + 1) * count] = piece[...].T
        values_ref[b, width:, :] = jnp.ones((extra_rows, shard_keys), jnp.bfloat16)


def score_chunk(key, query_pair, limit, start, scores_ref, slot):
    chunk, tile = key.shape[0], query_pair.shape[0]
    scores = lax.dot_general(
        jnp.concatenate([key, key], axis=1), query_pair, (((1,), (1,)), ((), ())), preferred_element_type=jnp.float32
    ).reshape(chunk // 8, 8, tile)
    position = lax.broadcasted_iota(jnp.int32, scores.shape, 0) * 8 + start
    sublane = lax.broadcasted_iota(jnp.int32, (8, tile), 0)
    scores = jnp.where(position <= (limit - sublane)[None], scores, masked_floor)
    scores_ref[slot, start : start + chunk, :] = scores.reshape(chunk, tile)
    return jnp.max(scores, axis=0)


def add_block(state, values_t, weights, shard_max):
    width = values_t.shape[0] - extra_rows
    sums = lax.dot_general(values_t, weights, (((1,), (0,)), ((), ())), preferred_element_type=jnp.float32)
    num, den = sums[:width], sums[width : width + 1]
    if state is None:
        return shard_max, den, num
    top, run_den, run_num = state
    new_top = jnp.maximum(top, shard_max)
    keep, fresh = jnp.exp2(top - new_top), jnp.exp2(shard_max - new_top)
    return new_top, run_den * keep + den * fresh, run_num * keep + num * fresh


def sweep_tiles(rows, tile, query_pair, keys, limits, scores_ref, put_weights, finish):
    shard_keys = keys[0].shape[0]
    chunk = min(512, shard_keys)
    chunks = shard_keys // chunk
    tiles = [(b, h) for b in range(len(keys)) for h in range(rows // tile)]
    count = len(tiles)
    running, tops = [None] * count, [None] * count
    for step in range(count + 2):
        for c in range(chunks):
            span = slice(c * chunk, (c + 1) * chunk)
            if step < count:
                b, h = tiles[step]
                lanes = slice(h * tile, (h + 1) * tile)
                peak = score_chunk(
                    keys[b][span, :], query_pair[lanes], limits[b][:, lanes], c * chunk, scores_ref, step % 2
                )
                running[step] = peak if c == 0 else jnp.maximum(running[step], peak)
            if 1 <= step <= count:
                t = step - 1
                if c == 0:
                    tops[t] = jnp.max(running[t], axis=0, keepdims=True)
                put_weights(t, *tiles[t], span, jnp.exp2(scores_ref[t % 2, span, :] - tops[t]).astype(jnp.bfloat16))
            if step >= 2 and c == min(1, chunks - 1):
                finish(step - 2, *tiles[step - 2], tops[step - 2])


def attend_tiles(scale, query, keys, values, limits, states, scores_ref, weights_ref, values_ref):
    states = list(states)
    query_pair = split_query(query, scale)
    transpose_values(values, values_ref)

    def put_weights(t, b, h, span, weights):
        weights_ref[t % 2, span, :] = weights

    def finish(t, b, h, shard_max):
        states[h] = add_block(states[h], values_ref[b], weights_ref[t % 2], shard_max)

    sweep_tiles(query.shape[0], scores_ref.shape[2], query_pair, keys, limits, scores_ref, put_weights, finish)
    return states


def weigh_kernel(scale, index, blocks, limits_ref, q_ref, *refs):
    me = lax.axis_index("ctx")
    count = len(blocks)
    keys, weights, tops, scores_ref = refs[:count], refs[count : 2 * count], refs[2 * count : 3 * count], refs[-1]
    tile = scores_ref.shape[2]
    limits = [limits_ref[index : index + 1, :] - (me ^ b) * keys[0].shape[0] for b in blocks]

    def put_weights(t, b, h, span, value):
        weights[b][span, h * tile : (h + 1) * tile] = value

    def finish(t, b, h, shard_max):
        tops[b][:, h * tile : (h + 1) * tile] = shard_max

    query_pair = split_query(q_ref[...], scale)
    sweep_tiles(q_ref.shape[0], tile, query_pair, keys, limits, scores_ref, put_weights, finish)


def finish_kernel(pieces, plan, weights_ref, peaks_ref, top_ref, den_ref, num_ref, *refs):
    state_refs = (top_ref, den_ref, num_ref)
    values, outs, values_ref = refs[:pieces], refs[pieces:-1], refs[-1]
    transpose_values([values], values_ref)
    if plan is None:
        state = tuple(ref[...] for ref in state_refs)
        state = add_block(state, values_ref[0], weights_ref[...], peaks_ref[...])
        for ref, value in zip(outs, state):
            ref[...] = value
        return
    for at, form, out, offset, lanes in plan:
        span = slice(at * lanes, (at + 1) * lanes)
        state = tuple(ref[:, span] for ref in state_refs)
        top, den, num = add_block(state, values_ref[0], weights_ref[:, span], peaks_ref[:, span])
        write_partial(outs[out:], form, slice(offset, offset + lanes), num * (1.0 / den), top + jnp.log2(den))


def encode(values, level):
    _, lanes = values.shape
    size = jnp.abs(values)
    peak = jnp.maximum(jnp.max(size, axis=0, keepdims=True), 1e-30).astype(jnp.bfloat16).astype(jnp.float32)
    code = jnp.exp2(size * (code_span / peak) + code_low)
    code = jnp.where(values < 0, -code, code)
    high = level.astype(jnp.bfloat16).astype(jnp.float32)
    rest = level - high
    middle = rest.astype(jnp.bfloat16).astype(jnp.float32)
    row = lax.broadcasted_iota(jnp.int32, (tail_rows, lanes), 0)
    tail = jnp.where(row == 0, high, jnp.where(row == 1, middle, jnp.where(row == 2, rest - middle, peak)))
    return code.astype(jnp.bfloat16), tail.astype(jnp.bfloat16)


def decode(codes, tail):
    codes, tail = codes.astype(jnp.float32), tail.astype(jnp.float32)
    level = tail[0:1] + tail[1:2] + tail[2:3]
    size = (jnp.log2(jnp.abs(codes)) - code_low) * (tail[3:4] * (1.0 / code_span))
    return jnp.where(codes < 0, -size, size), level


def spread_limits(me, own_tokens, head_count, offsets_ref, span_ref, limits_ref):
    count, lanes = limits_ref.shape
    width = offsets_ref.shape[1]
    per_row = width // own_tokens
    parts = []
    for k in range(count):
        device = me ^ (k * inner)
        row = offsets_ref[pl.ds(device // per_row, 1), :]
        row = pltpu.roll(row, (width - (device % per_row) * own_tokens) % width, 1)
        parts += [row >> 8, row & 255]
    parts = jnp.concatenate(parts, axis=0).astype(jnp.float32).astype(jnp.bfloat16)
    token = lax.broadcasted_iota(jnp.int32, (width, lanes), 0)
    lane = lax.broadcasted_iota(jnp.int32, (width, lanes), 1)
    first = token * head_count
    spread = jnp.where((lane >= first) & (lane < first + head_count), 1.0, 0.0).astype(jnp.bfloat16)
    wide = lax.dot_general(parts, spread, (((1,), (0,)), ((), ())), preferred_element_type=jnp.float32)
    wide = wide.astype(jnp.int32)
    for k in range(count):
        limits_ref[k : k + 1, :] = wide[2 * k : 2 * k + 1] * 256 + wide[2 * k + 1 : 2 * k + 2] + span_ref[...]


def attend_kernel(scale, index, blocks, pieces, has_state, plan, setup, *refs):
    me = lax.axis_index("ctx")
    refs = list(refs)
    if setup:
        offsets_ref, span_ref, q_hbm, k_hbm, v_hbm = refs[:5]
        arrived, q_ref = refs.pop(), refs.pop()
        scratch = [refs.pop() for _ in range(3)][::-1]
        v_ref, k_ref, limits_ref = refs.pop(), refs.pop(), refs.pop()
        pairs = ((q_hbm, q_ref), (k_hbm, k_ref), (v_hbm, v_ref))
        copies = [pltpu.make_async_copy(*pair, arrived.at[at]) for at, pair in enumerate(pairs)]
        for copy in copies:
            copy.start()
        spread_limits(me, *setup, offsets_ref, span_ref, limits_ref)
        for copy in copies:
            copy.wait()
        refs = [limits_ref, q_ref, k_ref, v_ref] + refs[5:]
    else:
        scratch = [refs.pop() for _ in range(3)][::-1]
        limits_ref, q_ref = refs[:2]
    rest = list(refs[2:])
    keys, values = [], []
    for count in pieces:
        keys.append(rest.pop(0))
        values.append([rest.pop(0) for _ in range(count)])
    rows, _ = q_ref.shape
    tile = scratch[0].shape[2]
    spans = [slice(at, at + tile) for at in range(0, rows, tile)]
    states = [None] * len(spans)
    if has_state:
        states = [tuple(ref[:, span] for ref in rest[:3]) for span in spans]
        rest = rest[3:]
    limits = [limits_ref[index : index + 1, :] - (me ^ b) * keys[0].shape[0] for b in blocks]
    states = attend_tiles(scale, q_ref[...], keys, values, limits, states, *scratch)
    if plan is None:
        for span, state in zip(spans, states):
            for ref, value in zip(rest, state):
                ref[:, span] = value
        return
    for at, form, out, offset, count in plan:
        top, den, num = (value[:, :count] for value in states[at])
        write_partial(rest[out:], form, slice(offset, offset + count), num * (1.0 / den), top + jnp.log2(den))


def write_partial(refs, form, span, value, level):
    width = value.shape[0]
    if form == "float":
        refs[0][:, span] = value
        refs[1][:, span] = level
    else:
        code, tail = encode(value, level)
        refs[0][:width, span] = code
        refs[0][width:, span] = tail


def combine(values, levels):
    top = functools.reduce(jnp.maximum, levels)
    factors = [jnp.exp2(level - top) for level in levels]
    total = functools.reduce(jnp.add, factors)
    inverse = 1.0 / total
    value = functools.reduce(jnp.add, [value * (factor * inverse) for value, factor in zip(values, factors)])
    return value, top + jnp.log2(total)


def combine_kernel(form, value_ref, level_ref, part_ref, *out_refs):
    width, lanes = value_ref.shape
    value, level = decode(part_ref[:width, :], part_ref[width:, :])
    value, level = combine([value_ref[...], value], [level_ref[...], level])
    write_partial(out_refs, form, slice(0, lanes), value, level)


def merge_kernel(groups, *refs):
    own_ref, own_level_ref = refs[:2]
    parts, out_ref = refs[2:-1], refs[-1]
    width = own_ref.shape[0]
    for span, members in groups:
        values, levels = [own_ref[:, span]], [own_level_ref[:, span]]
        for at, offset in members:
            lanes = slice(offset, offset + span.stop - span.start)
            value, level = decode(parts[at][:width, lanes], parts[at][width:, lanes])
            values.append(value)
            levels.append(level)
        out_ref[span, :] = combine(values, levels)[0].T.astype(out_ref.dtype)


def local(size, queries, cache_keys, cache_values, span_offset, positions):
    own_tokens, head_count, head_width = queries.shape
    shard_keys = cache_keys.shape[0]
    outer = size // inner
    rows = own_tokens * head_count
    me = lax.axis_index("ctx")
    place, owner = me % inner, me // inner
    scale = head_width ** (-0.5) * log2_e

    def swap(array, step):
        return lax.ppermute(array, "ctx", [(i, i ^ step) for i in range(size)])

    query = queries.reshape(rows, head_width)
    per_stage = max(outer // 4, 1)
    stages = [list(range(s, s + per_stage)) for s in range(0, outer, per_stage)]
    last = len(stages) - 1

    half = shard_keys // 2
    far_keys = swap(cache_keys, 2)
    far_values = [swap(cache_values[at * half : (at + 1) * half], 2) for at in range(2)]
    near_pair = [swap(cache_keys, 1), swap(cache_values, 1)]
    got = [query] + [None] * (outer - 1)

    def gather(index):
        for k in stages[index]:
            if k:
                low = k & -k
                got[k] = swap(got[k ^ low], inner * low)

    stage_rows = rows * per_stage
    tile = 256 if stage_rows % 256 == 0 else stage_rows

    fused_setup = per_stage == 1 and positions.shape[0] % 128 == 0 and 128 % own_tokens == 0
    if fused_setup:
        chain = [None]
    else:
        limits = (span_offset[0] + positions).reshape(outer, inner, own_tokens)
        limits = lax.dynamic_index_in_dim(limits, place, 1, keepdims=False)
        limits = [lax.dynamic_slice_in_dim(limits, owner ^ k, 1, axis=0) for k in range(outer)]
        limits = jnp.repeat(jnp.concatenate(limits, axis=0), head_count, axis=1)
        chain = [limits.reshape(len(stages), stage_rows)]

    def join(items, axis):
        return items[0] if len(items) == 1 else jnp.concatenate(items, axis=axis)

    vmem = pl.BlockSpec(memory_space=pltpu.VMEM)
    params = pltpu.CompilerParams(vmem_limit_bytes=20 << 20)
    pairs = [[cache_keys, cache_values], near_pair]
    stat = jax.ShapeDtypeStruct((1, stage_rows), jnp.float32)
    state_shapes = [stat, stat, jax.ShapeDtypeStruct((head_width, stage_rows), jnp.float32)]

    def packed_shape(lanes):
        return jax.ShapeDtypeStruct((head_width + tail_rows, lanes), jnp.bfloat16)

    def float_shapes(lanes):
        return [jax.ShapeDtypeStruct((size_of, lanes), jnp.float32) for size_of in (head_width, 1)]

    tiles = range(stage_rows // tile)
    whole_plan = [(at, "code", 0, at * tile, tile) for at in tiles]
    states = [None] * len(stages)

    def attend(index, blocks, plan=None, shapes=state_shapes):
        setup = None
        if chain[0] is None:
            setup = (own_tokens, head_count)
            shapes = shapes + [jax.ShapeDtypeStruct((len(stages), stage_rows), jnp.int32)]
            shapes += [jax.ShapeDtypeStruct(array.shape, array.dtype) for array in pairs[0]]
            own = [pltpu.with_memory_space_constraint(array, pltpu.HBM) for array in (query, *pairs[0])]
            operands = [positions.reshape(-1, 128), span_offset.reshape(1, 1)] + own
            specs = [vmem] * 2 + [pl.BlockSpec(memory_space=pltpu.HBM)] * 3
            extra = [pltpu.VMEM(query.shape, query.dtype), pltpu.SemaphoreType.DMA((3,))]
            operands += [array for b in blocks[1:] for array in pairs[b]]
        else:
            operands = [chain[0], stage_query[index]] + [array for b in blocks for array in pairs[b]]
            operands += list(states[index] or ())
            specs, extra = [], []
        results = pl.pallas_call(
            functools.partial(
                attend_kernel,
                scale,
                index,
                blocks,
                [len(pairs[b]) - 1 for b in blocks],
                states[index] is not None,
                plan,
                setup,
            ),
            in_specs=specs + [vmem] * (len(operands) - len(specs)),
            out_specs=[vmem] * len(shapes),
            out_shape=shapes,
            scratch_shapes=[
                pltpu.VMEM((2, shard_keys, tile), jnp.float32),
                pltpu.VMEM((2, shard_keys, tile), jnp.bfloat16),
                pltpu.VMEM((len(blocks), head_width + extra_rows, shard_keys), jnp.bfloat16),
            ]
            + extra,
            compiler_params=params,
        )(*operands)
        if setup:
            chain[0], pairs[0], results = results[-3], list(results[-2:]), results[:-3]
        chain[0], results = lax.optimization_barrier((chain[0], results))
        if plan is None:
            states[index] = results
        return results

    def hold(*arrays):
        chain[0], arrays = lax.optimization_barrier((chain[0], arrays))
        return list(arrays)

    stage_query = [None] * len(stages)

    def ready(index):
        stage_query[index] = join([got[k] for k in stages[index]], 0)

    for index in range(len(stages) - 1):
        gather(index)
        ready(index)
    attend(0, [0])
    for index in range(1, last - 1):
        attend(index, [0, 1])
    (far_keys,) = hold(far_keys)
    across_keys = swap(far_keys, 1)
    attend(last - 1, [0, 1])
    source = stages[last][0] ^ (stages[last][0] & -stages[last][0])
    (got[source],) = hold(got[source])
    gather(last)
    ready(last)
    across_values = [None, None]

    def pass_values(at):
        (far_values[at],) = hold(far_values[at])
        across_values[at] = swap(far_values[at], 1)

    pass_values(0)
    ahead = stage_query[last - 1]
    block = jax.ShapeDtypeStruct((shard_keys, stage_rows), jnp.bfloat16)
    weighed = pl.pallas_call(
        functools.partial(weigh_kernel, scale, last - 1, [2, 3]),
        in_specs=[vmem] * 4,
        out_specs=[vmem] * 4,
        out_shape=[block, block, stat, stat],
        scratch_shapes=[pltpu.VMEM((2, shard_keys, tile), jnp.float32)],
        compiler_params=params,
        name="weigh",
    )(chain[0], ahead, far_keys, across_keys)
    weighed = hold(*weighed)
    pass_values(1)

    def finish(values, weights, peaks, plan, shapes):
        results = pl.pallas_call(
            functools.partial(finish_kernel, len(values), plan),
            in_specs=[vmem] * (5 + len(values)),
            out_specs=[vmem] * len(shapes),
            out_shape=shapes,
            scratch_shapes=[pltpu.VMEM((1, head_width + extra_rows, shard_keys), jnp.bfloat16)],
            compiler_params=params,
        )(weights, peaks, *states[last - 1], *values)
        return hold(*results)

    states[last - 1] = finish(far_values, weighed[0], weighed[2], None, state_shapes)
    across_values = hold(*across_values)
    pairs += [[far_keys, *far_values], [across_keys, *across_values]]
    (packed,) = finish(across_values, weighed[1], weighed[3], whole_plan, [packed_shape(stage_rows)])
    own_plan = [(at, "float", 0, at * tile, tile) for at in tiles]
    parts = []

    def send(index, packed):
        for at, k in enumerate(stages[index]):
            if k:
                piece = packed if per_stage == 1 else packed[:, at * rows : (at + 1) * rows]
                parts.append(swap(piece, inner * k))

    coded = [packed_shape(stage_rows)]

    def fold(form, value, level, part, shapes):
        return pl.pallas_call(
            functools.partial(combine_kernel, form),
            in_specs=[vmem] * 3,
            out_specs=[vmem] * len(shapes),
            out_shape=shapes,
            compiler_params=params,
        )(value, level, part)

    if outer == 4:
        handed = swap(packed, inner)
        (packed,) = attend(1, [2, 3], whole_plan, coded)
        parts.append(swap(packed, inner))
        value, level = attend(3, [0, 1, 2, 3], own_plan, float_shapes(stage_rows))
        (handed,) = hold(handed)
        (joined,) = fold("code", value, level, handed, coded)
        (joined,) = hold(joined)
        parts.append(swap(joined, 3 * inner))
    else:
        send(last - 1, packed)
        send(last, attend(last, [0, 1, 2, 3], whole_plan, coded)[0])
        for index in range(last - 2, 0, -1):
            send(index, attend(index, [2, 3], whole_plan, coded)[0])
    if per_stage == 1:
        own = attend(0, [1, 2, 3], own_plan, float_shapes(rows))
        if outer == 4:
            own = fold("float", *own, parts.pop(0), float_shapes(rows))
    else:
        own_plan = [(0, "float", 1, 0, rows)]
        packed, *own = attend(
            0, [1, 2, 3], whole_plan + own_plan, [packed_shape(stage_rows)] + float_shapes(rows)
        )
        send(0, packed)
    groups = [(slice(0, rows), [(at, 0) for at in range(len(parts))])]
    merged = pl.pallas_call(
        functools.partial(merge_kernel, groups),
        in_specs=[vmem] * (2 + len(parts)),
        out_specs=vmem,
        out_shape=jax.ShapeDtypeStruct((rows, head_width), jnp.bfloat16),
        compiler_params=params,
        name="merge",
    )(*own, *parts)
    return merged.reshape(own_tokens, head_count, head_width)


def solution(mesh):
    in_specs = (P("ctx", "kvh", None), P("ctx", "kvh"), P("ctx", "kvh"), P(), P())
    out_specs = P("ctx", "kvh", None)
    size = mesh.shape["ctx"]

    def body(*args):
        return local(size, *args)

    return jax.shard_map(body, mesh=mesh, in_specs=in_specs, out_specs=out_specs, check_vma=False)
```

```python
import functools

import jax
import jax.numpy as jnp
from jax import lax
from jax.experimental import pallas as pl
from jax.experimental.pallas import tpu as pltpu
from jax.sharding import PartitionSpec as P


masked_floor = -1e30
log2_e = 1.4426950408889634
inner = 4
extra_rows = 16
tail_rows = 8
code_span = 240.0
code_low = -120.0


def split_query(query, scale):
    scaled = query.astype(jnp.float32) * scale
    high = scaled.astype(jnp.bfloat16)
    low = (scaled - high.astype(jnp.float32)).astype(jnp.bfloat16)
    return jnp.concatenate([high, low], axis=1)


def transpose_values(values, values_ref):
    for b, value in enumerate(values):
        shard_keys, width = value.shape
        values_ref[b, :width, :] = value[...].T
        values_ref[b, width:, :] = jnp.ones((extra_rows, shard_keys), jnp.bfloat16)


def score_chunk(key, query_pair, limit, start, scores_ref, slot):
    chunk, tile = key.shape[0], query_pair.shape[0]
    scores = lax.dot_general(
        jnp.concatenate([key, key], axis=1), query_pair, (((1,), (1,)), ((), ())), preferred_element_type=jnp.float32
    ).reshape(chunk // 8, 8, tile)
    position = lax.broadcasted_iota(jnp.int32, scores.shape, 0) * 8 + start
    sublane = lax.broadcasted_iota(jnp.int32, (8, tile), 0)
    scores = jnp.where(position <= (limit - sublane)[None], scores, masked_floor)
    scores_ref[slot, start : start + chunk, :] = scores.reshape(chunk, tile)
    return jnp.max(scores, axis=0)


def add_block(state, values_t, weights, shard_max):
    width = values_t.shape[0] - extra_rows
    sums = lax.dot_general(values_t, weights, (((1,), (0,)), ((), ())), preferred_element_type=jnp.float32)
    num, den = sums[:width], sums[width : width + 1]
    if state is None:
        return shard_max, den, num
    top, run_den, run_num = state
    new_top = jnp.maximum(top, shard_max)
    keep, fresh = jnp.exp2(top - new_top), jnp.exp2(shard_max - new_top)
    return new_top, run_den * keep + den * fresh, run_num * keep + num * fresh


def sweep_tiles(rows, tile, query_pair, keys, limits, scores_ref, put_weights, finish):
    shard_keys = keys[0].shape[0]
    chunk = min(512, shard_keys)
    chunks = shard_keys // chunk
    tiles = [(b, h) for b in range(len(keys)) for h in range(rows // tile)]
    count = len(tiles)
    running, tops = [None] * count, [None] * count
    for step in range(count + 2):
        for c in range(chunks):
            span = slice(c * chunk, (c + 1) * chunk)
            if step < count:
                b, h = tiles[step]
                lanes = slice(h * tile, (h + 1) * tile)
                peak = score_chunk(
                    keys[b][span, :], query_pair[lanes], limits[b][:, lanes], c * chunk, scores_ref, step % 2
                )
                running[step] = peak if c == 0 else jnp.maximum(running[step], peak)
            if 1 <= step <= count:
                t = step - 1
                if c == 0:
                    tops[t] = jnp.max(running[t], axis=0, keepdims=True)
                put_weights(t, *tiles[t], span, jnp.exp2(scores_ref[t % 2, span, :] - tops[t]).astype(jnp.bfloat16))
            if step >= 2 and c == min(1, chunks - 1):
                finish(step - 2, *tiles[step - 2], tops[step - 2])


def attend_tiles(scale, query, keys, values, limits, states, scores_ref, weights_ref, values_ref):
    states = list(states)
    query_pair = split_query(query, scale)
    transpose_values(values, values_ref)

    def put_weights(t, b, h, span, weights):
        weights_ref[t % 2, span, :] = weights

    def finish(t, b, h, shard_max):
        states[h] = add_block(states[h], values_ref[b], weights_ref[t % 2], shard_max)

    sweep_tiles(query.shape[0], scores_ref.shape[2], query_pair, keys, limits, scores_ref, put_weights, finish)
    return states


def weigh_kernel(scale, index, blocks, limits_ref, q_ref, *refs):
    me = lax.axis_index("ctx")
    count = len(blocks)
    keys, weights, tops, scores_ref = refs[:count], refs[count : 2 * count], refs[2 * count : 3 * count], refs[-1]
    tile = scores_ref.shape[2]
    limits = [limits_ref[index : index + 1, :] - (me ^ b) * keys[0].shape[0] for b in blocks]

    def put_weights(t, b, h, span, value):
        weights[b][span, h * tile : (h + 1) * tile] = value

    def finish(t, b, h, shard_max):
        tops[b][:, h * tile : (h + 1) * tile] = shard_max

    query_pair = split_query(q_ref[...], scale)
    sweep_tiles(q_ref.shape[0], tile, query_pair, keys, limits, scores_ref, put_weights, finish)


def finish_kernel(count, plan, *refs):
    values, weights, tops = refs[:count], refs[count : 2 * count], refs[2 * count : 3 * count]
    state_refs, outs, values_ref = refs[3 * count : 3 * count + 3], refs[3 * count + 3 : -1], refs[-1]
    transpose_values(values, values_ref)
    if plan is None:
        state = tuple(ref[...] for ref in state_refs)
        for b in range(count):
            state = add_block(state, values_ref[b], weights[b][...], tops[b][...])
        for ref, value in zip(outs, state):
            ref[...] = value
        return
    for at, form, out, offset, lanes in plan:
        span = slice(at * lanes, (at + 1) * lanes)
        state = tuple(ref[:, span] for ref in state_refs)
        for b in range(count):
            state = add_block(state, values_ref[b], weights[b][:, span], tops[b][:, span])
        top, den, num = state
        write_partial(outs[out:], form, slice(offset, offset + lanes), num * (1.0 / den), top + jnp.log2(den))


def encode(values, level):
    _, lanes = values.shape
    size = jnp.abs(values)
    peak = jnp.maximum(jnp.max(size, axis=0, keepdims=True), 1e-30).astype(jnp.bfloat16).astype(jnp.float32)
    code = jnp.exp2(size * (code_span / peak) + code_low)
    code = jnp.where(values < 0, -code, code)
    high = level.astype(jnp.bfloat16).astype(jnp.float32)
    rest = level - high
    middle = rest.astype(jnp.bfloat16).astype(jnp.float32)
    row = lax.broadcasted_iota(jnp.int32, (tail_rows, lanes), 0)
    tail = jnp.where(row == 0, high, jnp.where(row == 1, middle, jnp.where(row == 2, rest - middle, peak)))
    return code.astype(jnp.bfloat16), tail.astype(jnp.bfloat16)


def decode(codes, tail):
    codes, tail = codes.astype(jnp.float32), tail.astype(jnp.float32)
    level = tail[0:1] + tail[1:2] + tail[2:3]
    size = (jnp.log2(jnp.abs(codes)) - code_low) * (tail[3:4] * (1.0 / code_span))
    return jnp.where(codes < 0, -size, size), level


def spread_limits(me, own_tokens, head_count, offsets_ref, span_ref, limits_ref):
    count, lanes = limits_ref.shape
    width = offsets_ref.shape[1]
    per_row = width // own_tokens
    parts = []
    for k in range(count):
        device = me ^ (k * inner)
        row = offsets_ref[pl.ds(device // per_row, 1), :]
        row = pltpu.roll(row, (width - (device % per_row) * own_tokens) % width, 1)
        parts += [row >> 8, row & 255]
    parts = jnp.concatenate(parts, axis=0).astype(jnp.float32).astype(jnp.bfloat16)
    token = lax.broadcasted_iota(jnp.int32, (width, lanes), 0)
    lane = lax.broadcasted_iota(jnp.int32, (width, lanes), 1)
    first = token * head_count
    spread = jnp.where((lane >= first) & (lane < first + head_count), 1.0, 0.0).astype(jnp.bfloat16)
    wide = lax.dot_general(parts, spread, (((1,), (0,)), ((), ())), preferred_element_type=jnp.float32)
    wide = wide.astype(jnp.int32)
    for k in range(count):
        limits_ref[k : k + 1, :] = wide[2 * k : 2 * k + 1] * 256 + wide[2 * k + 1 : 2 * k + 2] + span_ref[...]


def attend_kernel(scale, index, blocks, has_state, plan, setup, *refs):
    me = lax.axis_index("ctx")
    refs = list(refs)
    if setup:
        offsets_ref, span_ref, q_hbm, k_hbm, v_hbm = refs[:5]
        arrived, q_ref = refs.pop(), refs.pop()
        scratch = [refs.pop() for _ in range(3)][::-1]
        v_ref, k_ref, limits_ref = refs.pop(), refs.pop(), refs.pop()
        pairs = ((q_hbm, q_ref), (k_hbm, k_ref), (v_hbm, v_ref))
        copies = [pltpu.make_async_copy(*pair, arrived.at[at]) for at, pair in enumerate(pairs)]
        for copy in copies:
            copy.start()
        spread_limits(me, *setup, offsets_ref, span_ref, limits_ref)
        for copy in copies:
            copy.wait()
        refs = [limits_ref, q_ref, k_ref, v_ref] + refs[5:]
    else:
        scratch = [refs.pop() for _ in range(3)][::-1]
        limits_ref, q_ref = refs[:2]
    keys = refs[2 : 2 + 2 * len(blocks) : 2]
    values = refs[3 : 3 + 2 * len(blocks) : 2]
    rest = list(refs[2 + 2 * len(blocks) :])
    rows, _ = q_ref.shape
    tile = scratch[0].shape[2]
    spans = [slice(at, at + tile) for at in range(0, rows, tile)]
    states = [None] * len(spans)
    if has_state:
        states = [tuple(ref[:, span] for ref in rest[:3]) for span in spans]
        rest = rest[3:]
    limits = [limits_ref[index : index + 1, :] - (me ^ b) * keys[0].shape[0] for b in blocks]
    states = attend_tiles(scale, q_ref[...], keys, values, limits, states, *scratch)
    if plan is None:
        for span, state in zip(spans, states):
            for ref, value in zip(rest, state):
                ref[:, span] = value
        return
    for at, form, out, offset, count in plan:
        top, den, num = (value[:, :count] for value in states[at])
        write_partial(rest[out:], form, slice(offset, offset + count), num * (1.0 / den), top + jnp.log2(den))


def write_partial(refs, form, span, value, level):
    width = value.shape[0]
    if form == "float":
        refs[0][:, span] = value
        refs[1][:, span] = level
    else:
        code, tail = encode(value, level)
        refs[0][:width, span] = code
        refs[0][width:, span] = tail


def combine(values, levels):
    top = functools.reduce(jnp.maximum, levels)
    factors = [jnp.exp2(level - top) for level in levels]
    total = functools.reduce(jnp.add, factors)
    inverse = 1.0 / total
    value = functools.reduce(jnp.add, [value * (factor * inverse) for value, factor in zip(values, factors)])
    return value, top + jnp.log2(total)


def combine_kernel(form, value_ref, level_ref, part_ref, *out_refs):
    width, lanes = value_ref.shape
    value, level = decode(part_ref[:width, :], part_ref[width:, :])
    value, level = combine([value_ref[...], value], [level_ref[...], level])
    write_partial(out_refs, form, slice(0, lanes), value, level)


def merge_kernel(groups, *refs):
    own_ref, own_level_ref = refs[:2]
    parts, out_ref = refs[2:-1], refs[-1]
    width = own_ref.shape[0]
    for span, members in groups:
        values, levels = [own_ref[:, span]], [own_level_ref[:, span]]
        for at, offset in members:
            lanes = slice(offset, offset + span.stop - span.start)
            value, level = decode(parts[at][:width, lanes], parts[at][width:, lanes])
            values.append(value)
            levels.append(level)
        out_ref[span, :] = combine(values, levels)[0].T.astype(out_ref.dtype)


def local(size, queries, cache_keys, cache_values, span_offset, positions):
    own_tokens, head_count, head_width = queries.shape
    shard_keys = cache_keys.shape[0]
    outer = size // inner
    rows = own_tokens * head_count
    me = lax.axis_index("ctx")
    place, owner = me % inner, me // inner
    scale = head_width ** (-0.5) * log2_e

    def swap(array, step):
        return lax.ppermute(array, "ctx", [(i, i ^ step) for i in range(size)])

    query = queries.reshape(rows, head_width)
    per_stage = max(outer // 4, 1)
    stages = [list(range(s, s + per_stage)) for s in range(0, outer, per_stage)]
    last = len(stages) - 1

    far_pair = [swap(cache_keys, 2), swap(cache_values, 2)]
    near_pair = [swap(cache_keys, 1), swap(cache_values, 1)]
    got = [query] + [None] * (outer - 1)

    def gather(index):
        for k in stages[index]:
            if k:
                low = k if outer == 4 else k & -k
                got[k] = swap(got[k ^ low], inner * low)

    stage_rows = rows * per_stage
    tile = 256 if stage_rows % 256 == 0 else stage_rows

    fused_setup = per_stage == 1 and positions.shape[0] % 128 == 0 and 128 % own_tokens == 0
    if fused_setup:
        chain = [None]
    else:
        limits = (span_offset[0] + positions).reshape(outer, inner, own_tokens)
        limits = lax.dynamic_index_in_dim(limits, place, 1, keepdims=False)
        limits = [lax.dynamic_slice_in_dim(limits, owner ^ k, 1, axis=0) for k in range(outer)]
        limits = jnp.repeat(jnp.concatenate(limits, axis=0), head_count, axis=1)
        chain = [limits.reshape(len(stages), stage_rows)]

    def join(items, axis):
        return items[0] if len(items) == 1 else jnp.concatenate(items, axis=axis)

    vmem = pl.BlockSpec(memory_space=pltpu.VMEM)
    params = pltpu.CompilerParams(vmem_limit_bytes=20 << 20)
    pairs = [[cache_keys, cache_values], near_pair]
    stat = jax.ShapeDtypeStruct((1, stage_rows), jnp.float32)
    state_shapes = [stat, stat, jax.ShapeDtypeStruct((head_width, stage_rows), jnp.float32)]

    def packed_shape(lanes):
        return jax.ShapeDtypeStruct((head_width + tail_rows, lanes), jnp.bfloat16)

    def float_shapes(lanes):
        return [jax.ShapeDtypeStruct((size_of, lanes), jnp.float32) for size_of in (head_width, 1)]

    tiles = range(stage_rows // tile)
    whole_plan = [(at, "code", 0, at * tile, tile) for at in tiles]
    states = [None] * len(stages)

    def attend(index, blocks, plan=None, shapes=state_shapes):
        setup = None
        if chain[0] is None:
            setup = (own_tokens, head_count)
            shapes = shapes + [jax.ShapeDtypeStruct((len(stages), stage_rows), jnp.int32)]
            shapes += [jax.ShapeDtypeStruct(array.shape, array.dtype) for array in pairs[0]]
            own = [pltpu.with_memory_space_constraint(array, pltpu.HBM) for array in (query, *pairs[0])]
            operands = [positions.reshape(-1, 128), span_offset.reshape(1, 1)] + own
            specs = [vmem] * 2 + [pl.BlockSpec(memory_space=pltpu.HBM)] * 3
            extra = [pltpu.VMEM(query.shape, query.dtype), pltpu.SemaphoreType.DMA((3,))]
            operands += [array for b in blocks[1:] for array in pairs[b]]
        else:
            operands = [chain[0], stage_query[index]] + [array for b in blocks for array in pairs[b]]
            operands += list(states[index] or ())
            specs, extra = [], []
        results = pl.pallas_call(
            functools.partial(
                attend_kernel, scale, index, blocks, states[index] is not None, plan, setup
            ),
            in_specs=specs + [vmem] * (len(operands) - len(specs)),
            out_specs=[vmem] * len(shapes),
            out_shape=shapes,
            scratch_shapes=[
                pltpu.VMEM((2, shard_keys, tile), jnp.float32),
                pltpu.VMEM((2, shard_keys, tile), jnp.bfloat16),
                pltpu.VMEM((len(blocks), head_width + extra_rows, shard_keys), jnp.bfloat16),
            ]
            + extra,
            compiler_params=params,
        )(*operands)
        if setup:
            chain[0], pairs[0], results = results[-3], list(results[-2:]), results[:-3]
        chain[0], results = lax.optimization_barrier((chain[0], results))
        if plan is None:
            states[index] = results
        return results

    def hold(*arrays):
        chain[0], arrays = lax.optimization_barrier((chain[0], arrays))
        return list(arrays)

    stage_query = [None] * len(stages)

    def ready(index):
        stage_query[index] = join([got[k] for k in stages[index]], 0)

    for index in range(len(stages) if outer == 4 else last):
        gather(index)
        ready(index)
    attend(0, [0])
    for index in range(1, last - 1):
        attend(index, [0, 1])
    if outer != 4:
        source = stages[last][0] ^ (stages[last][0] & -stages[last][0])
        (got[source],) = hold(got[source])
        gather(last)
        ready(last)
    far_pair[0], = hold(far_pair[0])
    across_keys = swap(far_pair[0], 1)
    attend(last - 1, [0, 1])
    ahead = stage_query[last - 1]
    block = jax.ShapeDtypeStruct((shard_keys, stage_rows), jnp.bfloat16)
    weighed = pl.pallas_call(
        functools.partial(weigh_kernel, scale, last - 1, [2, 3]),
        in_specs=[vmem] * 4,
        out_specs=[vmem] * 4,
        out_shape=[block, block, stat, stat],
        scratch_shapes=[pltpu.VMEM((2, shard_keys, tile), jnp.float32)],
        compiler_params=params,
        name="weigh",
    )(chain[0], ahead, far_pair[0], across_keys)
    weighed = hold(*weighed)
    far_pair[1], = hold(far_pair[1])
    across_values = swap(far_pair[1], 1)
    pairs += [far_pair, [across_keys, across_values]]

    def finish(values, weights, top, plan, shapes):
        results = pl.pallas_call(
            functools.partial(finish_kernel, 1, plan),
            in_specs=[vmem] * 6,
            out_specs=[vmem] * len(shapes),
            out_shape=shapes,
            scratch_shapes=[pltpu.VMEM((1, head_width + extra_rows, shard_keys), jnp.bfloat16)],
            compiler_params=params,
        )(values, weights, top, *states[last - 1])
        return hold(*results)

    states[last - 1] = finish(far_pair[1], weighed[0], weighed[2], None, state_shapes)
    if outer == 4:
        attend(1, [2])
    (across_values,) = hold(across_values)
    pairs[3] = [across_keys, across_values]
    (packed,) = finish(across_values, weighed[1], weighed[3], whole_plan, [packed_shape(stage_rows)])
    own_plan = [(at, "float", 0, at * tile, tile) for at in tiles]
    parts = []

    def send(index, packed):
        for at, k in enumerate(stages[index]):
            if k:
                piece = packed if per_stage == 1 else packed[:, at * rows : (at + 1) * rows]
                parts.append(swap(piece, inner * k))

    coded = [packed_shape(stage_rows)]

    def fold(form, value, level, part, shapes):
        return pl.pallas_call(
            functools.partial(combine_kernel, form),
            in_specs=[vmem] * 3,
            out_specs=[vmem] * len(shapes),
            out_shape=shapes,
            compiler_params=params,
        )(value, level, part)

    if outer == 4:
        handed = swap(packed, inner)
        (packed,) = attend(1, [3], whole_plan, coded)
        parts.append(swap(packed, inner))
        value, level = attend(3, [0, 1, 2, 3], own_plan, float_shapes(stage_rows))
        (handed,) = hold(handed)
        (joined,) = fold("code", value, level, handed, coded)
        (joined,) = hold(joined)
        parts.append(swap(joined, 3 * inner))
    else:
        send(last - 1, packed)
        send(last, attend(last, [0, 1, 2, 3], whole_plan, coded)[0])
        for index in range(last - 2, 0, -1):
            send(index, attend(index, [2, 3], whole_plan, coded)[0])
    if per_stage == 1:
        own = attend(0, [1, 2, 3], own_plan, float_shapes(rows))
        if outer == 4:
            own = fold("float", *own, parts.pop(0), float_shapes(rows))
    else:
        own_plan = [(0, "float", 1, 0, rows)]
        packed, *own = attend(
            0, [1, 2, 3], whole_plan + own_plan, [packed_shape(stage_rows)] + float_shapes(rows)
        )
        send(0, packed)
    groups = [(slice(0, rows), [(at, 0) for at in range(len(parts))])]
    merged = pl.pallas_call(
        functools.partial(merge_kernel, groups),
        in_specs=[vmem] * (2 + len(parts)),
        out_specs=vmem,
        out_shape=jax.ShapeDtypeStruct((rows, head_width), jnp.bfloat16),
        compiler_params=params,
        name="merge",
    )(*own, *parts)
    return merged.reshape(own_tokens, head_count, head_width)


def solution(mesh):
    in_specs = (P("ctx", "kvh", None), P("ctx", "kvh"), P("ctx", "kvh"), P(), P())
    out_specs = P("ctx", "kvh", None)
    size = mesh.shape["ctx"]

    def body(*args):
        return local(size, *args)

    return jax.shard_map(body, mesh=mesh, in_specs=in_specs, out_specs=out_specs, check_vma=False)
```

```python
import functools

import jax
import jax.numpy as jnp
from jax import lax
from jax.experimental import pallas as pl
from jax.experimental.pallas import tpu as pltpu
from jax.sharding import PartitionSpec as P


masked_floor = -1e30
log2_e = 1.4426950408889634
inner = 4
extra_rows = 16
tail_rows = 8
code_span = 240.0
code_low = -120.0


def split_query(query, scale):
    scaled = query.astype(jnp.float32) * scale
    high = scaled.astype(jnp.bfloat16)
    low = (scaled - high.astype(jnp.float32)).astype(jnp.bfloat16)
    return jnp.concatenate([high, low], axis=1)


def transpose_values(values, values_ref):
    for b, value in enumerate(values):
        shard_keys, width = value.shape
        values_ref[b, :width, :] = value[...].T
        values_ref[b, width:, :] = jnp.ones((extra_rows, shard_keys), jnp.bfloat16)


def score_chunk(key, query_pair, limit, start, scores_ref, slot):
    chunk, tile = key.shape[0], query_pair.shape[0]
    scores = lax.dot_general(
        jnp.concatenate([key, key], axis=1), query_pair, (((1,), (1,)), ((), ())), preferred_element_type=jnp.float32
    ).reshape(chunk // 8, 8, tile)
    position = lax.broadcasted_iota(jnp.int32, scores.shape, 0) * 8 + start
    sublane = lax.broadcasted_iota(jnp.int32, (8, tile), 0)
    scores = jnp.where(position <= (limit - sublane)[None], scores, masked_floor)
    scores_ref[slot, start : start + chunk, :] = scores.reshape(chunk, tile)
    return jnp.max(scores, axis=0)


def add_block(state, values_t, weights, shard_max):
    width = values_t.shape[0] - extra_rows
    sums = lax.dot_general(values_t, weights, (((1,), (0,)), ((), ())), preferred_element_type=jnp.float32)
    num, den = sums[:width], sums[width : width + 1]
    if state is None:
        return shard_max, den, num
    top, run_den, run_num = state
    new_top = jnp.maximum(top, shard_max)
    keep, fresh = jnp.exp2(top - new_top), jnp.exp2(shard_max - new_top)
    return new_top, run_den * keep + den * fresh, run_num * keep + num * fresh


def sweep_tiles(rows, tile, query_pair, keys, limits, scores_ref, put_weights, finish):
    shard_keys = keys[0].shape[0]
    chunk = min(512, shard_keys)
    chunks = shard_keys // chunk
    tiles = [(b, h) for b in range(len(keys)) for h in range(rows // tile)]
    count = len(tiles)
    running, tops = [None] * count, [None] * count
    for step in range(count + 2):
        for c in range(chunks):
            span = slice(c * chunk, (c + 1) * chunk)
            if step < count:
                b, h = tiles[step]
                lanes = slice(h * tile, (h + 1) * tile)
                peak = score_chunk(
                    keys[b][span, :], query_pair[lanes], limits[b][:, lanes], c * chunk, scores_ref, step % 2
                )
                running[step] = peak if c == 0 else jnp.maximum(running[step], peak)
            if 1 <= step <= count:
                t = step - 1
                if c == 0:
                    tops[t] = jnp.max(running[t], axis=0, keepdims=True)
                put_weights(t, *tiles[t], span, jnp.exp2(scores_ref[t % 2, span, :] - tops[t]).astype(jnp.bfloat16))
            if step >= 2 and c == min(1, chunks - 1):
                finish(step - 2, *tiles[step - 2], tops[step - 2])


def attend_tiles(scale, query, keys, values, limits, states, scores_ref, weights_ref, values_ref):
    states = list(states)
    query_pair = split_query(query, scale)
    transpose_values(values, values_ref)

    def put_weights(t, b, h, span, weights):
        weights_ref[t % 2, span, :] = weights

    def finish(t, b, h, shard_max):
        states[h] = add_block(states[h], values_ref[b], weights_ref[t % 2], shard_max)

    sweep_tiles(query.shape[0], scores_ref.shape[2], query_pair, keys, limits, scores_ref, put_weights, finish)
    return states


def weigh_kernel(scale, index, blocks, limits_ref, q_ref, *refs):
    me = lax.axis_index("ctx")
    count = len(blocks)
    keys, weights, tops, scores_ref = refs[:count], refs[count : 2 * count], refs[2 * count : 3 * count], refs[-1]
    tile = scores_ref.shape[2]
    limits = [limits_ref[index : index + 1, :] - (me ^ b) * keys[0].shape[0] for b in blocks]

    def put_weights(t, b, h, span, value):
        weights[b][span, h * tile : (h + 1) * tile] = value

    def finish(t, b, h, shard_max):
        tops[b][:, h * tile : (h + 1) * tile] = shard_max

    query_pair = split_query(q_ref[...], scale)
    sweep_tiles(q_ref.shape[0], tile, query_pair, keys, limits, scores_ref, put_weights, finish)


def finish_kernel(count, plan, *refs):
    values, weights, tops = refs[:count], refs[count : 2 * count], refs[2 * count : 3 * count]
    state_refs, outs, values_ref = refs[3 * count : 3 * count + 3], refs[3 * count + 3 : -1], refs[-1]
    transpose_values(values, values_ref)
    if plan is None:
        state = tuple(ref[...] for ref in state_refs)
        for b in range(count):
            state = add_block(state, values_ref[b], weights[b][...], tops[b][...])
        for ref, value in zip(outs, state):
            ref[...] = value
        return
    for at, form, out, offset, lanes in plan:
        span = slice(at * lanes, (at + 1) * lanes)
        state = tuple(ref[:, span] for ref in state_refs)
        for b in range(count):
            state = add_block(state, values_ref[b], weights[b][:, span], tops[b][:, span])
        top, den, num = state
        write_partial(outs[out:], form, slice(offset, offset + lanes), num * (1.0 / den), top + jnp.log2(den))


def encode(values, level):
    _, lanes = values.shape
    size = jnp.abs(values)
    peak = jnp.maximum(jnp.max(size, axis=0, keepdims=True), 1e-30).astype(jnp.bfloat16).astype(jnp.float32)
    code = jnp.exp2(size * (code_span / peak) + code_low)
    code = jnp.where(values < 0, -code, code)
    high = level.astype(jnp.bfloat16).astype(jnp.float32)
    rest = level - high
    middle = rest.astype(jnp.bfloat16).astype(jnp.float32)
    row = lax.broadcasted_iota(jnp.int32, (tail_rows, lanes), 0)
    tail = jnp.where(row == 0, high, jnp.where(row == 1, middle, jnp.where(row == 2, rest - middle, peak)))
    return code.astype(jnp.bfloat16), tail.astype(jnp.bfloat16)


def decode(codes, tail):
    codes, tail = codes.astype(jnp.float32), tail.astype(jnp.float32)
    level = tail[0:1] + tail[1:2] + tail[2:3]
    size = (jnp.log2(jnp.abs(codes)) - code_low) * (tail[3:4] * (1.0 / code_span))
    return jnp.where(codes < 0, -size, size), level


def spread_limits(me, own_tokens, head_count, offsets_ref, span_ref, limits_ref):
    count, lanes = limits_ref.shape
    width = offsets_ref.shape[1]
    per_row = width // own_tokens
    parts = []
    for k in range(count):
        device = me ^ (k * inner)
        row = offsets_ref[pl.ds(device // per_row, 1), :]
        row = pltpu.roll(row, (width - (device % per_row) * own_tokens) % width, 1)
        parts += [row >> 8, row & 255]
    parts = jnp.concatenate(parts, axis=0).astype(jnp.float32).astype(jnp.bfloat16)
    token = lax.broadcasted_iota(jnp.int32, (width, lanes), 0)
    lane = lax.broadcasted_iota(jnp.int32, (width, lanes), 1)
    first = token * head_count
    spread = jnp.where((lane >= first) & (lane < first + head_count), 1.0, 0.0).astype(jnp.bfloat16)
    wide = lax.dot_general(parts, spread, (((1,), (0,)), ((), ())), preferred_element_type=jnp.float32)
    wide = wide.astype(jnp.int32)
    for k in range(count):
        limits_ref[k : k + 1, :] = wide[2 * k : 2 * k + 1] * 256 + wide[2 * k + 1 : 2 * k + 2] + span_ref[...]


def attend_kernel(scale, index, blocks, has_state, plan, setup, *refs):
    me = lax.axis_index("ctx")
    refs = list(refs)
    if setup:
        offsets_ref, span_ref, q_hbm, k_hbm, v_hbm = refs[:5]
        arrived, q_ref = refs.pop(), refs.pop()
        scratch = [refs.pop() for _ in range(3)][::-1]
        v_ref, k_ref, limits_ref = refs.pop(), refs.pop(), refs.pop()
        pairs = ((q_hbm, q_ref), (k_hbm, k_ref), (v_hbm, v_ref))
        copies = [pltpu.make_async_copy(*pair, arrived.at[at]) for at, pair in enumerate(pairs)]
        for copy in copies:
            copy.start()
        spread_limits(me, *setup, offsets_ref, span_ref, limits_ref)
        for copy in copies:
            copy.wait()
        refs = [limits_ref, q_ref, k_ref, v_ref] + refs[5:]
    else:
        scratch = [refs.pop() for _ in range(3)][::-1]
        limits_ref, q_ref = refs[:2]
    keys = refs[2 : 2 + 2 * len(blocks) : 2]
    values = refs[3 : 3 + 2 * len(blocks) : 2]
    rest = list(refs[2 + 2 * len(blocks) :])
    rows, _ = q_ref.shape
    tile = scratch[0].shape[2]
    spans = [slice(at, at + tile) for at in range(0, rows, tile)]
    states = [None] * len(spans)
    if has_state:
        states = [tuple(ref[:, span] for ref in rest[:3]) for span in spans]
        rest = rest[3:]
    limits = [limits_ref[index : index + 1, :] - (me ^ b) * keys[0].shape[0] for b in blocks]
    states = attend_tiles(scale, q_ref[...], keys, values, limits, states, *scratch)
    if plan is None:
        for span, state in zip(spans, states):
            for ref, value in zip(rest, state):
                ref[:, span] = value
        return
    for at, form, out, offset, count in plan:
        top, den, num = (value[:, :count] for value in states[at])
        write_partial(rest[out:], form, slice(offset, offset + count), num * (1.0 / den), top + jnp.log2(den))


def write_partial(refs, form, span, value, level):
    width = value.shape[0]
    if form == "float":
        refs[0][:, span] = value
        refs[1][:, span] = level
    else:
        code, tail = encode(value, level)
        refs[0][:width, span] = code
        refs[0][width:, span] = tail


def combine(values, levels):
    top = functools.reduce(jnp.maximum, levels)
    factors = [jnp.exp2(level - top) for level in levels]
    total = functools.reduce(jnp.add, factors)
    inverse = 1.0 / total
    value = functools.reduce(jnp.add, [value * (factor * inverse) for value, factor in zip(values, factors)])
    return value, top + jnp.log2(total)


def combine_kernel(form, value_ref, level_ref, part_ref, *out_refs):
    width, lanes = value_ref.shape
    value, level = decode(part_ref[:width, :], part_ref[width:, :])
    value, level = combine([value_ref[...], value], [level_ref[...], level])
    write_partial(out_refs, form, slice(0, lanes), value, level)


def merge_kernel(groups, *refs):
    own_ref, own_level_ref = refs[:2]
    parts, out_ref = refs[2:-1], refs[-1]
    width = own_ref.shape[0]
    for span, members in groups:
        values, levels = [own_ref[:, span]], [own_level_ref[:, span]]
        for at, offset in members:
            lanes = slice(offset, offset + span.stop - span.start)
            value, level = decode(parts[at][:width, lanes], parts[at][width:, lanes])
            values.append(value)
            levels.append(level)
        out_ref[span, :] = combine(values, levels)[0].T.astype(out_ref.dtype)


def local(size, queries, cache_keys, cache_values, span_offset, positions):
    own_tokens, head_count, head_width = queries.shape
    shard_keys = cache_keys.shape[0]
    outer = size // inner
    rows = own_tokens * head_count
    me = lax.axis_index("ctx")
    place, owner = me % inner, me // inner
    scale = head_width ** (-0.5) * log2_e

    def swap(array, step):
        return lax.ppermute(array, "ctx", [(i, i ^ step) for i in range(size)])

    query = queries.reshape(rows, head_width)
    per_stage = max(outer // 4, 1)
    stages = [list(range(s, s + per_stage)) for s in range(0, outer, per_stage)]
    last = len(stages) - 1

    far_pair = [swap(cache_keys, 2), swap(cache_values, 2)]
    near_pair = [swap(cache_keys, 1), swap(cache_values, 1)]
    got = [query] + [None] * (outer - 1)

    def gather(index):
        for k in stages[index]:
            if k:
                low = k & -k
                got[k] = swap(got[k ^ low], inner * low)

    stage_rows = rows * per_stage
    tile = 256 if stage_rows % 256 == 0 else stage_rows

    fused_setup = per_stage == 1 and positions.shape[0] % 128 == 0 and 128 % own_tokens == 0
    if fused_setup:
        chain = [None]
    else:
        limits = (span_offset[0] + positions).reshape(outer, inner, own_tokens)
        limits = lax.dynamic_index_in_dim(limits, place, 1, keepdims=False)
        limits = [lax.dynamic_slice_in_dim(limits, owner ^ k, 1, axis=0) for k in range(outer)]
        limits = jnp.repeat(jnp.concatenate(limits, axis=0), head_count, axis=1)
        chain = [limits.reshape(len(stages), stage_rows)]

    def join(items, axis):
        return items[0] if len(items) == 1 else jnp.concatenate(items, axis=axis)

    vmem = pl.BlockSpec(memory_space=pltpu.VMEM)
    params = pltpu.CompilerParams(vmem_limit_bytes=20 << 20)
    pairs = [[cache_keys, cache_values], near_pair]
    stat = jax.ShapeDtypeStruct((1, stage_rows), jnp.float32)
    state_shapes = [stat, stat, jax.ShapeDtypeStruct((head_width, stage_rows), jnp.float32)]

    def packed_shape(lanes):
        return jax.ShapeDtypeStruct((head_width + tail_rows, lanes), jnp.bfloat16)

    def float_shapes(lanes):
        return [jax.ShapeDtypeStruct((size_of, lanes), jnp.float32) for size_of in (head_width, 1)]

    tiles = range(stage_rows // tile)
    whole_plan = [(at, "code", 0, at * tile, tile) for at in tiles]
    states = [None] * len(stages)

    def attend(index, blocks, plan=None, shapes=state_shapes):
        setup = None
        if chain[0] is None:
            setup = (own_tokens, head_count)
            shapes = shapes + [jax.ShapeDtypeStruct((len(stages), stage_rows), jnp.int32)]
            shapes += [jax.ShapeDtypeStruct(array.shape, array.dtype) for array in pairs[0]]
            own = [pltpu.with_memory_space_constraint(array, pltpu.HBM) for array in (query, *pairs[0])]
            operands = [positions.reshape(-1, 128), span_offset.reshape(1, 1)] + own
            specs = [vmem] * 2 + [pl.BlockSpec(memory_space=pltpu.HBM)] * 3
            extra = [pltpu.VMEM(query.shape, query.dtype), pltpu.SemaphoreType.DMA((3,))]
            operands += [array for b in blocks[1:] for array in pairs[b]]
        else:
            operands = [chain[0], stage_query[index]] + [array for b in blocks for array in pairs[b]]
            operands += list(states[index] or ())
            specs, extra = [], []
        results = pl.pallas_call(
            functools.partial(
                attend_kernel, scale, index, blocks, states[index] is not None, plan, setup
            ),
            in_specs=specs + [vmem] * (len(operands) - len(specs)),
            out_specs=[vmem] * len(shapes),
            out_shape=shapes,
            scratch_shapes=[
                pltpu.VMEM((2, shard_keys, tile), jnp.float32),
                pltpu.VMEM((2, shard_keys, tile), jnp.bfloat16),
                pltpu.VMEM((len(blocks), head_width + extra_rows, shard_keys), jnp.bfloat16),
            ]
            + extra,
            compiler_params=params,
        )(*operands)
        if setup:
            chain[0], pairs[0], results = results[-3], list(results[-2:]), results[:-3]
        chain[0], results = lax.optimization_barrier((chain[0], results))
        if plan is None:
            states[index] = results
        return results

    def hold(*arrays):
        chain[0], arrays = lax.optimization_barrier((chain[0], arrays))
        return list(arrays)

    stage_query = [None] * len(stages)

    def ready(index):
        stage_query[index] = join([got[k] for k in stages[index]], 0)

    for index in range(len(stages) - 1):
        gather(index)
        ready(index)
    attend(0, [0])
    for index in range(1, last - 1):
        attend(index, [0, 1])
    source = stages[last][0] ^ (stages[last][0] & -stages[last][0])
    (got[source],) = hold(got[source])
    gather(last)
    ready(last)
    far_pair[0], = hold(far_pair[0])
    across_keys = swap(far_pair[0], 1)
    attend(last - 1, [0, 1])
    ahead = stage_query[last - 1]
    block = jax.ShapeDtypeStruct((shard_keys, stage_rows), jnp.bfloat16)

    def weigh(block_index, keys):
        results = pl.pallas_call(
            functools.partial(weigh_kernel, scale, last - 1, [block_index]),
            in_specs=[vmem] * 3,
            out_specs=[vmem] * 2,
            out_shape=[block, stat],
            scratch_shapes=[pltpu.VMEM((2, shard_keys, tile), jnp.float32)],
            compiler_params=params,
        )(chain[0], ahead, keys)
        return hold(*results)

    far_weights = weigh(2, far_pair[0])
    far_pair[1], = hold(far_pair[1])
    across_values = swap(far_pair[1], 1)
    pairs += [far_pair, [across_keys, across_values]]

    def finish(values, weights, top, plan, shapes):
        results = pl.pallas_call(
            functools.partial(finish_kernel, 1, plan),
            in_specs=[vmem] * 6,
            out_specs=[vmem] * len(shapes),
            out_shape=shapes,
            scratch_shapes=[pltpu.VMEM((1, head_width + extra_rows, shard_keys), jnp.bfloat16)],
            compiler_params=params,
        )(values, weights, top, *states[last - 1])
        return hold(*results)

    states[last - 1] = finish(far_pair[1], *far_weights, None, state_shapes)
    across_weights = weigh(3, across_keys)
    (across_values,) = hold(across_values)
    pairs[3] = [across_keys, across_values]
    (packed,) = finish(across_values, *across_weights, whole_plan, [packed_shape(stage_rows)])
    own_plan = [(at, "float", 0, at * tile, tile) for at in tiles]
    parts = []

    def send(index, packed):
        for at, k in enumerate(stages[index]):
            if k:
                piece = packed if per_stage == 1 else packed[:, at * rows : (at + 1) * rows]
                parts.append(swap(piece, inner * k))

    coded = [packed_shape(stage_rows)]

    def fold(form, value, level, part, shapes):
        return pl.pallas_call(
            functools.partial(combine_kernel, form),
            in_specs=[vmem] * 3,
            out_specs=[vmem] * len(shapes),
            out_shape=shapes,
            compiler_params=params,
        )(value, level, part)

    if outer == 4:
        handed = swap(packed, inner)
        (packed,) = attend(1, [2, 3], whole_plan, coded)
        parts.append(swap(packed, inner))
        value, level = attend(3, [0, 1, 2, 3], own_plan, float_shapes(stage_rows))
        (handed,) = hold(handed)
        (joined,) = fold("code", value, level, handed, coded)
        (joined,) = hold(joined)
        parts.append(swap(joined, 3 * inner))
    else:
        send(last - 1, packed)
        send(last, attend(last, [0, 1, 2, 3], whole_plan, coded)[0])
        for index in range(last - 2, 0, -1):
            send(index, attend(index, [2, 3], whole_plan, coded)[0])
    if per_stage == 1:
        own = attend(0, [1, 2, 3], own_plan, float_shapes(rows))
        if outer == 4:
            own = fold("float", *own, parts.pop(0), float_shapes(rows))
    else:
        own_plan = [(0, "float", 1, 0, rows)]
        packed, *own = attend(
            0, [1, 2, 3], whole_plan + own_plan, [packed_shape(stage_rows)] + float_shapes(rows)
        )
        send(0, packed)
    groups = [(slice(0, rows), [(at, 0) for at in range(len(parts))])]
    merged = pl.pallas_call(
        functools.partial(merge_kernel, groups),
        in_specs=[vmem] * (2 + len(parts)),
        out_specs=vmem,
        out_shape=jax.ShapeDtypeStruct((rows, head_width), jnp.bfloat16),
        compiler_params=params,
        name="merge",
    )(*own, *parts)
    return merged.reshape(own_tokens, head_count, head_width)


def solution(mesh):
    in_specs = (P("ctx", "kvh", None), P("ctx", "kvh"), P("ctx", "kvh"), P(), P())
    out_specs = P("ctx", "kvh", None)
    size = mesh.shape["ctx"]

    def body(*args):
        return local(size, *args)

    return jax.shard_map(body, mesh=mesh, in_specs=in_specs, out_specs=out_specs, check_vma=False)
```

```python
import functools

import jax
import jax.numpy as jnp
from jax import lax
from jax.experimental import pallas as pl
from jax.experimental.pallas import tpu as pltpu
from jax.sharding import PartitionSpec as P


masked_floor = -1e30
log2_e = 1.4426950408889634
inner = 4
extra_rows = 16
tail_rows = 8
code_span = 240.0
code_low = -120.0


def split_query(query, scale):
    scaled = query.astype(jnp.float32) * scale
    high = scaled.astype(jnp.bfloat16)
    low = (scaled - high.astype(jnp.float32)).astype(jnp.bfloat16)
    return jnp.concatenate([high, low], axis=1)


def transpose_values(values, values_ref):
    for b, value in enumerate(values):
        shard_keys, width = value.shape
        values_ref[b, :width, :] = value[...].T
        values_ref[b, width:, :] = jnp.ones((extra_rows, shard_keys), jnp.bfloat16)


def score_chunk(key, query_pair, limit, start, scores_ref, slot):
    chunk, tile = key.shape[0], query_pair.shape[0]
    scores = lax.dot_general(
        jnp.concatenate([key, key], axis=1), query_pair, (((1,), (1,)), ((), ())), preferred_element_type=jnp.float32
    ).reshape(chunk // 8, 8, tile)
    position = lax.broadcasted_iota(jnp.int32, scores.shape, 0) * 8 + start
    sublane = lax.broadcasted_iota(jnp.int32, (8, tile), 0)
    scores = jnp.where(position <= (limit - sublane)[None], scores, masked_floor)
    scores_ref[slot, start : start + chunk, :] = scores.reshape(chunk, tile)
    return jnp.max(scores, axis=0)


def add_block(state, values_t, weights, shard_max):
    width = values_t.shape[0] - extra_rows
    sums = lax.dot_general(values_t, weights, (((1,), (0,)), ((), ())), preferred_element_type=jnp.float32)
    num, den = sums[:width], sums[width : width + 1]
    if state is None:
        return shard_max, den, num
    top, run_den, run_num = state
    new_top = jnp.maximum(top, shard_max)
    keep, fresh = jnp.exp2(top - new_top), jnp.exp2(shard_max - new_top)
    return new_top, run_den * keep + den * fresh, run_num * keep + num * fresh


def sweep_tiles(rows, tile, query_pair, keys, limits, scores_ref, put_weights, finish):
    shard_keys = keys[0].shape[0]
    chunk = min(512, shard_keys)
    chunks = shard_keys // chunk
    tiles = [(b, h) for b in range(len(keys)) for h in range(rows // tile)]
    count = len(tiles)
    running, tops = [None] * count, [None] * count
    for step in range(count + 2):
        for c in range(chunks):
            span = slice(c * chunk, (c + 1) * chunk)
            if step < count:
                b, h = tiles[step]
                lanes = slice(h * tile, (h + 1) * tile)
                peak = score_chunk(
                    keys[b][span, :], query_pair[lanes], limits[b][:, lanes], c * chunk, scores_ref, step % 2
                )
                running[step] = peak if c == 0 else jnp.maximum(running[step], peak)
            if 1 <= step <= count:
                t = step - 1
                if c == 0:
                    tops[t] = jnp.max(running[t], axis=0, keepdims=True)
                put_weights(t, *tiles[t], span, jnp.exp2(scores_ref[t % 2, span, :] - tops[t]).astype(jnp.bfloat16))
            if step >= 2 and c == min(1, chunks - 1):
                finish(step - 2, *tiles[step - 2], tops[step - 2])


def attend_tiles(scale, query, keys, values, limits, states, scores_ref, weights_ref, values_ref):
    states = list(states)
    query_pair = split_query(query, scale)
    transpose_values(values, values_ref)

    def put_weights(t, b, h, span, weights):
        weights_ref[t % 2, span, :] = weights

    def finish(t, b, h, shard_max):
        states[h] = add_block(states[h], values_ref[b], weights_ref[t % 2], shard_max)

    sweep_tiles(query.shape[0], scores_ref.shape[2], query_pair, keys, limits, scores_ref, put_weights, finish)
    return states


def weigh_kernel(scale, index, blocks, limits_ref, q_ref, *refs):
    me = lax.axis_index("ctx")
    count = len(blocks)
    keys, weights, tops, scores_ref = refs[:count], refs[count : 2 * count], refs[2 * count : 3 * count], refs[-1]
    tile = scores_ref.shape[2]
    limits = [limits_ref[index : index + 1, :] - (me ^ b) * keys[0].shape[0] for b in blocks]

    def put_weights(t, b, h, span, value):
        weights[b][span, h * tile : (h + 1) * tile] = value

    def finish(t, b, h, shard_max):
        tops[b][:, h * tile : (h + 1) * tile] = shard_max

    query_pair = split_query(q_ref[...], scale)
    sweep_tiles(q_ref.shape[0], tile, query_pair, keys, limits, scores_ref, put_weights, finish)


def finish_kernel(count, plan, *refs):
    values, weights, tops = refs[:count], refs[count : 2 * count], refs[2 * count : 3 * count]
    state_refs, outs, values_ref = refs[3 * count : 3 * count + 3], refs[3 * count + 3 : -1], refs[-1]
    transpose_values(values, values_ref)
    if plan is None:
        state = tuple(ref[...] for ref in state_refs)
        for b in range(count):
            state = add_block(state, values_ref[b], weights[b][...], tops[b][...])
        for ref, value in zip(outs, state):
            ref[...] = value
        return
    for at, form, out, offset, lanes in plan:
        span = slice(at * lanes, (at + 1) * lanes)
        state = tuple(ref[:, span] for ref in state_refs)
        for b in range(count):
            state = add_block(state, values_ref[b], weights[b][:, span], tops[b][:, span])
        top, den, num = state
        write_partial(outs[out:], form, slice(offset, offset + lanes), num * (1.0 / den), top + jnp.log2(den))


def encode(values, level):
    _, lanes = values.shape
    size = jnp.abs(values)
    peak = jnp.maximum(jnp.max(size, axis=0, keepdims=True), 1e-30).astype(jnp.bfloat16).astype(jnp.float32)
    code = jnp.exp2(size * (code_span / peak) + code_low)
    code = jnp.where(values < 0, -code, code)
    high = level.astype(jnp.bfloat16).astype(jnp.float32)
    rest = level - high
    middle = rest.astype(jnp.bfloat16).astype(jnp.float32)
    row = lax.broadcasted_iota(jnp.int32, (tail_rows, lanes), 0)
    tail = jnp.where(row == 0, high, jnp.where(row == 1, middle, jnp.where(row == 2, rest - middle, peak)))
    return code.astype(jnp.bfloat16), tail.astype(jnp.bfloat16)


def decode(codes, tail):
    codes, tail = codes.astype(jnp.float32), tail.astype(jnp.float32)
    level = tail[0:1] + tail[1:2] + tail[2:3]
    size = (jnp.log2(jnp.abs(codes)) - code_low) * (tail[3:4] * (1.0 / code_span))
    return jnp.where(codes < 0, -size, size), level


def spread_limits(me, own_tokens, head_count, offsets_ref, span_ref, limits_ref):
    count, lanes = limits_ref.shape
    width = offsets_ref.shape[1]
    per_row = width // own_tokens
    parts = []
    for k in range(count):
        device = me ^ (k * inner)
        row = offsets_ref[pl.ds(device // per_row, 1), :]
        row = pltpu.roll(row, (width - (device % per_row) * own_tokens) % width, 1)
        parts += [row >> 8, row & 255]
    parts = jnp.concatenate(parts, axis=0).astype(jnp.float32).astype(jnp.bfloat16)
    token = lax.broadcasted_iota(jnp.int32, (width, lanes), 0)
    lane = lax.broadcasted_iota(jnp.int32, (width, lanes), 1)
    first = token * head_count
    spread = jnp.where((lane >= first) & (lane < first + head_count), 1.0, 0.0).astype(jnp.bfloat16)
    wide = lax.dot_general(parts, spread, (((1,), (0,)), ((), ())), preferred_element_type=jnp.float32)
    wide = wide.astype(jnp.int32)
    for k in range(count):
        limits_ref[k : k + 1, :] = wide[2 * k : 2 * k + 1] * 256 + wide[2 * k + 1 : 2 * k + 2] + span_ref[...]


def setup_kernel(own_tokens, head_count, offsets_ref, span_ref, *refs):
    sources, limits_ref, targets, arrived = refs[:3], refs[3], refs[4:7], refs[7]
    copies = [pltpu.make_async_copy(*pair, arrived.at[at]) for at, pair in enumerate(zip(sources, targets))]
    for copy in copies:
        copy.start()
    spread_limits(lax.axis_index("ctx"), own_tokens, head_count, offsets_ref, span_ref, limits_ref)
    for copy in copies:
        copy.wait()


def attend_kernel(scale, index, blocks, has_state, plan, *refs):
    me = lax.axis_index("ctx")
    refs = list(refs)
    scratch = [refs.pop() for _ in range(3)][::-1]
    limits_ref, q_ref = refs[:2]
    keys = refs[2 : 2 + 2 * len(blocks) : 2]
    values = refs[3 : 3 + 2 * len(blocks) : 2]
    rest = list(refs[2 + 2 * len(blocks) :])
    rows, _ = q_ref.shape
    tile = scratch[0].shape[2]
    spans = [slice(at, at + tile) for at in range(0, rows, tile)]
    states = [None] * len(spans)
    if has_state:
        states = [tuple(ref[:, span] for ref in rest[:3]) for span in spans]
        rest = rest[3:]
    limits = [limits_ref[index : index + 1, :] - (me ^ b) * keys[0].shape[0] for b in blocks]
    states = attend_tiles(scale, q_ref[...], keys, values, limits, states, *scratch)
    if plan is None:
        for span, state in zip(spans, states):
            for ref, value in zip(rest, state):
                ref[:, span] = value
        return
    for at, form, out, offset, count in plan:
        top, den, num = (value[:, :count] for value in states[at])
        write_partial(rest[out:], form, slice(offset, offset + count), num * (1.0 / den), top + jnp.log2(den))


def write_partial(refs, form, span, value, level):
    width = value.shape[0]
    if form == "float":
        refs[0][:, span] = value
        refs[1][:, span] = level
    else:
        code, tail = encode(value, level)
        refs[0][:width, span] = code
        refs[0][width:, span] = tail


def combine(values, levels):
    top = functools.reduce(jnp.maximum, levels)
    factors = [jnp.exp2(level - top) for level in levels]
    total = functools.reduce(jnp.add, factors)
    inverse = 1.0 / total
    value = functools.reduce(jnp.add, [value * (factor * inverse) for value, factor in zip(values, factors)])
    return value, top + jnp.log2(total)


def combine_kernel(form, value_ref, level_ref, part_ref, *out_refs):
    width, lanes = value_ref.shape
    value, level = decode(part_ref[:width, :], part_ref[width:, :])
    value, level = combine([value_ref[...], value], [level_ref[...], level])
    write_partial(out_refs, form, slice(0, lanes), value, level)


def merge_kernel(groups, *refs):
    own_ref, own_level_ref = refs[:2]
    parts, out_ref = refs[2:-1], refs[-1]
    width = own_ref.shape[0]
    for span, members in groups:
        values, levels = [own_ref[:, span]], [own_level_ref[:, span]]
        for at, offset in members:
            lanes = slice(offset, offset + span.stop - span.start)
            value, level = decode(parts[at][:width, lanes], parts[at][width:, lanes])
            values.append(value)
            levels.append(level)
        out_ref[span, :] = combine(values, levels)[0].T.astype(out_ref.dtype)


def local(size, queries, cache_keys, cache_values, span_offset, positions):
    own_tokens, head_count, head_width = queries.shape
    shard_keys = cache_keys.shape[0]
    outer = size // inner
    rows = own_tokens * head_count
    me = lax.axis_index("ctx")
    place, owner = me % inner, me // inner
    scale = head_width ** (-0.5) * log2_e

    def swap(array, step):
        return lax.ppermute(array, "ctx", [(i, i ^ step) for i in range(size)])

    query = queries.reshape(rows, head_width)
    per_stage = max(outer // 4, 1)
    stages = [list(range(s, s + per_stage)) for s in range(0, outer, per_stage)]
    last = len(stages) - 1

    far_pair = [swap(cache_keys, 2), swap(cache_values, 2)]
    near_pair = [swap(cache_keys, 1), swap(cache_values, 1)]
    got = [query] + [None] * (outer - 1)

    def gather(index):
        for k in stages[index]:
            if k:
                low = k & -k
                got[k] = swap(got[k ^ low], inner * low)

    stage_rows = rows * per_stage
    tile = 256 if stage_rows % 256 == 0 else stage_rows

    fused_setup = per_stage == 1 and positions.shape[0] % 128 == 0 and 128 % own_tokens == 0
    if fused_setup:
        chain = [None]
    else:
        limits = (span_offset[0] + positions).reshape(outer, inner, own_tokens)
        limits = lax.dynamic_index_in_dim(limits, place, 1, keepdims=False)
        limits = [lax.dynamic_slice_in_dim(limits, owner ^ k, 1, axis=0) for k in range(outer)]
        limits = jnp.repeat(jnp.concatenate(limits, axis=0), head_count, axis=1)
        chain = [limits.reshape(len(stages), stage_rows)]

    def join(items, axis):
        return items[0] if len(items) == 1 else jnp.concatenate(items, axis=axis)

    vmem = pl.BlockSpec(memory_space=pltpu.VMEM)
    params = pltpu.CompilerParams(vmem_limit_bytes=20 << 20)
    pairs = [[cache_keys, cache_values], near_pair]
    stat = jax.ShapeDtypeStruct((1, stage_rows), jnp.float32)
    state_shapes = [stat, stat, jax.ShapeDtypeStruct((head_width, stage_rows), jnp.float32)]

    def packed_shape(lanes):
        return jax.ShapeDtypeStruct((head_width + tail_rows, lanes), jnp.bfloat16)

    def float_shapes(lanes):
        return [jax.ShapeDtypeStruct((size_of, lanes), jnp.float32) for size_of in (head_width, 1)]

    tiles = range(stage_rows // tile)
    whole_plan = [(at, "code", 0, at * tile, tile) for at in tiles]
    states = [None] * len(stages)

    def attend(index, blocks, plan=None, shapes=state_shapes):
        operands = [chain[0], stage_query[index]] + [array for b in blocks for array in pairs[b]]
        operands += list(states[index] or ())
        results = pl.pallas_call(
            functools.partial(
                attend_kernel, scale, index, blocks, states[index] is not None, plan
            ),
            in_specs=[vmem] * len(operands),
            out_specs=[vmem] * len(shapes),
            out_shape=shapes,
            scratch_shapes=[
                pltpu.VMEM((2, shard_keys, tile), jnp.float32),
                pltpu.VMEM((2, shard_keys, tile), jnp.bfloat16),
                pltpu.VMEM((len(blocks), head_width + extra_rows, shard_keys), jnp.bfloat16),
            ],
            compiler_params=params,
        )(*operands)
        chain[0], results = lax.optimization_barrier((chain[0], results))
        if plan is None:
            states[index] = results
        return results

    def hold(*arrays):
        chain[0], arrays = lax.optimization_barrier((chain[0], arrays))
        return list(arrays)

    stage_query = [None] * len(stages)

    def ready(index):
        stage_query[index] = join([got[k] for k in stages[index]], 0)

    for index in range(len(stages) - 1):
        gather(index)
        ready(index)
    if fused_setup:
        own = [pltpu.with_memory_space_constraint(array, pltpu.HBM) for array in (query, *pairs[0])]
        chain[0], stage_query[0], *pairs[0] = pl.pallas_call(
            functools.partial(setup_kernel, own_tokens, head_count),
            in_specs=[vmem] * 2 + [pl.BlockSpec(memory_space=pltpu.HBM)] * 3,
            out_specs=[vmem] * 4,
            out_shape=[jax.ShapeDtypeStruct((len(stages), stage_rows), jnp.int32)]
            + [jax.ShapeDtypeStruct(array.shape, array.dtype) for array in own],
            scratch_shapes=[pltpu.SemaphoreType.DMA((3,))],
            compiler_params=params,
            name="setup",
        )(positions.reshape(-1, 128), span_offset.reshape(1, 1), *own)
    for index in range(1, last - 1):
        attend(index, [0, 1])
    block = jax.ShapeDtypeStruct((shard_keys, stage_rows), jnp.bfloat16)

    def weigh(index, block_index, keys):
        results = pl.pallas_call(
            functools.partial(weigh_kernel, scale, index, [block_index]),
            in_specs=[vmem] * 3,
            out_specs=[vmem] * 2,
            out_shape=[block, stat],
            scratch_shapes=[pltpu.VMEM((2, shard_keys, tile), jnp.float32)],
            compiler_params=params,
        )(chain[0], stage_query[index], keys)
        return hold(*results)

    far_pair[0], = hold(far_pair[0])
    across_keys = swap(far_pair[0], 1)
    if outer == 4:
        first_weights = weigh(1, 2, far_pair[0])
    source = stages[last][0] ^ (stages[last][0] & -stages[last][0])
    (got[source],) = hold(got[source])
    gather(last)
    ready(last)
    attend(last - 1, [0, 1])
    far_weights = weigh(last - 1, 2, far_pair[0])
    far_pair[1], = hold(far_pair[1])
    across_values = swap(far_pair[1], 1)
    pairs += [far_pair, [across_keys, across_values]]

    def finish(index, values, weights, top, plan, shapes):
        results = pl.pallas_call(
            functools.partial(finish_kernel, 1, plan),
            in_specs=[vmem] * 6,
            out_specs=[vmem] * len(shapes),
            out_shape=shapes,
            scratch_shapes=[pltpu.VMEM((1, head_width + extra_rows, shard_keys), jnp.bfloat16)],
            compiler_params=params,
        )(values, weights, top, *states[index])
        return hold(*results)

    states[last - 1] = finish(last - 1, far_pair[1], *far_weights, None, state_shapes)
    across_weights = weigh(last - 1, 3, across_keys)
    (across_values,) = hold(across_values)
    pairs[3] = [across_keys, across_values]
    (packed,) = finish(last - 1, across_values, *across_weights, whole_plan, [packed_shape(stage_rows)])
    own_plan = [(at, "float", 0, at * tile, tile) for at in tiles]
    parts = []

    def send(index, packed):
        for at, k in enumerate(stages[index]):
            if k:
                piece = packed if per_stage == 1 else packed[:, at * rows : (at + 1) * rows]
                parts.append(swap(piece, inner * k))

    coded = [packed_shape(stage_rows)]

    def fold(form, value, level, part, shapes):
        return pl.pallas_call(
            functools.partial(combine_kernel, form),
            in_specs=[vmem] * 3,
            out_specs=[vmem] * len(shapes),
            out_shape=shapes,
            compiler_params=params,
        )(value, level, part)

    if outer == 4:
        handed = swap(packed, inner)
        states[1] = finish(1, far_pair[1], *first_weights, None, state_shapes)
        (packed,) = attend(1, [3], whole_plan, coded)
        parts.append(swap(packed, inner))
        value, level = attend(3, [0, 1, 2, 3], own_plan, float_shapes(stage_rows))
        (handed,) = hold(handed)
        (joined,) = fold("code", value, level, handed, coded)
        (joined,) = hold(joined)
        parts.append(swap(joined, 3 * inner))
    else:
        send(last - 1, packed)
        send(last, attend(last, [0, 1, 2, 3], whole_plan, coded)[0])
        for index in range(last - 2, 0, -1):
            send(index, attend(index, [2, 3], whole_plan, coded)[0])
    if per_stage == 1:
        own = attend(0, [0, 1, 2, 3], own_plan, float_shapes(rows))
        if outer == 4:
            own = fold("float", *own, parts.pop(0), float_shapes(rows))
    else:
        own_plan = [(0, "float", 1, 0, rows)]
        packed, *own = attend(
            0, [0, 1, 2, 3], whole_plan + own_plan, [packed_shape(stage_rows)] + float_shapes(rows)
        )
        send(0, packed)
    groups = [(slice(0, rows), [(at, 0) for at in range(len(parts))])]
    merged = pl.pallas_call(
        functools.partial(merge_kernel, groups),
        in_specs=[vmem] * (2 + len(parts)),
        out_specs=vmem,
        out_shape=jax.ShapeDtypeStruct((rows, head_width), jnp.bfloat16),
        compiler_params=params,
        name="merge",
    )(*own, *parts)
    return merged.reshape(own_tokens, head_count, head_width)


def solution(mesh):
    in_specs = (P("ctx", "kvh", None), P("ctx", "kvh"), P("ctx", "kvh"), P(), P())
    out_specs = P("ctx", "kvh", None)
    size = mesh.shape["ctx"]

    def body(*args):
        return local(size, *args)

    return jax.shard_map(body, mesh=mesh, in_specs=in_specs, out_specs=out_specs, check_vma=False)
```

```python
import functools

import jax
import jax.numpy as jnp
from jax import lax
from jax.experimental import pallas as pl
from jax.experimental.pallas import tpu as pltpu
from jax.sharding import PartitionSpec as P


masked_floor = -1e30
log2_e = 1.4426950408889634
inner = 4
extra_rows = 16
tail_rows = 8
code_span = 240.0
code_low = -120.0


def split_query(query, scale):
    scaled = query.astype(jnp.float32) * scale
    high = scaled.astype(jnp.bfloat16)
    low = (scaled - high.astype(jnp.float32)).astype(jnp.bfloat16)
    return jnp.concatenate([high, low], axis=1)


def transpose_values(values, values_ref):
    for b, value in enumerate(values):
        shard_keys, width = value.shape
        values_ref[b, :width, :] = value[...].T
        values_ref[b, width:, :] = jnp.ones((extra_rows, shard_keys), jnp.bfloat16)


def score_chunk(key, query_pair, limit, start, scores_ref, slot):
    chunk, tile = key.shape[0], query_pair.shape[0]
    scores = lax.dot_general(
        jnp.concatenate([key, key], axis=1), query_pair, (((1,), (1,)), ((), ())), preferred_element_type=jnp.float32
    ).reshape(chunk // 8, 8, tile)
    position = lax.broadcasted_iota(jnp.int32, scores.shape, 0) * 8 + start
    sublane = lax.broadcasted_iota(jnp.int32, (8, tile), 0)
    scores = jnp.where(position <= (limit - sublane)[None], scores, masked_floor)
    scores_ref[slot, start : start + chunk, :] = scores.reshape(chunk, tile)
    return jnp.max(scores, axis=0)


def add_block(state, values_t, weights, shard_max):
    width = values_t.shape[0] - extra_rows
    sums = lax.dot_general(values_t, weights, (((1,), (0,)), ((), ())), preferred_element_type=jnp.float32)
    num, den = sums[:width], sums[width : width + 1]
    if state is None:
        return shard_max, den, num
    top, run_den, run_num = state
    new_top = jnp.maximum(top, shard_max)
    keep, fresh = jnp.exp2(top - new_top), jnp.exp2(shard_max - new_top)
    return new_top, run_den * keep + den * fresh, run_num * keep + num * fresh


def sweep_tiles(rows, tile, query_pair, keys, limits, scores_ref, put_weights, finish):
    shard_keys = keys[0].shape[0]
    chunk = min(512, shard_keys)
    chunks = shard_keys // chunk
    tiles = [(b, h) for b in range(len(keys)) for h in range(rows // tile)]
    count = len(tiles)
    running, tops = [None] * count, [None] * count
    for step in range(count + 2):
        for c in range(chunks):
            span = slice(c * chunk, (c + 1) * chunk)
            if step < count:
                b, h = tiles[step]
                lanes = slice(h * tile, (h + 1) * tile)
                peak = score_chunk(
                    keys[b][span, :], query_pair[lanes], limits[b][:, lanes], c * chunk, scores_ref, step % 2
                )
                running[step] = peak if c == 0 else jnp.maximum(running[step], peak)
            if 1 <= step <= count:
                t = step - 1
                if c == 0:
                    tops[t] = jnp.max(running[t], axis=0, keepdims=True)
                put_weights(t, *tiles[t], span, jnp.exp2(scores_ref[t % 2, span, :] - tops[t]).astype(jnp.bfloat16))
            if step >= 2 and c == min(1, chunks - 1):
                finish(step - 2, *tiles[step - 2], tops[step - 2])


def attend_tiles(scale, query, keys, values, limits, states, scores_ref, weights_ref, values_ref):
    states = list(states)
    query_pair = split_query(query, scale)
    transpose_values(values, values_ref)

    def put_weights(t, b, h, span, weights):
        weights_ref[t % 2, span, :] = weights

    def finish(t, b, h, shard_max):
        states[h] = add_block(states[h], values_ref[b], weights_ref[t % 2], shard_max)

    sweep_tiles(query.shape[0], scores_ref.shape[2], query_pair, keys, limits, scores_ref, put_weights, finish)
    return states


def weigh_kernel(scale, index, blocks, limits_ref, q_ref, *refs):
    me = lax.axis_index("ctx")
    count = len(blocks)
    keys, weights, tops, scores_ref = refs[:count], refs[count : 2 * count], refs[2 * count : 3 * count], refs[-1]
    tile = scores_ref.shape[2]
    limits = [limits_ref[index : index + 1, :] - (me ^ b) * keys[0].shape[0] for b in blocks]

    def put_weights(t, b, h, span, value):
        weights[b][span, h * tile : (h + 1) * tile] = value

    def finish(t, b, h, shard_max):
        tops[b][:, h * tile : (h + 1) * tile] = shard_max

    query_pair = split_query(q_ref[...], scale)
    sweep_tiles(q_ref.shape[0], tile, query_pair, keys, limits, scores_ref, put_weights, finish)


def finish_kernel(count, plan, *refs):
    values, weights, tops = refs[:count], refs[count : 2 * count], refs[2 * count : 3 * count]
    state_refs, outs, values_ref = refs[3 * count : 3 * count + 3], refs[3 * count + 3 : -1], refs[-1]
    transpose_values(values, values_ref)
    if plan is None:
        state = tuple(ref[...] for ref in state_refs)
        for b in range(count):
            state = add_block(state, values_ref[b], weights[b][...], tops[b][...])
        for ref, value in zip(outs, state):
            ref[...] = value
        return
    for at, form, out, offset, lanes in plan:
        span = slice(at * lanes, (at + 1) * lanes)
        state = tuple(ref[:, span] for ref in state_refs)
        for b in range(count):
            state = add_block(state, values_ref[b], weights[b][:, span], tops[b][:, span])
        top, den, num = state
        write_partial(outs[out:], form, slice(offset, offset + lanes), num * (1.0 / den), top + jnp.log2(den))


def encode(values, level):
    _, lanes = values.shape
    size = jnp.abs(values)
    peak = jnp.maximum(jnp.max(size, axis=0, keepdims=True), 1e-30).astype(jnp.bfloat16).astype(jnp.float32)
    code = jnp.exp2(size * (code_span / peak) + code_low)
    code = jnp.where(values < 0, -code, code)
    high = level.astype(jnp.bfloat16).astype(jnp.float32)
    rest = level - high
    middle = rest.astype(jnp.bfloat16).astype(jnp.float32)
    row = lax.broadcasted_iota(jnp.int32, (tail_rows, lanes), 0)
    tail = jnp.where(row == 0, high, jnp.where(row == 1, middle, jnp.where(row == 2, rest - middle, peak)))
    return code.astype(jnp.bfloat16), tail.astype(jnp.bfloat16)


def decode(codes, tail):
    codes, tail = codes.astype(jnp.float32), tail.astype(jnp.float32)
    level = tail[0:1] + tail[1:2] + tail[2:3]
    size = (jnp.log2(jnp.abs(codes)) - code_low) * (tail[3:4] * (1.0 / code_span))
    return jnp.where(codes < 0, -size, size), level


def spread_limits(me, own_tokens, head_count, offsets_ref, span_ref, limits_ref):
    count, lanes = limits_ref.shape
    width = offsets_ref.shape[1]
    per_row = width // own_tokens
    parts = []
    for k in range(count):
        device = me ^ (k * inner)
        row = offsets_ref[pl.ds(device // per_row, 1), :]
        row = pltpu.roll(row, (width - (device % per_row) * own_tokens) % width, 1)
        parts += [row >> 8, row & 255]
    parts = jnp.concatenate(parts, axis=0).astype(jnp.float32).astype(jnp.bfloat16)
    token = lax.broadcasted_iota(jnp.int32, (width, lanes), 0)
    lane = lax.broadcasted_iota(jnp.int32, (width, lanes), 1)
    first = token * head_count
    spread = jnp.where((lane >= first) & (lane < first + head_count), 1.0, 0.0).astype(jnp.bfloat16)
    wide = lax.dot_general(parts, spread, (((1,), (0,)), ((), ())), preferred_element_type=jnp.float32)
    wide = wide.astype(jnp.int32)
    for k in range(count):
        limits_ref[k : k + 1, :] = wide[2 * k : 2 * k + 1] * 256 + wide[2 * k + 1 : 2 * k + 2] + span_ref[...]


def setup_kernel(own_tokens, head_count, offsets_ref, span_ref, *refs):
    sources, limits_ref, targets, arrived = refs[:3], refs[3], refs[4:7], refs[7]
    copies = [pltpu.make_async_copy(*pair, arrived.at[at]) for at, pair in enumerate(zip(sources, targets))]
    for copy in copies:
        copy.start()
    spread_limits(lax.axis_index("ctx"), own_tokens, head_count, offsets_ref, span_ref, limits_ref)
    for copy in copies:
        copy.wait()


def attend_kernel(scale, index, blocks, has_state, plan, *refs):
    me = lax.axis_index("ctx")
    refs = list(refs)
    scratch = [refs.pop() for _ in range(3)][::-1]
    limits_ref, q_ref = refs[:2]
    keys = refs[2 : 2 + 2 * len(blocks) : 2]
    values = refs[3 : 3 + 2 * len(blocks) : 2]
    rest = list(refs[2 + 2 * len(blocks) :])
    rows, _ = q_ref.shape
    tile = scratch[0].shape[2]
    spans = [slice(at, at + tile) for at in range(0, rows, tile)]
    states = [None] * len(spans)
    if has_state:
        states = [tuple(ref[:, span] for ref in rest[:3]) for span in spans]
        rest = rest[3:]
    limits = [limits_ref[index : index + 1, :] - (me ^ b) * keys[0].shape[0] for b in blocks]
    states = attend_tiles(scale, q_ref[...], keys, values, limits, states, *scratch)
    if plan is None:
        for span, state in zip(spans, states):
            for ref, value in zip(rest, state):
                ref[:, span] = value
        return
    for at, form, out, offset, count in plan:
        top, den, num = (value[:, :count] for value in states[at])
        write_partial(rest[out:], form, slice(offset, offset + count), num * (1.0 / den), top + jnp.log2(den))


def write_partial(refs, form, span, value, level):
    width = value.shape[0]
    if form == "float":
        refs[0][:, span] = value
        refs[1][:, span] = level
    else:
        code, tail = encode(value, level)
        refs[0][:width, span] = code
        refs[0][width:, span] = tail


def combine(values, levels):
    top = functools.reduce(jnp.maximum, levels)
    factors = [jnp.exp2(level - top) for level in levels]
    total = functools.reduce(jnp.add, factors)
    inverse = 1.0 / total
    value = functools.reduce(jnp.add, [value * (factor * inverse) for value, factor in zip(values, factors)])
    return value, top + jnp.log2(total)


def combine_kernel(form, value_ref, level_ref, part_ref, *out_refs):
    width, lanes = value_ref.shape
    value, level = decode(part_ref[:width, :], part_ref[width:, :])
    value, level = combine([value_ref[...], value], [level_ref[...], level])
    write_partial(out_refs, form, slice(0, lanes), value, level)


def merge_kernel(groups, *refs):
    own_ref, own_level_ref = refs[:2]
    parts, out_ref = refs[2:-1], refs[-1]
    width = own_ref.shape[0]
    for span, members in groups:
        values, levels = [own_ref[:, span]], [own_level_ref[:, span]]
        for at, offset in members:
            lanes = slice(offset, offset + span.stop - span.start)
            value, level = decode(parts[at][:width, lanes], parts[at][width:, lanes])
            values.append(value)
            levels.append(level)
        out_ref[span, :] = combine(values, levels)[0].T.astype(out_ref.dtype)


def local(size, queries, cache_keys, cache_values, span_offset, positions):
    own_tokens, head_count, head_width = queries.shape
    shard_keys = cache_keys.shape[0]
    outer = size // inner
    rows = own_tokens * head_count
    me = lax.axis_index("ctx")
    place, owner = me % inner, me // inner
    scale = head_width ** (-0.5) * log2_e

    def swap(array, step):
        return lax.ppermute(array, "ctx", [(i, i ^ step) for i in range(size)])

    query = queries.reshape(rows, head_width)
    per_stage = max(outer // 4, 1)
    stages = [list(range(s, s + per_stage)) for s in range(0, outer, per_stage)]
    last = len(stages) - 1

    far_pair = [swap(cache_keys, 2), swap(cache_values, 2)]
    near_pair = [swap(cache_keys, 1), swap(cache_values, 1)]
    got = [query] + [None] * (outer - 1)

    def gather(index):
        for k in stages[index]:
            if k:
                low = k & -k
                got[k] = swap(got[k ^ low], inner * low)

    stage_rows = rows * per_stage
    tile = 256 if stage_rows % 256 == 0 else stage_rows

    fused_setup = per_stage == 1 and positions.shape[0] % 128 == 0 and 128 % own_tokens == 0
    if fused_setup:
        chain = [None]
    else:
        limits = (span_offset[0] + positions).reshape(outer, inner, own_tokens)
        limits = lax.dynamic_index_in_dim(limits, place, 1, keepdims=False)
        limits = [lax.dynamic_slice_in_dim(limits, owner ^ k, 1, axis=0) for k in range(outer)]
        limits = jnp.repeat(jnp.concatenate(limits, axis=0), head_count, axis=1)
        chain = [limits.reshape(len(stages), stage_rows)]

    def join(items, axis):
        return items[0] if len(items) == 1 else jnp.concatenate(items, axis=axis)

    vmem = pl.BlockSpec(memory_space=pltpu.VMEM)
    params = pltpu.CompilerParams(vmem_limit_bytes=20 << 20)
    pairs = [[cache_keys, cache_values], near_pair]
    stat = jax.ShapeDtypeStruct((1, stage_rows), jnp.float32)
    state_shapes = [stat, stat, jax.ShapeDtypeStruct((head_width, stage_rows), jnp.float32)]

    def packed_shape(lanes):
        return jax.ShapeDtypeStruct((head_width + tail_rows, lanes), jnp.bfloat16)

    def float_shapes(lanes):
        return [jax.ShapeDtypeStruct((size_of, lanes), jnp.float32) for size_of in (head_width, 1)]

    tiles = range(stage_rows // tile)
    whole_plan = [(at, "code", 0, at * tile, tile) for at in tiles]
    states = [None] * len(stages)

    def attend(index, blocks, plan=None, shapes=state_shapes):
        operands = [chain[0], stage_query[index]] + [array for b in blocks for array in pairs[b]]
        operands += list(states[index] or ())
        results = pl.pallas_call(
            functools.partial(
                attend_kernel, scale, index, blocks, states[index] is not None, plan
            ),
            in_specs=[vmem] * len(operands),
            out_specs=[vmem] * len(shapes),
            out_shape=shapes,
            scratch_shapes=[
                pltpu.VMEM((2, shard_keys, tile), jnp.float32),
                pltpu.VMEM((2, shard_keys, tile), jnp.bfloat16),
                pltpu.VMEM((len(blocks), head_width + extra_rows, shard_keys), jnp.bfloat16),
            ],
            compiler_params=params,
        )(*operands)
        chain[0], results = lax.optimization_barrier((chain[0], results))
        if plan is None:
            states[index] = results
        return results

    def hold(*arrays):
        chain[0], arrays = lax.optimization_barrier((chain[0], arrays))
        return list(arrays)

    stage_query = [None] * len(stages)

    def ready(index):
        stage_query[index] = join([got[k] for k in stages[index]], 0)

    for index in range(len(stages) - 1):
        gather(index)
        ready(index)
    if fused_setup:
        own = [pltpu.with_memory_space_constraint(array, pltpu.HBM) for array in (query, *pairs[0])]
        chain[0], stage_query[0], *pairs[0] = pl.pallas_call(
            functools.partial(setup_kernel, own_tokens, head_count),
            in_specs=[vmem] * 2 + [pl.BlockSpec(memory_space=pltpu.HBM)] * 3,
            out_specs=[vmem] * 4,
            out_shape=[jax.ShapeDtypeStruct((len(stages), stage_rows), jnp.int32)]
            + [jax.ShapeDtypeStruct(array.shape, array.dtype) for array in own],
            scratch_shapes=[pltpu.SemaphoreType.DMA((3,))],
            compiler_params=params,
            name="setup",
        )(positions.reshape(-1, 128), span_offset.reshape(1, 1), *own)
    for index in range(1, last - 1):
        attend(index, [0, 1])
    block = jax.ShapeDtypeStruct((shard_keys, stage_rows), jnp.bfloat16)

    def weigh(index, block_index, keys):
        results = pl.pallas_call(
            functools.partial(weigh_kernel, scale, index, [block_index]),
            in_specs=[vmem] * 3,
            out_specs=[vmem] * 2,
            out_shape=[block, stat],
            scratch_shapes=[pltpu.VMEM((2, shard_keys, tile), jnp.float32)],
            compiler_params=params,
        )(chain[0], stage_query[index], keys)
        return hold(*results)

    far_pair[0], = hold(far_pair[0])
    across_keys = swap(far_pair[0], 1)
    source = stages[last][0] ^ (stages[last][0] & -stages[last][0])
    (got[source],) = hold(got[source])
    gather(last)
    ready(last)
    attend(last - 1, [0, 1])
    far_weights = weigh(last - 1, 2, far_pair[0])
    far_pair[1], = hold(far_pair[1])
    across_values = swap(far_pair[1], 1)
    pairs += [far_pair, [across_keys, across_values]]

    def finish(index, values, weights, top, plan, shapes):
        results = pl.pallas_call(
            functools.partial(finish_kernel, 1, plan),
            in_specs=[vmem] * 6,
            out_specs=[vmem] * len(shapes),
            out_shape=shapes,
            scratch_shapes=[pltpu.VMEM((1, head_width + extra_rows, shard_keys), jnp.bfloat16)],
            compiler_params=params,
        )(values, weights, top, *states[index])
        return hold(*results)

    states[last - 1] = finish(last - 1, far_pair[1], *far_weights, None, state_shapes)
    across_weights = weigh(last - 1, 3, across_keys)
    (across_values,) = hold(across_values)
    pairs[3] = [across_keys, across_values]
    (packed,) = finish(last - 1, across_values, *across_weights, whole_plan, [packed_shape(stage_rows)])
    own_plan = [(at, "float", 0, at * tile, tile) for at in tiles]
    parts = []

    def send(index, packed):
        for at, k in enumerate(stages[index]):
            if k:
                piece = packed if per_stage == 1 else packed[:, at * rows : (at + 1) * rows]
                parts.append(swap(piece, inner * k))

    coded = [packed_shape(stage_rows)]

    def fold(form, value, level, part, shapes):
        return pl.pallas_call(
            functools.partial(combine_kernel, form),
            in_specs=[vmem] * 3,
            out_specs=[vmem] * len(shapes),
            out_shape=shapes,
            compiler_params=params,
        )(value, level, part)

    if outer == 4:
        handed = swap(packed, inner)
        (packed,) = attend(1, [2, 3], whole_plan, coded)
        parts.append(swap(packed, inner))
        value, level = attend(3, [0, 1, 2, 3], own_plan, float_shapes(stage_rows))
        (handed,) = hold(handed)
        (joined,) = fold("code", value, level, handed, coded)
        (joined,) = hold(joined)
        parts.append(swap(joined, 3 * inner))
    else:
        send(last - 1, packed)
        send(last, attend(last, [0, 1, 2, 3], whole_plan, coded)[0])
        for index in range(last - 2, 0, -1):
            send(index, attend(index, [2, 3], whole_plan, coded)[0])
    if per_stage == 1:
        own = attend(0, [0, 1, 2, 3], own_plan, float_shapes(rows))
        if outer == 4:
            own = fold("float", *own, parts.pop(0), float_shapes(rows))
    else:
        own_plan = [(0, "float", 1, 0, rows)]
        packed, *own = attend(
            0, [0, 1, 2, 3], whole_plan + own_plan, [packed_shape(stage_rows)] + float_shapes(rows)
        )
        send(0, packed)
    groups = [(slice(0, rows), [(at, 0) for at in range(len(parts))])]
    merged = pl.pallas_call(
        functools.partial(merge_kernel, groups),
        in_specs=[vmem] * (2 + len(parts)),
        out_specs=vmem,
        out_shape=jax.ShapeDtypeStruct((rows, head_width), jnp.bfloat16),
        compiler_params=params,
        name="merge",
    )(*own, *parts)
    return merged.reshape(own_tokens, head_count, head_width)


def solution(mesh):
    in_specs = (P("ctx", "kvh", None), P("ctx", "kvh"), P("ctx", "kvh"), P(), P())
    out_specs = P("ctx", "kvh", None)
    size = mesh.shape["ctx"]

    def body(*args):
        return local(size, *args)

    return jax.shard_map(body, mesh=mesh, in_specs=in_specs, out_specs=out_specs, check_vma=False)
```
